256 devices in a mesh: row: 16 (over z, core), col: 16 (over y, x).
Axes of the slice: x: 4, y: 4, z: 8, core: 2. Of those that a mesh axis runs over, the one named last changes fastest.
Arguments:
- schur_blocks: bfloat16 [2, 16, 2, 16, 256, 256], P(None, 'row', None, 'col'), may hold values from -0.1875 to 0.1875
- known_blocks: float32 [2, 16, 2, 16, 256, 256], P(None, 'row', None, 'col'), may hold values from -6 to 6
- eigen_pairs: float32 [2, 16, 2, 256, 256], P(None, 'row'), as said below
- eigenvalues: float32 [32, 256], replicated, may hold values from 1 to 8.95, as said below
Outputs:
- updated: float32 [2, 16, 2, 16, 256, 256], P(None, 'row', None, 'col')
The draws below stay inside these ranges and needn't reach their ends.
Inputs may be any that keep to these rules, and one draw needn't show every extreme that they name: For each block, eigen_pairs[a, r, 0] is unit upper triangular and eigen_pairs[a, r, 1] is its inverse. `eigenvalues`: row i lies within 1 + i / 4 and 1.2 + i / 4.
All inputs are finite; a program needn't handle non-finite values.
Results may differ from the reference program's by a relative error of at most 0.0017.
Values may be sent and summed in bfloat16 or wider, within the bound.
A program may use at most 128 MiB of HBM per device.

```python
import math
import jax
import jax.numpy as jnp
from jax import lax

BS = 256
FIRST = 8
DIAGS = 4
BPR = 2
BPC = 2
N_ROW = 16
N_COL = 16


def draw_eigen_pairs(key, part):
    count = BPR * N_ROW
    spread = 0.32 / math.sqrt(BS)
    upper = jax.random.normal(key, (count, BS, BS), jnp.float32) * spread
    identity = jnp.eye(BS, dtype=jnp.float32)
    vectors = jnp.triu(upper, 1) + identity
    inverses = lax.linalg.triangular_solve(vectors, jnp.broadcast_to(identity, vectors.shape), left_side=True, lower=False)
    return jnp.stack([vectors, inverses], axis=1).reshape(BPR, N_ROW, 2, BS, BS)


def draw_eigenvalues(key, part):
    count = BPR * N_ROW
    base = 1.0 + 0.25 * jnp.arange(count, dtype=jnp.float32)[:, None]
    fraction = jax.random.uniform(key, (count, BS), jnp.float32)
    return base + 0.2 * fraction


def level_of(own_key, extent, shards, low, high):
    level = 1.0
    for axis_at, blocks in shards:
        draws = jax.random.uniform(jax.random.fold_in(jax.random.fold_in(own_key, 6), axis_at), (blocks,), jnp.float32, low / len(shards), high / len(shards))
        level = level * jnp.repeat(jnp.exp(draws), extent[axis_at] // blocks).reshape((-1,) + (1,) * (len(extent) - 1 - axis_at))
    return level


def noise(key, extent, scale, bound, pieces=(), held_as=jnp.bfloat16):
    entries = jax.random.normal(key, extent, jnp.float32) * scale
    if len(pieces) > 0:
        entries = level_of(key, extent, pieces, -0.22, 0.18) * entries
    return jnp.clip(entries, min=-bound, max=bound).astype(held_as)


def setup_inputs(seed: int = 0) -> dict:
    key_of = jax.random.split(jax.random.key(seed), 5)
    schur_blocks = noise(key_of[0], (BPR, N_ROW, BPC, N_COL, BS, BS), (4 * BS) ** -0.5, 0.1875, ((1, 16), (3, 16)))
    known_blocks = noise(key_of[1], (BPR, N_ROW, BPC, N_COL, BS, BS), 1.0, 6.0, ((1, 16), (3, 16)), jnp.float32)
    eigen_pairs = draw_eigen_pairs(jax.random.fold_in(key_of[4], 71), 0)
    eigenvalues = draw_eigenvalues(jax.random.fold_in(key_of[4], 71), 0)
    return dict(schur_blocks=schur_blocks, known_blocks=known_blocks, eigen_pairs=eigen_pairs, eigenvalues=eigenvalues)


def full_dot(left_side, right_side):
    return jnp.dot(left_side.astype(jnp.float32), right_side.astype(jnp.float32), precision=lax.Precision.HIGHEST, preferred_element_type=jnp.float32)

def reference(schur_blocks, known_blocks, eigen_pairs, eigenvalues):
    blocks_total = BPR * N_ROW

    def schur_at(row_block, col_block):
        return schur_blocks[row_block // N_ROW, row_block % N_ROW, col_block // N_COL, col_block % N_COL]
    rounded = {}

    def factor_at(row_block, col_block):
        if (row_block, col_block) in rounded:
            return rounded[row_block, col_block]
        return known_blocks[row_block // N_ROW, row_block % N_ROW, col_block // N_COL, col_block % N_COL].astype(jnp.bfloat16)
    placed_blocks = []
    first_major = []
    first_minor = []
    second_major = []
    second_minor = []
    for distance in range(FIRST, FIRST + DIAGS):
        for row_block in range(blocks_total - distance):
            col_block = row_block + distance
            running = jnp.zeros((BS, BS), jnp.float32)
            for middle in range(row_block, col_block):
                running = running + jnp.dot(factor_at(row_block, middle).astype(jnp.float32), schur_at(middle, col_block).astype(jnp.float32), preferred_element_type=jnp.float32)
            for middle in range(row_block + 1, col_block + 1):
                running = running - jnp.dot(schur_at(row_block, middle).astype(jnp.float32), factor_at(middle, col_block).astype(jnp.float32), preferred_element_type=jnp.float32)
            pair_left = eigen_pairs[row_block // N_ROW, row_block % N_ROW]
            pair_right = eigen_pairs[col_block // N_ROW, col_block % N_ROW]
            spacing = eigenvalues[row_block][:, None] - eigenvalues[col_block][None, :]
            mixed_block = full_dot(full_dot(pair_left[1], running), pair_right[0]) / spacing
            solved = full_dot(full_dot(pair_left[0], mixed_block), pair_right[1])
            rounded[row_block, col_block] = solved.astype(jnp.bfloat16)
            placed_blocks.append(solved)
            first_major.append(row_block // N_ROW)
            first_minor.append(row_block % N_ROW)
            second_major.append(col_block // N_COL)
            second_minor.append(col_block % N_COL)
    index_one = jnp.array(first_major).astype(jnp.int32)
    index_two = jnp.array(first_minor).astype(jnp.int32)
    index_three = jnp.array(second_major).astype(jnp.int32)
    index_four = jnp.array(second_minor).astype(jnp.int32)
    return known_blocks.at[index_one, index_two, index_three, index_four].set(jnp.stack(placed_blocks))
```

```python
import functools

import jax
import jax.numpy as jnp
from jax import lax
from jax.experimental import pallas as pl
from jax.experimental.pallas import tpu as pltpu
from jax.sharding import PartitionSpec as P

FIRST = 8
DIAGS = 4
SIDE = 16
TOTAL = 32
MESH = pl.DeviceIdType.MESH


def remote(src, dst, send_sem, recv_sem, row, col):
    return pltpu.make_async_remote_copy(
        src_ref=src, dst_ref=dst, send_sem=send_sem, recv_sem=recv_sem,
        device_id=(row, col), device_id_type=MESH,
    )


def arrived(ref, sem):
    pltpu.make_async_copy(ref, ref, sem).wait()


def wrap(x):
    return lax.rem(x + 2 * SIDE, SIDE)


def dot(a, b):
    return jnp.dot(a, b, preferred_element_type=jnp.float32)


def halves(x):
    high = x.astype(jnp.bfloat16)
    return high, (x - high.astype(jnp.float32)).astype(jnp.bfloat16)


def left_dot(a, x):
    high, low = halves(x)
    return dot(a, high) + dot(a, low)


def right_dot(x, b):
    high, low = halves(x)
    return dot(high, b) + dot(low, b)


def kernel(
    schur, known, pairs, lam, out,
    row_f, row_s, col_f, col_s, vj, new_r, new_c, total, gap, fresh,
    q_row_f, q_row_s, q_col_f, q_col_s, q_vj, q_new_r, q_new_c,
    s_src, s_ring_f, s_ring_s, s_chain_f, s_chain_s, s_chain_v, s_own, s_new,
):
    r = lax.axis_index("row")
    c = lax.axis_index("col")
    e = wrap(c - r)
    m = e - FIRST
    is_target = (e >= FIRST) & (e < FIRST + DIAGS)
    later = []

    def send(cond, *args):
        copy = remote(*args)

        @pl.when(cond)
        def _():
            copy.start()

        later.append((cond, copy))

    barrier = pltpu.get_barrier_semaphore()

    def greet(step, carry):
        pl.semaphore_signal(barrier, inc=1, device_id=(wrap(r + step), c), device_id_type=MESH)
        pl.semaphore_signal(barrier, inc=1, device_id=(r, wrap(c + step)), device_id_type=MESH)
        return carry

    lax.fori_loop(1, SIDE, greet, 0)
    pl.semaphore_wait(barrier, 2 * (SIDE - 1))

    near = e < FIRST
    eb = jnp.minimum(e, FIRST - 1)
    col_to = wrap(r + FIRST + lax.rem(e, DIAGS))
    places = []
    for t in (0, 1):
        k = r + SIDE * t
        j = k + e
        b = jnp.minimum(j // SIDE, 1)
        to_row = near & (k < TOTAL - FIRST)
        to_col = near & (j >= FIRST) & (j < TOTAL)
        last = jnp.minimum(DIAGS - 1, j - FIRST)
        i_to = j - FIRST - jnp.where(e >= DIAGS, 0, last)
        places.append((b, to_row, to_col, wrap(i_to), jnp.clip(i_to // SIDE, 0, 1)))
    for n, (ref, row_ref, col_ref, q_row, q_col) in enumerate(
        ((known, row_f, col_f, q_row_f, q_col_f), (schur, row_s, col_s, q_row_s, q_col_s))
    ):
        for t in (0, 1):
            b, to_row, to_col, row_to, t_to = places[t]
            used = e >= n
            send(to_row & used, ref.at[t, b], row_ref.at[t, eb], s_src.at[t, 2 * n], q_row.at[t, eb], r, col_to)
            send(to_col & used, ref.at[t, b], col_ref.at[t_to, eb], s_src.at[t, 2 * n + 1], q_col.at[t_to, eb], row_to, c)
    for t in (0, 1):
        b, to_row, to_col, row_to, t_to = places[t]
        send(to_col & (e == 0), pairs.at[t], vj.at[t_to], s_src.at[t, 4], q_vj.at[t_to], row_to, c)

    mb = jnp.clip(m, 0, DIAGS - 1)
    col_plus = wrap(r + FIRST + lax.rem(mb + 1, DIAGS))
    col_minus = wrap(r + FIRST + lax.rem(mb + DIAGS - 1, DIAGS))

    part, real, low_mem, high_mem = [], [], [], []
    for t in (0, 1):
        i = r + SIDE * t
        j = i + FIRST + m
        part.append(is_target & (i < TOTAL - FIRST))
        real.append(is_target & (j < TOTAL))
        low_mem.append(is_target & (j < TOTAL) & (m > 0))
        high_mem.append(is_target & (j < TOTAL) & (m < DIAGS - 1) & (i >= 1))

    def member(t, delta):
        i = r + SIDE * t - delta
        return wrap(i), jnp.clip(i // SIDE, 0, 1)

    for t in (0, 1):
        i = r + SIDE * t
        j = i + FIRST + m
        b = jnp.clip(j // SIDE, 0, 1)
        at = FIRST + mb

        @pl.when(real[t])
        def _():
            pltpu.make_async_copy(schur.at[t, b], row_s.at[t, at], q_row_s.at[t, at]).start()
            pltpu.make_async_copy(schur.at[t, b], col_s.at[t, at], q_col_s.at[t, at]).start()
            rows = jnp.broadcast_to(lam[pl.ds(i, 1), :], total.shape[1:]).T
            gap[t] = 1.0 / (rows - lam[pl.ds(jnp.clip(j, 0, TOTAL - 1), 1), :])
            total[t] = jnp.zeros(total.shape[1:], jnp.float32)

        for d in range(1, DIAGS):
            fits = real[t] & (m + d < DIAGS)
            send(fits & (j + d < TOTAL), schur.at[t, b], row_s.at[t, at], s_own.at[t, 0, d - 1], q_row_s.at[t, at], r, wrap(c + d))
            row_to, t_to = member(t, d)
            send(fits & (i >= d), schur.at[t, b], col_s.at[t_to, at], s_own.at[t, 1, d - 1], q_col_s.at[t_to, at], row_to, c)

    def ring_f(t, x, d):
        return remote(row_f.at[t, x], row_f.at[t, x], s_ring_f.at[t, x, d], q_row_f.at[t, x], r, (col_plus, col_minus)[d])

    def ring_s(t, x, d):
        return remote(row_s.at[t, x], row_s.at[t, x], s_ring_s.at[t, x, d], q_row_s.at[t, x], r, (col_plus, col_minus)[d])

    def chain_copy(t, x, ref, send_sems, recv_sems, up):
        row_to, t_to = member(t, 1 if up else -1)
        return remote(ref.at[t, x], ref.at[t_to, x], send_sems.at[t, x], recv_sems.at[t_to, x], row_to, c)

    def chain_v(t):
        row_to, t_to = member(t, -1)
        return remote(vj.at[t], vj.at[t_to], s_chain_v.at[t], q_vj.at[t_to], row_to, c)

    def ring_conds(t, x):
        away = lax.rem(mb - x + 2 * DIAGS, DIAGS)
        return away

    def accumulate(t, x):
        other = FIRST + mb - x
        total[t] += dot(row_f[t, other], col_s[t, x]) - dot(row_s[t, x], col_f[t, other])

    def run_if(cond, fn):
        pl.when(cond)(fn)

    def f_actions(t, x, what):
        away = ring_conds(t, x)
        run_if(part[t] & (away <= 1), lambda: what(ring_f(t, x, 0)))
        run_if(part[t] & (away == 0), lambda: what(ring_f(t, x, 1)))

    def s_actions(t, x, what):
        away = ring_conds(t, x)
        run_if(part[t] & (away == 0), lambda: what(ring_s(t, x, 0)))
        run_if(part[t] & ((away == 0) | (away == DIAGS - 1)), lambda: what(ring_s(t, x, 1)))

    def chain_actions(t, x, ref, send_sems, recv_sems, what):
        run_if(high_mem[t] & (x >= DIAGS), lambda: what(chain_copy(t, x, ref, send_sems, recv_sems, True)))
        run_if(low_mem[t] & (x < DIAGS), lambda: what(chain_copy(t, x, ref, send_sems, recv_sems, False)))

    def start(copy):
        copy.start()

    def sent(copy):
        copy.wait_send()

    def f_step(x, carry):
        for t in (0, 1):

            @pl.when(part[t])
            def _():
                arrived(row_f.at[t, x], q_row_f.at[t, x])

            f_actions(t, x, start)

            @pl.when(real[t])
            def _():
                arrived(col_f.at[t, x], q_col_f.at[t, x])

            chain_actions(t, x, col_f, s_chain_f, q_col_f, start)
        return carry

    lax.fori_loop(0, FIRST, f_step, 0)

    def s_step(x, carry):
        for t in (0, 1):

            @pl.when(part[t])
            def _():
                arrived(row_s.at[t, x], q_row_s.at[t, x])

            s_actions(t, x, start)

            @pl.when(real[t])
            def _():
                arrived(col_s.at[t, x], q_col_s.at[t, x])

            chain_actions(t, x, col_s, s_chain_s, q_col_s, start)
        for t in (0, 1):

            @pl.when(real[t] & (x > m))
            def _():
                accumulate(t, x)

        return carry

    lax.fori_loop(1, FIRST, s_step, 0)

    def far_step(x, carry):
        for t in (0, 1):

            @pl.when(real[t] & (x <= FIRST + m))
            def _():
                arrived(row_s.at[t, x], q_row_s.at[t, x])
                arrived(col_s.at[t, x], q_col_s.at[t, x])
                accumulate(t, x)

        return carry

    lax.fori_loop(FIRST, FIRST + DIAGS, far_step, 0)

    for t in (0, 1):

        @pl.when(real[t])
        def _():
            arrived(vj.at[t], q_vj.at[t])

        run_if(low_mem[t], lambda: start(chain_v(t)))

    for before in range(DIAGS - 1):
        for t in (0, 1):

            @pl.when(real[t] & (m > before))
            def _():
                near = jnp.clip(m - before, 1, DIAGS - 1)
                arrived(new_r.at[t, before], q_new_r.at[t, before])
                arrived(new_c.at[t, before], q_new_c.at[t, before])
                total[t] += dot(new_r[t, before], col_s[t, near]) - dot(row_s[t, near], new_c[t, before])

    @pl.when(is_target)
    def _():
        both = (0, 1)
        x = [left_dot(pairs[t, 1], total[t]) for t in both]
        x = [right_dot(x[t], vj[t, 0]) * gap[t] for t in both]
        x = [left_dot(pairs[t, 0], x[t]) for t in both]
        x = [right_dot(x[t], vj[t, 1]) for t in both]
        for t in both:
            fresh[t] = x[t].astype(jnp.bfloat16)
            out[t] = x[t]

    mb3 = jnp.minimum(mb, DIAGS - 2)
    for d in range(1, DIAGS):
        for t in (0, 1):
            i = r + SIDE * t
            fits = real[t] & (m + d < DIAGS)
            row_to, t_to = member(t, d)
            send(fits & (i + FIRST + m + d < TOTAL), fresh.at[t], new_r.at[t, mb3], s_new.at[t, 0, d - 1], q_new_r.at[t, mb3], r, wrap(c + d))
            send(fits & (i >= d), fresh.at[t], new_c.at[t_to, mb3], s_new.at[t, 1, d - 1], q_new_c.at[t_to, mb3], row_to, c)

    for cond, copy in later:
        run_if(cond, lambda: copy.wait_send())

    def drain(x, carry):
        for t in (0, 1):
            f_actions(t, x, sent)
            chain_actions(t, x, col_f, s_chain_f, q_col_f, sent)

            @pl.when(x >= 1)
            def _():
                s_actions(t, x, sent)
                chain_actions(t, x, col_s, s_chain_s, q_col_s, sent)

        return carry

    lax.fori_loop(0, FIRST, drain, 0)
    for t in (0, 1):
        run_if(low_mem[t], lambda: sent(chain_v(t)))


def exchange(schur, known, pairs, lam):
    bs = schur.shape[-1]
    half, full = jnp.bfloat16, jnp.float32
    dma = pltpu.SemaphoreType.DMA
    vmem = pl.BlockSpec(memory_space=pltpu.VMEM)
    return pl.pallas_call(
        kernel,
        out_shape=jax.ShapeDtypeStruct((2, bs, bs), full),
        in_specs=[vmem] * 4,
        out_specs=vmem,
        scratch_shapes=[
            pltpu.VMEM((2, FIRST, bs, bs), half),
            pltpu.VMEM((2, FIRST + DIAGS, bs, bs), half),
            pltpu.VMEM((2, FIRST, bs, bs), half),
            pltpu.VMEM((2, FIRST + DIAGS, bs, bs), half),
            pltpu.VMEM((2, 2, bs, bs), half),
            pltpu.VMEM((2, DIAGS - 1, bs, bs), half),
            pltpu.VMEM((2, DIAGS - 1, bs, bs), half),
            pltpu.VMEM((2, bs, bs), full),
            pltpu.VMEM((2, bs, bs), full),
            pltpu.VMEM((2, bs, bs), half),
            dma((2, FIRST)), dma((2, FIRST + DIAGS)), dma((2, FIRST)), dma((2, FIRST + DIAGS)),
            dma((2,)), dma((2, DIAGS - 1)), dma((2, DIAGS - 1)),
            dma((2, 5)), dma((2, FIRST, 2)), dma((2, FIRST, 2)), dma((2, FIRST)), dma((2, FIRST)),
            dma((2,)), dma((2, 2, DIAGS - 1)), dma((2, 2, DIAGS - 1)),
        ],
        compiler_params=pltpu.CompilerParams(
            collective_id=0, has_side_effects=True, vmem_limit_bytes=40 * 1024 * 1024
        ),
    )(schur, known, pairs, lam)


def body(schur_blocks, known_blocks, eigen_pairs, eigenvalues):
    known = known_blocks[:, 0, :, 0]
    solved = exchange(
        schur_blocks[:, 0, :, 0],
        known.astype(jnp.bfloat16),
        eigen_pairs[:, 0].astype(jnp.bfloat16),
        eigenvalues,
    )
    rows = lax.axis_index("row") + SIDE * jnp.arange(2)[:, None]
    cols = lax.axis_index("col") + SIDE * jnp.arange(2)[None, :]
    away = cols - rows
    new = (away >= FIRST) & (away < FIRST + DIAGS)
    output = jnp.where(new[:, :, None, None], solved[:, None], known)
    return output[:, None, :, None]


def solution(mesh):
    return jax.shard_map(
        body,
        mesh=mesh,
        in_specs=(
            P(None, "row", None, "col", None, None),
            P(None, "row", None, "col", None, None),
            P(None, "row", None, None, None),
            P(),
        ),
        out_specs=P(None, "row", None, "col", None, None),
        check_vma=False,
    )
```

```python
import functools

import jax
import jax.numpy as jnp
from jax import lax
from jax.experimental import pallas as pl
from jax.experimental.pallas import tpu as pltpu
from jax.sharding import PartitionSpec as P

FIRST = 8
DIAGS = 4
SIDE = 16
TOTAL = 32
MESH = pl.DeviceIdType.MESH


def remote(src, dst, send_sem, recv_sem, row, col):
    return pltpu.make_async_remote_copy(
        src_ref=src, dst_ref=dst, send_sem=send_sem, recv_sem=recv_sem,
        device_id=(row, col), device_id_type=MESH,
    )


def arrived(ref, sem):
    pltpu.make_async_copy(ref, ref, sem).wait()


def wrap(x):
    return lax.rem(x + 2 * SIDE, SIDE)


def dot(a, b):
    return jnp.dot(a, b, preferred_element_type=jnp.float32)


def halves(x):
    high = x.astype(jnp.bfloat16)
    return high, (x - high.astype(jnp.float32)).astype(jnp.bfloat16)


def left_dot(a, x):
    high, low = halves(x)
    return dot(a, high) + dot(a, low)


def right_dot(x, b):
    high, low = halves(x)
    return dot(high, b) + dot(low, b)


def kernel(
    schur, known, pairs, lam, out,
    row_f, row_s, col_f, col_s, vj, new_r, new_c, total, gap, fresh,
    q_row_f, q_row_s, q_col_f, q_col_s, q_vj, q_new_r, q_new_c,
    s_src, s_ring_f, s_ring_s, s_chain_f, s_chain_s, s_chain_v, s_own, s_new,
):
    r = lax.axis_index("row")
    c = lax.axis_index("col")
    e = wrap(c - r)
    m = e - FIRST
    is_target = (e >= FIRST) & (e < FIRST + DIAGS)
    later = []

    def send(cond, *args):
        copy = remote(*args)

        @pl.when(cond)
        def _():
            copy.start()

        later.append((cond, copy))

    barrier = pltpu.get_barrier_semaphore()

    def greet(step, carry):
        pl.semaphore_signal(barrier, inc=1, device_id=(wrap(r + step), c), device_id_type=MESH)
        pl.semaphore_signal(barrier, inc=1, device_id=(r, wrap(c + step)), device_id_type=MESH)
        return carry

    lax.fori_loop(1, SIDE, greet, 0)
    pl.semaphore_wait(barrier, 2 * (SIDE - 1))

    near = e < FIRST
    eb = jnp.minimum(e, FIRST - 1)
    col_to = wrap(r + FIRST + lax.rem(e, DIAGS))
    places = []
    for t in (0, 1):
        k = r + SIDE * t
        j = k + e
        b = jnp.minimum(j // SIDE, 1)
        to_row = near & (k < TOTAL - FIRST)
        to_col = near & (j >= FIRST) & (j < TOTAL)
        last = jnp.minimum(DIAGS - 1, j - FIRST)
        i_to = j - FIRST - jnp.where(e >= DIAGS, 0, last)
        places.append((b, to_row, to_col, wrap(i_to), jnp.clip(i_to // SIDE, 0, 1)))
    for n, (ref, row_ref, col_ref, q_row, q_col) in enumerate(
        ((known, row_f, col_f, q_row_f, q_col_f), (schur, row_s, col_s, q_row_s, q_col_s))
    ):
        for t in (0, 1):
            b, to_row, to_col, row_to, t_to = places[t]
            used = e >= n
            send(to_row & used, ref.at[t, b], row_ref.at[t, eb], s_src.at[t, 2 * n], q_row.at[t, eb], r, col_to)
            send(to_col & used, ref.at[t, b], col_ref.at[t_to, eb], s_src.at[t, 2 * n + 1], q_col.at[t_to, eb], row_to, c)
    for t in (0, 1):
        b, to_row, to_col, row_to, t_to = places[t]
        send(to_col & (e == 0), pairs.at[t], vj.at[t_to], s_src.at[t, 4], q_vj.at[t_to], row_to, c)

    mb = jnp.clip(m, 0, DIAGS - 1)
    col_plus = wrap(r + FIRST + lax.rem(mb + 1, DIAGS))
    col_minus = wrap(r + FIRST + lax.rem(mb + DIAGS - 1, DIAGS))

    part, real, low_mem, high_mem = [], [], [], []
    for t in (0, 1):
        i = r + SIDE * t
        j = i + FIRST + m
        part.append(is_target & (i < TOTAL - FIRST))
        real.append(is_target & (j < TOTAL))
        low_mem.append(is_target & (j < TOTAL) & (m > 0))
        high_mem.append(is_target & (j < TOTAL) & (m < DIAGS - 1) & (i >= 1))

    def member(t, delta):
        i = r + SIDE * t - delta
        return wrap(i), jnp.clip(i // SIDE, 0, 1)

    for t in (0, 1):
        i = r + SIDE * t
        j = i + FIRST + m
        b = jnp.clip(j // SIDE, 0, 1)
        at = FIRST + mb

        @pl.when(real[t])
        def _():
            pltpu.make_async_copy(schur.at[t, b], row_s.at[t, at], q_row_s.at[t, at]).start()
            pltpu.make_async_copy(schur.at[t, b], col_s.at[t, at], q_col_s.at[t, at]).start()
            rows = jnp.broadcast_to(lam[pl.ds(i, 1), :], total.shape[1:]).T
            gap[t] = 1.0 / (rows - lam[pl.ds(jnp.clip(j, 0, TOTAL - 1), 1), :])
            total[t] = jnp.zeros(total.shape[1:], jnp.float32)

        for d in range(1, DIAGS):
            fits = real[t] & (m + d < DIAGS)
            send(fits & (j + d < TOTAL), schur.at[t, b], row_s.at[t, at], s_own.at[t, 0, d - 1], q_row_s.at[t, at], r, wrap(c + d))
            row_to, t_to = member(t, d)
            send(fits & (i >= d), schur.at[t, b], col_s.at[t_to, at], s_own.at[t, 1, d - 1], q_col_s.at[t_to, at], row_to, c)

    def ring_f(t, x, d):
        return remote(row_f.at[t, x], row_f.at[t, x], s_ring_f.at[t, x, d], q_row_f.at[t, x], r, (col_plus, col_minus)[d])

    def ring_s(t, x, d):
        return remote(row_s.at[t, x], row_s.at[t, x], s_ring_s.at[t, x, d], q_row_s.at[t, x], r, (col_plus, col_minus)[d])

    def chain_copy(t, x, ref, send_sems, recv_sems, up):
        row_to, t_to = member(t, 1 if up else -1)
        return remote(ref.at[t, x], ref.at[t_to, x], send_sems.at[t, x], recv_sems.at[t_to, x], row_to, c)

    def chain_v(t):
        row_to, t_to = member(t, -1)
        return remote(vj.at[t], vj.at[t_to], s_chain_v.at[t], q_vj.at[t_to], row_to, c)

    def accumulate(t, x):
        other = FIRST + mb - x
        total[t] += dot(row_f[t, other], col_s[t, x]) - dot(row_s[t, x], col_f[t, other])

    def run_if(cond, fn):
        pl.when(cond)(fn)

    kinds = (
        (row_f, q_row_f, ring_f, 0, col_f, s_chain_f, q_col_f),
        (row_s, q_row_s, ring_s, 1, col_s, s_chain_s, q_col_s),
    )

    late0 = is_target & (r + e >= SIDE + FIRST)
    t_col = (jnp.int32(0), jnp.where(real[1], 1, 0))
    col_live = (real[0] & ~late0, real[1] | late0)

    def place(n):
        i = r + SIDE * t_col[n]
        last = jnp.minimum(DIAGS - 1, i + m)
        up = col_live[n] & (m < last)
        down = col_live[n] & (m > 0)
        return up, down, last - m

    def row_entry(kind, t, start):
        ref, sems, ring, dest = kind[0], kind[1], kind[2], kind[3]
        for x in (mb, mb + DIAGS):

            @pl.when(part[t] & (x >= dest))
            def _():
                if start:
                    arrived(ref.at[t, x], sems.at[t, x])
                    ring(t, x, 0).start()
                    ring(t, x, 1).start()
                else:
                    ring(t, x, 0).wait_send()
                    ring(t, x, 1).wait_send()

    def row_relay(kind, t, start):
        ref, sems, ring, dest = kind[0], kind[1], kind[2], kind[3]
        base = lax.rem(mb + (1 if dest else DIAGS - 1), DIAGS)
        for x in (base, base + DIAGS):

            @pl.when(part[t] & (x >= dest))
            def _():
                if start:
                    arrived(ref.at[t, x], sems.at[t, x])
                    ring(t, x, dest).start()
                else:
                    ring(t, x, dest).wait_send()

    def col_relay(kind, n, depths, start):
        ref, send_sems, recv_sems = kind[4:]
        up, down, from_last = place(n)
        t = t_col[n]
        up_now, down_now = jnp.bool_(False), jnp.bool_(False)
        for depth in depths:
            up_now |= up & (m == depth)
            down_now |= down & (from_last == depth)

        def step(x, carry):
            @pl.when(up_now)
            def _():
                copy = chain_copy(t, x + DIAGS, ref, send_sems, recv_sems, True)
                if start:
                    arrived(ref.at[t, x + DIAGS], recv_sems.at[t, x + DIAGS])
                    copy.start()
                else:
                    copy.wait_send()

            @pl.when(down_now & (x >= kind[3]))
            def _():
                copy = chain_copy(t, x, ref, send_sems, recv_sems, False)
                if start:
                    arrived(ref.at[t, x], recv_sems.at[t, x])
                    copy.start()
                else:
                    copy.wait_send()

            return carry

        lax.fori_loop(0, DIAGS, step, 0)

    rounds = tuple((kind, n) for kind in kinds for n in (0, 1))

    def first_hops(n):
        kind, t = rounds[n]
        row_entry(kind, t, True)
        col_relay(kind, t, (0,), True)
        col_relay(kind, t, (1,), True)

    def second_hops(n):
        kind, t = rounds[n]
        row_relay(kind, t, True)
        col_relay(kind, t, (2,), True)

    for n in range(len(rounds)):
        first_hops(n)
        if n:
            second_hops(n - 1)
    second_hops(len(rounds) - 1)

    up_of, down_of = [], []
    for t in (0, 1):
        last = jnp.minimum(DIAGS - 1, r + SIDE * t + m)
        up_of.append(m < last)
        down_of.append(m > 0)

    def rest(x, carry):
        away = lax.rem(mb - x + 2 * DIAGS, DIAGS)
        for t in (0, 1):
            ends = jnp.where(x >= DIAGS, ~up_of[t], ~down_of[t])
            run_if(part[t] & (away >= 2), lambda: arrived(row_f.at[t, x], q_row_f.at[t, x]))
            run_if(real[t] & ends, lambda: arrived(col_f.at[t, x], q_col_f.at[t, x]))

            @pl.when(x >= 1)
            def _():
                run_if(part[t] & ((away == 1) | (away == 2)), lambda: arrived(row_s.at[t, x], q_row_s.at[t, x]))
                run_if(real[t] & ends, lambda: arrived(col_s.at[t, x], q_col_s.at[t, x]))

        return carry

    lax.fori_loop(0, FIRST, rest, 0)

    def far(x, carry):
        for t in (0, 1):

            @pl.when(real[t] & (x >= FIRST) & (x <= FIRST + m))
            def _():
                arrived(row_s.at[t, x], q_row_s.at[t, x])
                arrived(col_s.at[t, x], q_col_s.at[t, x])

            @pl.when(real[t] & (x > m) & (x <= FIRST + m))
            def _():
                accumulate(t, x)

        return carry

    lax.fori_loop(1, FIRST + DIAGS, far, 0)

    for n in (0, 1):
        _, down, from_last = place(n)
        t = t_col[n]
        for depth in range(DIAGS - 1):

            @pl.when(down & (from_last == depth))
            def _():
                arrived(vj.at[t], q_vj.at[t])
                chain_v(t).start()

    for t in (0, 1):
        run_if(real[t] & ~down_of[t], lambda: arrived(vj.at[t], q_vj.at[t]))

    for before in range(DIAGS - 1):
        for t in (0, 1):

            @pl.when(real[t] & (m > before))
            def _():
                near = jnp.clip(m - before, 1, DIAGS - 1)
                arrived(new_r.at[t, before], q_new_r.at[t, before])
                arrived(new_c.at[t, before], q_new_c.at[t, before])
                total[t] += dot(new_r[t, before], col_s[t, near]) - dot(row_s[t, near], new_c[t, before])

    @pl.when(is_target)
    def _():
        both = (0, 1)
        x = [left_dot(pairs[t, 1], total[t]) for t in both]
        x = [right_dot(x[t], vj[t, 0]) * gap[t] for t in both]
        x = [left_dot(pairs[t, 0], x[t]) for t in both]
        x = [right_dot(x[t], vj[t, 1]) for t in both]
        for t in both:
            fresh[t] = x[t].astype(jnp.bfloat16)
            out[t] = x[t]

    mb3 = jnp.minimum(mb, DIAGS - 2)
    for d in range(1, DIAGS):
        for t in (0, 1):
            i = r + SIDE * t
            fits = real[t] & (m + d < DIAGS)
            row_to, t_to = member(t, d)
            send(fits & (i + FIRST + m + d < TOTAL), fresh.at[t], new_r.at[t, mb3], s_new.at[t, 0, d - 1], q_new_r.at[t, mb3], r, wrap(c + d))
            send(fits & (i >= d), fresh.at[t], new_c.at[t_to, mb3], s_new.at[t, 1, d - 1], q_new_c.at[t_to, mb3], row_to, c)

    for cond, copy in later:
        run_if(cond, lambda: copy.wait_send())

    for kind, n in rounds:
        row_entry(kind, n, False)
        row_relay(kind, n, False)
        col_relay(kind, n, (0, 1, 2), False)
    for n in (0, 1):
        _, down, _ = place(n)
        run_if(down, lambda: chain_v(t_col[n]).wait_send())


def exchange(schur, known, pairs, lam):
    bs = schur.shape[-1]
    half, full = jnp.bfloat16, jnp.float32
    dma = pltpu.SemaphoreType.DMA
    vmem = pl.BlockSpec(memory_space=pltpu.VMEM)
    return pl.pallas_call(
        kernel,
        out_shape=jax.ShapeDtypeStruct((2, bs, bs), full),
        in_specs=[vmem] * 4,
        out_specs=vmem,
        scratch_shapes=[
            pltpu.VMEM((2, FIRST, bs, bs), half),
            pltpu.VMEM((2, FIRST + DIAGS, bs, bs), half),
            pltpu.VMEM((2, FIRST, bs, bs), half),
            pltpu.VMEM((2, FIRST + DIAGS, bs, bs), half),
            pltpu.VMEM((2, 2, bs, bs), half),
            pltpu.VMEM((2, DIAGS - 1, bs, bs), half),
            pltpu.VMEM((2, DIAGS - 1, bs, bs), half),
            pltpu.VMEM((2, bs, bs), full),
            pltpu.VMEM((2, bs, bs), full),
            pltpu.VMEM((2, bs, bs), half),
            dma((2, FIRST)), dma((2, FIRST + DIAGS)), dma((2, FIRST)), dma((2, FIRST + DIAGS)),
            dma((2,)), dma((2, DIAGS - 1)), dma((2, DIAGS - 1)),
            dma((2, 5)), dma((2, FIRST, 2)), dma((2, FIRST, 2)), dma((2, FIRST)), dma((2, FIRST)),
            dma((2,)), dma((2, 2, DIAGS - 1)), dma((2, 2, DIAGS - 1)),
        ],
        compiler_params=pltpu.CompilerParams(
            collective_id=0, has_side_effects=True, vmem_limit_bytes=40 * 1024 * 1024
        ),
    )(schur, known, pairs, lam)


def body(schur_blocks, known_blocks, eigen_pairs, eigenvalues):
    known = known_blocks[:, 0, :, 0]
    solved = exchange(
        schur_blocks[:, 0, :, 0],
        known.astype(jnp.bfloat16),
        eigen_pairs[:, 0].astype(jnp.bfloat16),
        eigenvalues,
    )
    rows = lax.axis_index("row") + SIDE * jnp.arange(2)[:, None]
    cols = lax.axis_index("col") + SIDE * jnp.arange(2)[None, :]
    away = cols - rows
    new = (away >= FIRST) & (away < FIRST + DIAGS)
    output = jnp.where(new[:, :, None, None], solved[:, None], known)
    return output[:, None, :, None]


def solution(mesh):
    return jax.shard_map(
        body,
        mesh=mesh,
        in_specs=(
            P(None, "row", None, "col", None, None),
            P(None, "row", None, "col", None, None),
            P(None, "row", None, None, None),
            P(),
        ),
        out_specs=P(None, "row", None, "col", None, None),
        check_vma=False,
    )
```

```python
import jax
import jax.numpy as jnp
from jax import lax
from jax.experimental import pallas as pl
from jax.experimental.pallas import tpu as pltpu
from jax.sharding import PartitionSpec as P

FIRST = 8
DIAGS = 4
SIDE = 16
XS = 4
TOTAL = 32
MESH = pl.DeviceIdType.MESH


def arrived(ref, sem):
    pltpu.make_async_copy(ref, ref, sem).wait()


def wrap(x):
    return lax.rem(x + 2 * SIDE, SIDE)


def line_of(i):
    return lax.rem((i + FIRST) // XS + 2 * (i // SIDE), XS)


def dot(a, b):
    return jnp.dot(a, b, preferred_element_type=jnp.float32)


def halves(x):
    high = x.astype(jnp.bfloat16)
    return high, (x - high.astype(jnp.float32)).astype(jnp.bfloat16)


def left_dot(a, x):
    high, low = halves(x)
    return dot(a, high) + dot(a, low)


def right_dot(x, b):
    high, low = halves(x)
    return dot(high, b) + dot(low, b)


def kernel(
    schur, known, pairs, lam, out,
    row_f, row_s, col_f, col_s, vj, new_r, new_c, total, gap, fresh, solved,
    q_row_f, q_row_s, q_col_f, q_col_s, q_vj, q_new_r, q_new_c, q_out,
    s_src, s_ring_f, s_ring_s, s_chain_f, s_chain_s, s_chain_v, s_own, s_new, s_out,
):
    r = lax.axis_index("row")
    c = lax.axis_index("col")
    x_at, y_at = lax.rem(c, XS), c // XS
    e = wrap(c - r)
    later = []

    def remote(src, dst, send_sem, recv_sem, row, col):
        return pltpu.make_async_remote_copy(
            src_ref=src, dst_ref=dst, send_sem=send_sem, recv_sem=recv_sem,
            device_id=(row, col), device_id_type=MESH,
        )

    def run_if(cond, fn):
        pl.when(cond)(fn)

    def send(cond, *args):
        copy = remote(*args)
        run_if(cond, copy.start)
        later.append((cond, copy))

    def send_in_row(cond, src, dst, send_sem, recv_sem, col):
        run_if(cond & (col == c), pltpu.make_async_copy(src, dst, recv_sem).start)
        send(cond & (col != c), src, dst, send_sem, recv_sem, r, col)

    barrier = pltpu.get_barrier_semaphore()

    def meet(row, col):
        pl.semaphore_signal(barrier, inc=1, device_id=(row, col), device_id_type=MESH)

    def greet_line(step, carry):
        meet(lax.rem(r + step // XS, SIDE), XS * lax.rem(y_at + step, XS) + x_at)
        return carry

    def greet_row(step, carry):
        meet(r, XS * lax.rem(step, XS) + lax.rem(x_at + 1 + step // XS, XS))
        return carry

    lines = SIDE * XS - 1
    others = XS * (XS - 1)
    lax.fori_loop(1, lines + 1, greet_line, 0)
    lax.fori_loop(0, others, greet_row, 0)
    pl.semaphore_wait(barrier, lines + others)

    def seat(i):
        return wrap(i), XS * line_of(i) + x_at

    near = e < FIRST
    eb = jnp.minimum(e, FIRST - 1)
    places = []
    for t in (0, 1):
        k = r + SIDE * t
        j = k + e
        b = jnp.minimum(j // SIDE, 1)
        to_row = near & (k < TOTAL - FIRST)
        to_col = near & (j >= FIRST) & (j < TOTAL)
        last = jnp.minimum(DIAGS - 1, j - FIRST)
        i_to = jnp.maximum(j - FIRST - jnp.where(e >= DIAGS, 0, last), 0)
        places.append((b, to_row, to_col, seat(k)[1], seat(i_to)))
    for n, (ref, row_ref, col_ref, q_row, q_col) in enumerate(
        ((known, row_f, col_f, q_row_f, q_col_f), (schur, row_s, col_s, q_row_s, q_col_s))
    ):
        for t in (0, 1):
            b, to_row, to_col, col_to, entry = places[t]
            used = e >= n
            send_in_row(to_row & used, ref.at[t, b], row_ref.at[eb], s_src.at[t, 2 * n], q_row.at[eb], col_to)
            send(to_col & used, ref.at[t, b], col_ref.at[eb], s_src.at[t, 2 * n + 1], q_col.at[eb], *entry)

    mo = jnp.clip(e - FIRST, 0, DIAGS - 1)
    owner = (e >= FIRST) & (e < FIRST + DIAGS)
    owned = []
    for t in (0, 1):
        k = r + SIDE * t
        j = k + e
        b = jnp.minimum(j // SIDE, 1)
        slot = FIRST + mo
        owned.append(owner & (j < TOTAL))
        for d in range(DIAGS):
            fits = owner & (j + d < TOTAL) & (mo + d < DIAGS)
            col_to = XS * line_of(k) + lax.rem(x_at + d, XS)
            send_in_row(fits, schur.at[t, b], row_s.at[slot], s_own.at[t, 0, d], q_row_s.at[slot], col_to)
            if d:
                fits = owned[t] & (mo + d < DIAGS) & (k >= d)
                send(fits, schur.at[t, b], col_s.at[slot], s_own.at[t, 1, d], q_col_s.at[slot], *seat(jnp.maximum(k - d, 0)))

    for t in (0, 1):
        _, _, to_col, _, entry = places[t]
        send(to_col & (e == 0), pairs.at[t], vj, s_src.at[t, 4], q_vj.at[0], *entry)

    second = (r < TOTAL - SIDE - FIRST) & (y_at == r // XS)
    part = second | (y_at == line_of(r))
    t = jnp.where(second, 1, 0)
    i = r + SIDE * t
    m = lax.rem(x_at + SIDE - r, XS)
    j = i + FIRST + m
    real = part & (j < TOTAL)
    last = jnp.minimum(DIAGS - 1, i + m)
    up = real & (m < last)
    down = real & (m > 0)
    col_next = (XS * y_at + lax.rem(x_at + 1, XS), XS * y_at + lax.rem(x_at + XS - 1, XS))

    @pl.when(real)
    def _():
        rows = jnp.broadcast_to(lam[pl.ds(i, 1), :], total.shape).T
        gap[...] = 1.0 / (rows - lam[pl.ds(jnp.minimum(j, TOTAL - 1), 1), :])
        total[...] = jnp.zeros(total.shape, jnp.float32)

    kinds = (
        (row_f, q_row_f, s_ring_f, 0, col_f, s_chain_f, q_col_f),
        (row_s, q_row_s, s_ring_s, 1, col_s, s_chain_s, q_col_s),
    )

    def ring(kind, x, d):
        ref, sems, send_sems = kind[:3]
        return remote(ref.at[x], ref.at[x], send_sems.at[x, d], sems.at[x], r, col_next[d])

    def chain(kind, x, step):
        ref, send_sems, sems = kind[4:]
        return remote(ref.at[x], ref.at[x], send_sems.at[x], sems.at[x], *seat(jnp.maximum(i - step, 0)))

    def chain_v():
        return remote(vj, vj, s_chain_v.at[0], q_vj.at[0], *seat(i + 1))

    def row_entry(kind, start):
        ref, sems, least = kind[0], kind[1], kind[3]
        for x in (m, m + DIAGS):

            @pl.when(part & (x >= least))
            def _():
                if start:
                    arrived(ref.at[x], sems.at[x])
                    ring(kind, x, 0).start()
                    ring(kind, x, 1).start()
                else:
                    ring(kind, x, 0).wait_send()
                    ring(kind, x, 1).wait_send()

    def row_relay(kind, start):
        ref, sems, least = kind[0], kind[1], kind[3]
        base = lax.rem(m + (1 if least else DIAGS - 1), DIAGS)
        for x in (base, base + DIAGS):

            @pl.when(part & (x >= least))
            def _():
                if start:
                    arrived(ref.at[x], sems.at[x])
                    ring(kind, x, least).start()
                else:
                    ring(kind, x, least).wait_send()

    def col_relay(kind, depths, start):
        ref, _, sems = kind[4:]
        up_now, down_now = jnp.bool_(False), jnp.bool_(False)
        for depth in depths:
            up_now |= up & (m == depth)
            down_now |= down & (last - m == depth)

        def move(x, step):
            copy = chain(kind, x, step)
            if start:
                arrived(ref.at[x], sems.at[x])
                copy.start()
            else:
                copy.wait_send()

        def step(x, carry):
            run_if(up_now, lambda: move(x + DIAGS, 1))
            run_if(down_now & (x >= kind[3]), lambda: move(x, -1))
            return carry

        lax.fori_loop(0, DIAGS, step, 0)

    def first_hops(kind):
        row_entry(kind, True)
        col_relay(kind, (0,), True)
        col_relay(kind, (1,), True)

    def second_hops(kind):
        row_relay(kind, True)
        col_relay(kind, (2,), True)

    first_hops(kinds[0])
    first_hops(kinds[1])
    second_hops(kinds[0])
    second_hops(kinds[1])
    for depth in range(DIAGS - 1):

        @pl.when(down & (last - m == depth))
        def _():
            arrived(vj, q_vj.at[0])
            chain_v().start()

    def rest_f(x, carry):
        away = lax.rem(m - x + 2 * DIAGS, DIAGS)
        ends = jnp.where(x >= DIAGS, ~up, ~down)
        run_if(part & (away >= 2), lambda: arrived(row_f.at[x], q_row_f.at[x]))
        run_if(real & ends, lambda: arrived(col_f.at[x], q_col_f.at[x]))
        return carry

    lax.fori_loop(0, FIRST, rest_f, 0)

    def far(x, carry):
        @pl.when(real & (x < FIRST + m))
        def _():
            arrived(row_s.at[x], q_row_s.at[x])
            arrived(col_s.at[x], q_col_s.at[x])
            near_x = FIRST + m - x
            total[...] += dot(row_f[near_x], col_s[x]) - dot(row_s[x], col_f[near_x])

        @pl.when(real & (x == FIRST + m))
        def _():
            arrived(row_s.at[x], q_row_s.at[x])
            total[...] += dot(row_f[0], row_s[x]) - dot(row_s[x], col_f[0])

        return carry

    lax.fori_loop(FIRST, FIRST + DIAGS, far, 0)

    def rest_s(x, carry):
        away = lax.rem(m - x + 2 * DIAGS, DIAGS)
        ends = jnp.where(x >= DIAGS, ~up, ~down)
        run_if(part & ((away == 1) | (away == 2)), lambda: arrived(row_s.at[x], q_row_s.at[x]))
        run_if(real & ends, lambda: arrived(col_s.at[x], q_col_s.at[x]))

        @pl.when(real & (x > m))
        def _():
            near_x = FIRST + m - x
            total[...] += dot(row_f[near_x], col_s[x]) - dot(row_s[x], col_f[near_x])

        return carry

    lax.fori_loop(1, FIRST, rest_s, 0)
    run_if(real & ~down, lambda: arrived(vj, q_vj.at[0]))

    for before in range(DIAGS - 1):

        @pl.when(real & (m > before))
        def _():
            near_x = m - before
            arrived(new_r.at[before], q_new_r.at[before])
            arrived(new_c.at[before], q_new_c.at[before])
            total[...] += dot(new_r[before], col_s[near_x]) - dot(row_s[near_x], new_c[before])

    @pl.when(real)
    def _():
        x = left_dot(pairs[t, 1], total[...])
        x = right_dot(x, vj[0]) * gap[...]
        x = left_dot(pairs[t, 0], x)
        x = right_dot(x, vj[1])
        fresh[...] = x.astype(jnp.bfloat16)
        solved[...] = x

    mine = jnp.minimum(m, DIAGS - 2)
    for d in range(1, DIAGS):
        fits = real & (m + d < DIAGS)
        send(fits & (j + d < TOTAL), fresh, new_r.at[mine], s_new.at[0, d - 1], q_new_r.at[mine], r, XS * y_at + lax.rem(x_at + d, XS))
        send(fits & (i >= d), fresh, new_c.at[mine], s_new.at[1, d - 1], q_new_c.at[mine], *seat(jnp.maximum(i - d, 0)))
    send_in_row(real, solved, out.at[t], s_out.at[0], q_out.at[t], lax.rem(j, SIDE))

    for n in (0, 1):
        run_if(owned[n], lambda: arrived(out.at[n], q_out.at[n]))

    for cond, copy in later:
        run_if(cond, copy.wait_send)
    for kind in kinds:
        row_entry(kind, False)
        row_relay(kind, False)
        col_relay(kind, (0, 1, 2), False)
    run_if(down, lambda: chain_v().wait_send())


def exchange(schur, known, pairs, lam):
    bs = schur.shape[-1]
    half, full = jnp.bfloat16, jnp.float32
    dma = pltpu.SemaphoreType.DMA
    vmem = pl.BlockSpec(memory_space=pltpu.VMEM)
    return pl.pallas_call(
        kernel,
        out_shape=jax.ShapeDtypeStruct((2, bs, bs), full),
        in_specs=[vmem] * 4,
        out_specs=vmem,
        scratch_shapes=[
            pltpu.VMEM((FIRST, bs, bs), half),
            pltpu.VMEM((FIRST + DIAGS, bs, bs), half),
            pltpu.VMEM((FIRST, bs, bs), half),
            pltpu.VMEM((FIRST + DIAGS, bs, bs), half),
            pltpu.VMEM((2, bs, bs), half),
            pltpu.VMEM((DIAGS - 1, bs, bs), half),
            pltpu.VMEM((DIAGS - 1, bs, bs), half),
            pltpu.VMEM((bs, bs), full),
            pltpu.VMEM((bs, bs), full),
            pltpu.VMEM((bs, bs), half),
            pltpu.VMEM((bs, bs), full),
            dma((FIRST,)), dma((FIRST + DIAGS,)), dma((FIRST,)), dma((FIRST + DIAGS,)),
            dma((1,)), dma((DIAGS - 1,)), dma((DIAGS - 1,)), dma((2,)),
            dma((2, 5)), dma((FIRST, 2)), dma((FIRST, 2)), dma((FIRST,)), dma((FIRST,)),
            dma((1,)), dma((2, 2, DIAGS)), dma((2, DIAGS - 1)), dma((1,)),
        ],
        compiler_params=pltpu.CompilerParams(
            collective_id=0, has_side_effects=True, vmem_limit_bytes=40 * 1024 * 1024
        ),
    )(schur, known, pairs, lam)


def body(schur_blocks, known_blocks, eigen_pairs, eigenvalues):
    known = known_blocks[:, 0, :, 0]
    solved = exchange(
        schur_blocks[:, 0, :, 0],
        known.astype(jnp.bfloat16),
        eigen_pairs[:, 0].astype(jnp.bfloat16),
        eigenvalues,
    )
    rows = lax.axis_index("row") + SIDE * jnp.arange(2)[:, None]
    cols = lax.axis_index("col") + SIDE * jnp.arange(2)[None, :]
    away = cols - rows
    new = (away >= FIRST) & (away < FIRST + DIAGS)
    output = jnp.where(new[:, :, None, None], solved[:, None], known)
    return output[:, None, :, None]


def solution(mesh):
    return jax.shard_map(
        body,
        mesh=mesh,
        in_specs=(
            P(None, "row", None, "col", None, None),
            P(None, "row", None, "col", None, None),
            P(None, "row", None, None, None),
            P(),
        ),
        out_specs=P(None, "row", None, "col", None, None),
        check_vma=False,
    )
```

```python
import jax
import jax.numpy as jnp
from jax import lax
from jax.experimental import pallas as pl
from jax.experimental.pallas import tpu as pltpu
from jax.sharding import PartitionSpec as P

FIRST = 8
DIAGS = 4
SIDE = 16
XS = 4
TOTAL = 32
MESH = pl.DeviceIdType.MESH

SENDS = ("cF0", "cF1", "rF1", "rS0", "rF0", "rS1", "cS0", "cS1", "own", "v")
WAITS = ("eF", "0F", "1F", "eS", "0S", "lS", "2F", "1S", "lF", "v0", "v1", "2S", "v2")
TURN = {"F": 1, "S": 1}


def arrived(ref, sem):
    pltpu.make_async_copy(ref, ref, sem).wait()


def wrap(x):
    return lax.rem(x + 2 * SIDE, SIDE)


def line_of(i):
    return lax.rem((i + FIRST) // XS + i // SIDE, XS)


def dot(a, b):
    return jnp.dot(a, b, preferred_element_type=jnp.float32)


def halves(x):
    high = x.astype(jnp.bfloat16)
    return high, (x - high.astype(jnp.float32)).astype(jnp.bfloat16)


def left_dot(a, x):
    high, low = halves(x)
    return dot(a, high) + dot(a, low)


def right_dot(x, b):
    high, low = halves(x)
    return dot(high, b) + dot(low, b)


def kernel(
    schur, known, pairs, lam, out,
    row_f, row_s, col_f, col_s, vj, new_r, new_c, total, gap, fresh, solved,
    q_row_f, q_row_s, q_col_f, q_col_s, q_vj, q_new_r, q_new_c, q_out,
    s_src, s_ring_f, s_ring_s, s_chain_f, s_chain_s, s_chain_v, s_own, s_new, s_out,
):
    r = lax.axis_index("row")
    c = lax.axis_index("col")
    x_at, y_at = lax.rem(c, XS), c // XS
    e = wrap(c - r)
    later = []

    def remote(src, dst, send_sem, recv_sem, row, col):
        return pltpu.make_async_remote_copy(
            src_ref=src, dst_ref=dst, send_sem=send_sem, recv_sem=recv_sem,
            device_id=(row, col), device_id_type=MESH,
        )

    def run_if(cond, fn):
        pl.when(cond)(fn)

    def send(cond, *args):
        copy = remote(*args)
        run_if(cond, copy.start)
        later.append((cond, copy))

    def send_in_row(cond, src, dst, send_sem, recv_sem, col):
        run_if(cond & (col == c), pltpu.make_async_copy(src, dst, recv_sem).start)
        send(cond & (col != c), src, dst, send_sem, recv_sem, r, col)

    barrier = pltpu.get_barrier_semaphore()

    def meet(row, col):
        pl.semaphore_signal(barrier, inc=1, device_id=(row, col), device_id_type=MESH)

    def greet_line(step, carry):
        meet(lax.rem(r + step // XS, SIDE), XS * lax.rem(y_at + step, XS) + x_at)
        return carry

    def greet_row(step, carry):
        meet(r, XS * lax.rem(step, XS) + lax.rem(x_at + 1 + step // XS, XS))
        return carry

    lines = SIDE * XS - 1
    others = XS * (XS - 1)
    lax.fori_loop(1, lines + 1, greet_line, 0)
    lax.fori_loop(0, others, greet_row, 0)
    pl.semaphore_wait(barrier, lines + others)

    def seat(i):
        return wrap(i), XS * line_of(i) + x_at

    near = e < FIRST
    eb = jnp.minimum(e, FIRST - 1)
    places = []
    for t in (0, 1):
        k = r + SIDE * t
        j = k + e
        b = jnp.minimum(j // SIDE, 1)
        to_row = near & (k < TOTAL - FIRST)
        to_col = near & (j >= FIRST) & (j < TOTAL)
        last = jnp.minimum(DIAGS - 1, j - FIRST)
        i_to = jnp.maximum(j - FIRST - jnp.where(e >= DIAGS, 0, last), 0)
        places.append((b, to_row, to_col, seat(k)[1], seat(i_to)))
    def send_near(group, kind, t):
        n = "FS".index(kind)
        b, to_row, to_col, col_to, entry = places[t]
        ref = (known, schur)[n]
        used = e >= n
        if group == "r":
            dst, sems = ((row_f, q_row_f), (row_s, q_row_s))[n]
            send_in_row(to_row & used, ref.at[t, b], dst.at[eb], s_src.at[t, 2 * n], sems.at[eb], col_to)
        else:
            dst, sems = ((col_f, q_col_f), (col_s, q_col_s))[n]
            send(to_col & used, ref.at[t, b], dst.at[eb], s_src.at[t, 2 * n + 1], sems.at[eb], *entry)

    mo = jnp.clip(e - FIRST, 0, DIAGS - 1)
    owner = (e >= FIRST) & (e < FIRST + DIAGS)
    owned = [owner & (r + SIDE * t + e < TOTAL) for t in (0, 1)]

    def send_own(t):
        k = r + SIDE * t
        j = k + e
        b = jnp.minimum(j // SIDE, 1)
        slot = FIRST + mo
        for d in range(DIAGS):
            fits = owner & (j + d < TOTAL) & (mo + d < DIAGS)
            col_to = XS * line_of(k) + lax.rem(x_at + d, XS)
            send_in_row(fits, schur.at[t, b], row_s.at[slot], s_own.at[t, 0, d], q_row_s.at[slot], col_to)
            if d:
                fits = owned[t] & (mo + d < DIAGS) & (k >= d)
                send(fits, schur.at[t, b], col_s.at[slot], s_own.at[t, 1, d], q_col_s.at[slot], *seat(jnp.maximum(k - d, 0)))

    for token in SENDS:
        if token == "own":
            send_own(0)
            send_own(1)
        elif token == "v":
            for t in (0, 1):
                _, _, to_col, _, entry = places[t]
                send(to_col & (e == 0), pairs.at[t], vj, s_src.at[t, 4], q_vj.at[0], *entry)
        else:
            send_near(token[0], token[1], int(token[2]))

    second = (r < TOTAL - SIDE - FIRST) & (y_at == line_of(r + SIDE))
    part = second | (y_at == line_of(r))
    t = jnp.where(second, 1, 0)
    i = r + SIDE * t
    m = lax.rem(x_at + SIDE - r, XS)
    j = i + FIRST + m
    real = part & (j < TOTAL)
    last = jnp.minimum(DIAGS - 1, i + m)
    up = real & (m < last)
    down = real & (m > 0)
    col_next = (XS * y_at + lax.rem(x_at + 1, XS), XS * y_at + lax.rem(x_at + XS - 1, XS))

    @pl.when(real)
    def _():
        rows = jnp.broadcast_to(lam[pl.ds(i, 1), :], total.shape).T
        gap[...] = 1.0 / (rows - lam[pl.ds(jnp.minimum(j, TOTAL - 1), 1), :])
        total[...] = jnp.zeros(total.shape, jnp.float32)

    kinds = (
        (row_f, q_row_f, s_ring_f, 0, col_f, s_chain_f, q_col_f),
        (row_s, q_row_s, s_ring_s, 1, col_s, s_chain_s, q_col_s),
    )

    def ring(kind, x, d):
        ref, sems, send_sems = kind[:3]
        return remote(ref.at[x], ref.at[x], send_sems.at[x, d], sems.at[x], r, col_next[d])

    def chain(kind, x, step):
        ref, send_sems, sems = kind[4:]
        return remote(ref.at[x], ref.at[x], send_sems.at[x], sems.at[x], *seat(jnp.maximum(i - step, 0)))

    def chain_v():
        return remote(vj, vj, s_chain_v.at[0], q_vj.at[0], *seat(i + 1))

    def row_entry(kind, start):
        ref, sems, least = kind[0], kind[1], kind[3]
        for x in (m, m + DIAGS):

            @pl.when(part & (x >= least))
            def _():
                if start:
                    arrived(ref.at[x], sems.at[x])
                    ring(kind, x, 0).start()
                    ring(kind, x, 1).start()
                else:
                    ring(kind, x, 0).wait_send()
                    ring(kind, x, 1).wait_send()

    def row_relay(kind, start):
        ref, sems, least = kind[0], kind[1], kind[3]
        turn = TURN["FS"[least]]
        base = lax.rem(m + DIAGS - turn, DIAGS)
        for x in (base, base + DIAGS):

            @pl.when(part & (x >= least))
            def _():
                copy = ring(kind, x, 0 if turn == 1 else 1)
                if start:
                    arrived(ref.at[x], sems.at[x])
                    copy.start()
                else:
                    copy.wait_send()

    def col_relay(kind, depths, start):
        ref, _, sems = kind[4:]
        up_now, down_now = jnp.bool_(False), jnp.bool_(False)
        for depth in depths:
            up_now |= up & (m == depth)
            down_now |= down & (last - m == depth)

        def move(x, step):
            copy = chain(kind, x, step)
            if start:
                arrived(ref.at[x], sems.at[x])
                copy.start()
            else:
                copy.wait_send()

        def step(x, carry):
            run_if(up_now, lambda: move(x + DIAGS, 1))
            run_if(down_now & (x >= kind[3]), lambda: move(x, -1))
            return carry

        lax.fori_loop(0, DIAGS, step, 0)

    for token in WAITS:
        if token[0] == "v":
            depth = int(token[1])

            @pl.when(down & (last - m == depth))
            def _():
                arrived(vj, q_vj.at[0])
                chain_v().start()

        else:
            kind = kinds["FS".index(token[1])]
            if token[0] == "e":
                row_entry(kind, True)
            elif token[0] == "l":
                row_relay(kind, True)
            else:
                col_relay(kind, (int(token[0]),), True)

    def kept(kind, x):
        away = lax.rem(m - x + 2 * DIAGS, DIAGS)
        relay = 1 if TURN[kind] == 1 else DIAGS - 1
        return part & (away != 0) & (away != relay)

    def rest_f(x, carry):
        ends = jnp.where(x >= DIAGS, ~up, ~down)
        run_if(kept("F", x), lambda: arrived(row_f.at[x], q_row_f.at[x]))
        run_if(real & ends, lambda: arrived(col_f.at[x], q_col_f.at[x]))
        return carry

    lax.fori_loop(0, FIRST, rest_f, 0)

    def far(x, carry):
        @pl.when(real & (x < FIRST + m))
        def _():
            arrived(row_s.at[x], q_row_s.at[x])
            arrived(col_s.at[x], q_col_s.at[x])
            near_x = FIRST + m - x
            total[...] += dot(row_f[near_x], col_s[x]) - dot(row_s[x], col_f[near_x])

        @pl.when(real & (x == FIRST + m))
        def _():
            arrived(row_s.at[x], q_row_s.at[x])
            total[...] += dot(row_f[0], row_s[x]) - dot(row_s[x], col_f[0])

        return carry

    lax.fori_loop(FIRST, FIRST + DIAGS, far, 0)

    def rest_s(x, carry):
        ends = jnp.where(x >= DIAGS, ~up, ~down)
        run_if(kept("S", x), lambda: arrived(row_s.at[x], q_row_s.at[x]))
        run_if(real & ends, lambda: arrived(col_s.at[x], q_col_s.at[x]))

        @pl.when(real & (x > m))
        def _():
            near_x = FIRST + m - x
            total[...] += dot(row_f[near_x], col_s[x]) - dot(row_s[x], col_f[near_x])

        return carry

    lax.fori_loop(1, FIRST, rest_s, 0)
    run_if(real & ~down, lambda: arrived(vj, q_vj.at[0]))

    for before in range(DIAGS - 1):

        @pl.when(real & (m > before))
        def _():
            near_x = m - before
            arrived(new_r.at[before], q_new_r.at[before])
            arrived(new_c.at[before], q_new_c.at[before])
            total[...] += dot(new_r[before], col_s[near_x]) - dot(row_s[near_x], new_c[before])

    @pl.when(real)
    def _():
        x = left_dot(pairs[t, 1], total[...])
        x = right_dot(x, vj[0]) * gap[...]
        x = left_dot(pairs[t, 0], x)
        x = right_dot(x, vj[1])
        fresh[...] = x.astype(jnp.bfloat16)
        solved[...] = x

    mine = jnp.minimum(m, DIAGS - 2)
    for d in range(1, DIAGS):
        fits = real & (m + d < DIAGS)
        send(fits & (j + d < TOTAL), fresh, new_r.at[mine], s_new.at[0, d - 1], q_new_r.at[mine], r, XS * y_at + lax.rem(x_at + d, XS))
        send(fits & (i >= d), fresh, new_c.at[mine], s_new.at[1, d - 1], q_new_c.at[mine], *seat(jnp.maximum(i - d, 0)))
    send_in_row(real, solved, out.at[t], s_out.at[0], q_out.at[t], lax.rem(j, SIDE))

    for n in (0, 1):
        run_if(owned[n], lambda: arrived(out.at[n], q_out.at[n]))

    for cond, copy in later:
        run_if(cond, copy.wait_send)
    for kind in kinds:
        row_entry(kind, False)
        row_relay(kind, False)
        col_relay(kind, (0, 1, 2), False)
    run_if(down, lambda: chain_v().wait_send())


def exchange(schur, known, pairs, lam):
    bs = schur.shape[-1]
    half, full = jnp.bfloat16, jnp.float32
    dma = pltpu.SemaphoreType.DMA
    vmem = pl.BlockSpec(memory_space=pltpu.VMEM)
    return pl.pallas_call(
        kernel,
        out_shape=jax.ShapeDtypeStruct((2, bs, bs), full),
        in_specs=[vmem] * 4,
        out_specs=vmem,
        scratch_shapes=[
            pltpu.VMEM((FIRST, bs, bs), half),
            pltpu.VMEM((FIRST + DIAGS, bs, bs), half),
            pltpu.VMEM((FIRST, bs, bs), half),
            pltpu.VMEM((FIRST + DIAGS, bs, bs), half),
            pltpu.VMEM((2, bs, bs), half),
            pltpu.VMEM((DIAGS - 1, bs, bs), half),
            pltpu.VMEM((DIAGS - 1, bs, bs), half),
            pltpu.VMEM((bs, bs), full),
            pltpu.VMEM((bs, bs), full),
            pltpu.VMEM((bs, bs), half),
            pltpu.VMEM((bs, bs), full),
            dma((FIRST,)), dma((FIRST + DIAGS,)), dma((FIRST,)), dma((FIRST + DIAGS,)),
            dma((1,)), dma((DIAGS - 1,)), dma((DIAGS - 1,)), dma((2,)),
            dma((2, 5)), dma((FIRST, 2)), dma((FIRST, 2)), dma((FIRST,)), dma((FIRST,)),
            dma((1,)), dma((2, 2, DIAGS)), dma((2, DIAGS - 1)), dma((1,)),
        ],
        compiler_params=pltpu.CompilerParams(
            collective_id=0, has_side_effects=True, vmem_limit_bytes=40 * 1024 * 1024
        ),
    )(schur, known, pairs, lam)


def body(schur_blocks, known_blocks, eigen_pairs, eigenvalues):
    known = known_blocks[:, 0, :, 0]
    solved = exchange(
        schur_blocks[:, 0, :, 0],
        known.astype(jnp.bfloat16),
        eigen_pairs[:, 0].astype(jnp.bfloat16),
        eigenvalues,
    )
    rows = lax.axis_index("row") + SIDE * jnp.arange(2)[:, None]
    cols = lax.axis_index("col") + SIDE * jnp.arange(2)[None, :]
    away = cols - rows
    new = (away >= FIRST) & (away < FIRST + DIAGS)
    output = jnp.where(new[:, :, None, None], solved[:, None], known)
    return output[:, None, :, None]


def solution(mesh):
    return jax.shard_map(
        body,
        mesh=mesh,
        in_specs=(
            P(None, "row", None, "col", None, None),
            P(None, "row", None, "col", None, None),
            P(None, "row", None, None, None),
            P(),
        ),
        out_specs=P(None, "row", None, "col", None, None),
        check_vma=False,
    )
```

```python
import jax
import jax.numpy as jnp
from jax import lax
from jax.experimental import pallas as pl
from jax.experimental.pallas import tpu as pltpu
from jax.sharding import PartitionSpec as P

FIRST = 8
DIAGS = 4
SIDE = 16
XS = 4
TOTAL = 32
AWAY = 4
MESH = pl.DeviceIdType.MESH

SENDS = ("cF0", "cS0", "cF1", "cS1", "rF0", "rS0", "rF1", "rS1", "own", "x", "v")
WAITS = (("0", "e", "1", "l", "2", "v0", "v1", "v2"), ("0", "e", "1", "l", "2", "3"))
ENTRY = ((3, 3, 3, 3, 0, 0, 0, 0), (0, 0, 0, 0, 0, 1, 2, 3))
TURN = ((1, 1), (1, 1))
CHAIN_ORDER = (4, 0, 5, 1, 6, 2, 7, 3)


def arrived(ref, sem):
    pltpu.make_async_copy(ref, ref, sem).wait()


def wrap(x):
    return lax.rem(x + 2 * SIDE, SIDE)


def line_of(i, second):
    return lax.rem((i + FIRST) // XS + (1 + 2 * second) * (i // SIDE), XS)


def pick(index, table):
    chosen = jnp.int32(table[0])
    for n, value in enumerate(table[1:], 1):
        chosen = jnp.where(index == n, value, chosen)
    return chosen


def dot(a, b):
    return jnp.dot(a, b, preferred_element_type=jnp.float32)


def halves(x):
    high = x.astype(jnp.bfloat16)
    return high, (x - high.astype(jnp.float32)).astype(jnp.bfloat16)


def left_dot(a, x):
    high, low = halves(x)
    return dot(a, high) + dot(a, low)


def right_dot(x, b):
    high, low = halves(x)
    return dot(high, b) + dot(low, b)


def kernel(
    schur, known, pairs, lam, out,
    ring, chain, near_s, vj, new_r, new_c, other, total, gap, fresh, solved,
    q_ring, q_chain, q_near, q_vj, q_new_r, q_new_c, q_other, q_out,
    s_src, s_ring, s_chain, s_v, s_own, s_near, s_new, s_out,
):
    r = lax.axis_index("row")
    c = lax.axis_index("col")
    x_at, y_at = lax.rem(c, XS), c // XS
    e = wrap(c - r)
    later = []

    def remote(src, dst, send_sem, recv_sem, row, col):
        return pltpu.make_async_remote_copy(
            src_ref=src, dst_ref=dst, send_sem=send_sem, recv_sem=recv_sem,
            device_id=(row, col), device_id_type=MESH,
        )

    def run_if(cond, fn):
        pl.when(cond)(fn)

    def send(cond, src, dst, send_sem, recv_sem, row, col):
        copy = remote(src, dst, send_sem, recv_sem, row, col)
        run_if(cond, copy.start)
        later.append((cond, copy))

    def send_any(cond, src, dst, send_sem, recv_sem, row, col):
        here = (row == r) & (col == c)
        run_if(cond & here, pltpu.make_async_copy(src, dst, recv_sem).start)
        send(cond & ~here, src, dst, send_sem, recv_sem, row, col)

    def seat(i, second, x=x_at):
        return wrap(i + AWAY * second), XS * line_of(i, second) + x

    barrier = pltpu.get_barrier_semaphore()

    def meet(row, col):
        pl.semaphore_signal(barrier, inc=1, device_id=(row, col), device_id_type=MESH)

    def greet_line(step, carry):
        meet(lax.rem(r + step // XS, SIDE), XS * lax.rem(y_at + step, XS) + x_at)
        return carry

    def greet_row(step, carry):
        col = XS * lax.rem(step, XS) + lax.rem(x_at + 1 + step // XS, XS)
        meet(r, col)
        meet(wrap(r + AWAY), col)
        meet(wrap(r - AWAY), col)
        return carry

    lines = SIDE * XS - 1
    others = XS * (XS - 1)
    lax.fori_loop(1, lines + 1, greet_line, 0)
    lax.fori_loop(0, others, greet_row, 0)
    pl.semaphore_wait(barrier, lines + 3 * others)

    near = e < FIRST
    eb = jnp.minimum(e, FIRST - 1)
    places = []
    for t in (0, 1):
        k = r + SIDE * t
        j = k + e
        b = jnp.minimum(j // SIDE, 1)
        last = jnp.clip(j - FIRST, 0, DIAGS - 1)
        to_ring = near & (k < TOTAL - FIRST)
        to_chain = near & (j >= FIRST) & (j < TOTAL)
        entries = [
            seat(jnp.maximum(j - FIRST - jnp.minimum(pick(eb, ENTRY[n]), last), 0), n) for n in (0, 1)
        ]
        v_entry = seat(jnp.maximum(j - FIRST - last, 0), 0)
        places.append((k, j, b, to_ring, to_chain, entries, v_entry))

    mo = jnp.clip(e - FIRST, 0, DIAGS - 1)
    owner = (e >= FIRST) & (e < FIRST + DIAGS)
    owned = [owner & (places[t][1] < TOTAL) for t in (0, 1)]

    def send_near(group, kind, t):
        k, j, b, to_ring, to_chain, entries, _ = places[t]
        n = "FS".index(kind)
        src = (known, schur)[n].at[t, b]
        used = e >= n
        at = 2 * n + (group == "c")
        if group == "r":
            send_any(to_ring & used, src, ring.at[eb], s_src.at[t, at], q_ring.at[eb], *seat(k, n))
        else:
            send_any(to_chain & used, src, chain.at[eb], s_src.at[t, at], q_chain.at[eb], *entries[1 - n])

    def send_own(t):
        k, j, b = places[t][:3]
        slot = FIRST + mo
        for d in range(DIAGS):
            fits = owner & (j + d < TOTAL) & (mo + d < DIAGS)
            send(fits, schur.at[t, b], ring.at[slot], s_own.at[t, 0, d], q_ring.at[slot], *seat(k, 1, lax.rem(x_at + d, XS)))
            fits = owned[t] & (mo + d < DIAGS) & (k >= d)
            send_any(fits, schur.at[t, b], chain.at[slot], s_own.at[t, 1, d], q_chain.at[slot], *seat(jnp.maximum(k - d, 0), 0))

    def send_close(t):
        k, j, b = places[t][:3]
        slot = jnp.clip(e - 1, 0, DIAGS - 2)
        for d in range(DIAGS - 1):
            fits = (e >= 1) & (e + d < DIAGS) & (j + FIRST + d < TOTAL)
            send_any(fits, schur.at[t, b], near_s.at[slot], s_near.at[t, d], q_near.at[slot], *seat(k, 0, lax.rem(x_at + d, XS)))

    for token in SENDS:
        if token == "own":
            send_own(0)
            send_own(1)
        elif token == "x":
            send_close(0)
            send_close(1)
        elif token == "v":
            for t in (0, 1):
                send(places[t][4] & (e == 0), pairs.at[t], vj, s_src.at[t, 4], q_vj.at[0], *places[t][6])
        else:
            send_near(token[0], token[1], int(token[2]))

    i0 = wrap(r - AWAY)
    few = TOTAL - SIDE - FIRST
    first0, first1 = y_at == line_of(r, 0), (r < few) & (y_at == line_of(r + SIDE, 0))
    second0, second1 = y_at == line_of(i0, 1), (i0 < few) & (y_at == line_of(i0 + SIDE, 1))
    is_second = second0 | second1
    part = first0 | first1 | is_second
    kind = jnp.where(is_second, 1, 0)
    t = jnp.where(first1 | second1, 1, 0)
    i = jnp.where(is_second, i0, r) + SIDE * t
    m = lax.rem(x_at + 2 * SIDE - i, XS)
    j = i + FIRST + m
    real = part & (j < TOTAL)
    last = jnp.minimum(DIAGS - 1, i + m)
    takes = (part & ~is_second, is_second)
    adds = (real & ~is_second, real & is_second)
    col_next = (XS * y_at + lax.rem(x_at + 1, XS), XS * y_at + lax.rem(x_at + XS - 1, XS))

    @pl.when(adds[0])
    def _():
        rows = jnp.broadcast_to(lam[pl.ds(i, 1), :], total.shape).T
        gap[...] = 1.0 / (rows - lam[pl.ds(jnp.minimum(j, TOTAL - 1), 1), :])

    @pl.when(real)
    def _():
        total[...] = jnp.zeros(total.shape, jnp.float32)

    def member(step):
        return seat(jnp.maximum(i - step, 0), kind)

    def ring_copy(x, d):
        return remote(ring.at[x], ring.at[x], s_ring.at[x, d], q_ring.at[x], r, col_next[d])

    def chain_copy(x, d):
        return remote(chain.at[x], chain.at[x], s_chain.at[x, d], q_chain.at[x], *member(1 - 2 * d))

    def v_copy():
        return remote(vj, vj, s_v.at[0], q_vj.at[0], *member(-1))

    def ring_first(n, start):
        for x in (m, m + DIAGS):

            @pl.when(takes[n] & (x >= n))
            def _():
                if start:
                    arrived(ring.at[x], q_ring.at[x])
                for d in (0, 1):
                    ring_copy(x, d).start() if start else ring_copy(x, d).wait_send()

    def ring_second(n, start):
        for high in (0, 1):
            turn = TURN[n][high]
            x = lax.rem(m + DIAGS - turn, DIAGS) + DIAGS * high

            @pl.when(takes[n] & (x >= n))
            def _():
                copy = ring_copy(x, 0 if turn == 1 else 1)
                if start:
                    arrived(ring.at[x], q_ring.at[x])
                    copy.start()
                else:
                    copy.wait_send()

    def chain_moves(n, x):
        at = jnp.minimum(ENTRY[n][x], last)
        up = adds[n] & (m >= at) & (m < last)
        down = adds[n] & (m <= at) & (m > 0)
        return up, down, jnp.abs(m - at)

    def chain_slots(n):
        return [x for x in CHAIN_ORDER if x + n > 0]

    def chain_hop(n, depth):
        for x in chain_slots(n):
            up, down, hops = chain_moves(n, x)
            now = hops == depth
            run_if((up | down) & now, lambda: arrived(chain.at[x], q_chain.at[x]))
            run_if(up & now, chain_copy(x, 0).start)
            run_if(down & now, chain_copy(x, 1).start)

    v_moves = adds[0] & (m > 0)

    def v_hop(depth):
        @pl.when(v_moves & (last - m == depth))
        def _():
            arrived(vj, q_vj.at[0])
            v_copy().start()

    for n in (0, 1):
        for token in WAITS[n]:
            if token == "e":
                ring_first(n, True)
            elif token == "l":
                ring_second(n, True)
            elif token[0] == "v":
                v_hop(int(token[1]))
            else:
                chain_hop(n, int(token))

    def ring_rest(n, x):
        away = lax.rem(m - x + 2 * DIAGS, DIAGS)
        turn = TURN[n][x // DIAGS]
        mine = takes[n] & (away != 0) & (away != lax.rem(turn + DIAGS, DIAGS))
        run_if(mine, lambda: arrived(ring.at[x], q_ring.at[x]))

    def chain_rest(n, x):
        up, down, _ = chain_moves(n, x)
        run_if(adds[n] & ~(up | down), lambda: arrived(chain.at[x], q_chain.at[x]))

    def accumulate(x):
        other_x = FIRST + m - x
        total[...] += dot(ring[jnp.where(is_second, x, other_x)], chain[jnp.where(is_second, other_x, x)])

    for x in range(FIRST):
        ring_rest(0, x)
        chain_rest(1, x)

    def far(x, carry):
        @pl.when(real & (x <= FIRST + m))
        def _():
            run_if(~is_second, lambda: arrived(chain.at[x], q_chain.at[x]))
            run_if(is_second, lambda: arrived(ring.at[x], q_ring.at[x]))
            accumulate(x)

        return carry

    lax.fori_loop(FIRST, FIRST + DIAGS, far, 0)
    for x in range(1, FIRST):
        chain_rest(0, x)
        ring_rest(1, x)
        run_if(real & (x > m), lambda: accumulate(x))

    @pl.when(adds[1])
    def _():
        fresh[...] = total[...].astype(jnp.bfloat16)

    send(adds[1], fresh, other, s_out.at[1], q_other.at[0], *seat(i, 0))

    @pl.when(adds[0])
    def _():
        arrived(other, q_other.at[0])
        total[...] -= other[...].astype(jnp.float32)

    run_if(adds[0] & (m == 0), lambda: arrived(vj, q_vj.at[0]))

    for before in range(DIAGS - 1):

        @pl.when(adds[0] & (m > before))
        def _():
            arrived(near_s.at[before], q_near.at[before])

    for before in range(DIAGS - 1):

        @pl.when(adds[0] & (m > before))
        def _():
            away = m - before
            arrived(new_r.at[before], q_new_r.at[before])
            arrived(new_c.at[before], q_new_c.at[before])
            total[...] += dot(new_r[before], chain[away]) - dot(near_s[away - 1], new_c[before])

    @pl.when(adds[0])
    def _():
        x = left_dot(pairs[t, 1], total[...])
        x = right_dot(x, vj[0]) * gap[...]
        x = left_dot(pairs[t, 0], x)
        x = right_dot(x, vj[1])
        fresh[...] = x.astype(jnp.bfloat16)
        solved[...] = x

    mine = jnp.minimum(m, DIAGS - 2)
    for d in range(1, DIAGS):
        fits = adds[0] & (m + d < DIAGS)
        send(fits & (j + d < TOTAL), fresh, new_r.at[mine], s_new.at[0, d - 1], q_new_r.at[mine], r, XS * y_at + lax.rem(x_at + d, XS))
        send(fits & (i >= d), fresh, new_c.at[mine], s_new.at[1, d - 1], q_new_c.at[mine], *seat(jnp.maximum(i - d, 0), 0))
    send_any(adds[0], solved, out.at[t], s_out.at[0], q_out.at[t], wrap(i), lax.rem(j, SIDE))

    for n in (0, 1):
        run_if(owned[n], lambda: arrived(out.at[n], q_out.at[n]))

    for cond, copy in later:
        run_if(cond, copy.wait_send)
    for n in (0, 1):
        ring_first(n, False)
        ring_second(n, False)
        for x in chain_slots(n):
            up, down, _ = chain_moves(n, x)
            run_if(up, chain_copy(x, 0).wait_send)
            run_if(down, chain_copy(x, 1).wait_send)
    run_if(v_moves, lambda: v_copy().wait_send())


def exchange(schur, known, pairs, lam):
    bs = schur.shape[-1]
    half, full = jnp.bfloat16, jnp.float32
    dma = pltpu.SemaphoreType.DMA
    vmem = pl.BlockSpec(memory_space=pltpu.VMEM)
    band = FIRST + DIAGS
    return pl.pallas_call(
        kernel,
        out_shape=jax.ShapeDtypeStruct((2, bs, bs), full),
        in_specs=[vmem] * 4,
        out_specs=vmem,
        scratch_shapes=[
            pltpu.VMEM((band, bs, bs), half),
            pltpu.VMEM((band, bs, bs), half),
            pltpu.VMEM((DIAGS - 1, bs, bs), half),
            pltpu.VMEM((2, bs, bs), half),
            pltpu.VMEM((DIAGS - 1, bs, bs), half),
            pltpu.VMEM((DIAGS - 1, bs, bs), half),
            pltpu.VMEM((bs, bs), half),
            pltpu.VMEM((bs, bs), full),
            pltpu.VMEM((bs, bs), full),
            pltpu.VMEM((bs, bs), half),
            pltpu.VMEM((bs, bs), full),
            dma((band,)), dma((band,)), dma((DIAGS - 1,)), dma((1,)),
            dma((DIAGS - 1,)), dma((DIAGS - 1,)), dma((1,)), dma((2,)),
            dma((2, 5)), dma((band, 2)), dma((band, 2)), dma((1,)), dma((2, 2, DIAGS)),
            dma((2, DIAGS - 1)), dma((2, DIAGS - 1)), dma((2,)),
        ],
        compiler_params=pltpu.CompilerParams(
            collective_id=0, has_side_effects=True, vmem_limit_bytes=40 * 1024 * 1024
        ),
    )(schur, known, pairs, lam)


def body(schur_blocks, known_blocks, eigen_pairs, eigenvalues):
    known = known_blocks[:, 0, :, 0]
    solved = exchange(
        schur_blocks[:, 0, :, 0],
        known.astype(jnp.bfloat16),
        eigen_pairs[:, 0].astype(jnp.bfloat16),
        eigenvalues,
    )
    rows = lax.axis_index("row") + SIDE * jnp.arange(2)[:, None]
    cols = lax.axis_index("col") + SIDE * jnp.arange(2)[None, :]
    away = cols - rows
    new = (away >= FIRST) & (away < FIRST + DIAGS)
    output = jnp.where(new[:, :, None, None], solved[:, None], known)
    return output[:, None, :, None]


def solution(mesh):
    return jax.shard_map(
        body,
        mesh=mesh,
        in_specs=(
            P(None, "row", None, "col", None, None),
            P(None, "row", None, "col", None, None),
            P(None, "row", None, None, None),
            P(),
        ),
        out_specs=P(None, "row", None, "col", None, None),
        check_vma=False,
    )
```

```python
import jax
import jax.numpy as jnp
from jax import lax
from jax.experimental import pallas as pl
from jax.experimental.pallas import tpu as pltpu
from jax.sharding import PartitionSpec as P

FIRST = 8
DIAGS = 4
SIDE = 16
XS = 4
TOTAL = 32
AWAY = 4
MESH = pl.DeviceIdType.MESH

SENDS = ("x", "cS0", "rS1", "rF0", "cF1", "rS0", "v", "own", "cF0", "cS1", "rF1")
WAITS = (("e", "v0", "v1", "v2", "l", "2", "1", "0", "3"), ("0", "e", "1", "2", "3", "l"))
ENTRY = ((3, 0, 0, 0, 0, 0, 0, 0), (0, 0, 0, 1, 0, 1, 2, 3))
TURN = ((1, 1), (1, 1))
CHAIN_ORDER = (4, 0, 5, 1, 6, 2, 7, 3)


def arrived(ref, sem):
    pltpu.make_async_copy(ref, ref, sem).wait()


def wrap(x):
    return lax.rem(x + 2 * SIDE, SIDE)


def line_of(i, second):
    return lax.rem((i + FIRST) // XS + (1 + 2 * second) * (i // SIDE), XS)


def pick(index, table):
    chosen = jnp.int32(table[0])
    for n, value in enumerate(table[1:], 1):
        chosen = jnp.where(index == n, value, chosen)
    return chosen


def dot(a, b):
    return jnp.dot(a, b, preferred_element_type=jnp.float32)


def halves(x):
    high = x.astype(jnp.bfloat16)
    return high, (x - high.astype(jnp.float32)).astype(jnp.bfloat16)


def left_dot(a, x):
    high, low = halves(x)
    return dot(a, high) + dot(a, low)


def right_dot(x, b):
    high, low = halves(x)
    return dot(high, b) + dot(low, b)


def kernel(
    schur, known_full, pairs_full, lam, out,
    known, pairs, known_in, pairs_in, ring, chain, near_s, vj, new_r, new_c, other, total, gap, fresh, solved,
    q_in, q_ring, q_chain, q_near, q_vj, q_new_r, q_new_c, q_other, q_out,
    s_src, s_ring, s_chain, s_v, s_own, s_near, s_new, s_out,
):
    r = lax.axis_index("row")
    c = lax.axis_index("col")
    x_at, y_at = lax.rem(c, XS), c // XS
    e = wrap(c - r)
    later = []

    def remote(src, dst, send_sem, recv_sem, row, col):
        return pltpu.make_async_remote_copy(
            src_ref=src, dst_ref=dst, send_sem=send_sem, recv_sem=recv_sem,
            device_id=(row, col), device_id_type=MESH,
        )

    def run_if(cond, fn):
        pl.when(cond)(fn)

    def send(cond, src, dst, send_sem, recv_sem, row, col):
        copy = remote(src, dst, send_sem, recv_sem, row, col)
        run_if(cond, copy.start)
        later.append((cond, copy))

    def send_any(cond, src, dst, send_sem, recv_sem, row, col):
        here = (row == r) & (col == c)
        run_if(cond & here, pltpu.make_async_copy(src, dst, recv_sem).start)
        send(cond & ~here, src, dst, send_sem, recv_sem, row, col)

    def seat(i, second, x=x_at):
        return wrap(i + AWAY * second), XS * line_of(i, second) + x

    fetch = [pltpu.make_async_copy(pairs_full, pairs_in, q_in.at[2])]
    for t in (0, 1):
        b = jnp.minimum((r + SIDE * t + e) // SIDE, 1)
        fetch.append(pltpu.make_async_copy(known_full.at[t, b], known_in.at[t], q_in.at[t]))
    for copy in fetch:
        copy.start()

    barrier = pltpu.get_barrier_semaphore()

    def meet(row, col):
        pl.semaphore_signal(barrier, inc=1, device_id=(row, col), device_id_type=MESH)

    def greet_line(step, carry):
        meet(lax.rem(r + step // XS, SIDE), XS * lax.rem(y_at + step, XS) + x_at)
        return carry

    def greet_row(step, carry):
        col = XS * lax.rem(step, XS) + lax.rem(x_at + 1 + step // XS, XS)
        meet(r, col)
        meet(wrap(r + AWAY), col)
        meet(wrap(r - AWAY), col)
        return carry

    lines = SIDE * XS - 1
    others = XS * (XS - 1)
    lax.fori_loop(1, lines + 1, greet_line, 0)
    lax.fori_loop(0, others, greet_row, 0)
    for copy in fetch:
        copy.wait()
    known[...] = known_in[...].astype(jnp.bfloat16)
    pairs[...] = pairs_in[...].astype(jnp.bfloat16)
    pl.semaphore_wait(barrier, lines + 3 * others)

    near = e < FIRST
    eb = jnp.minimum(e, FIRST - 1)
    places = []
    for t in (0, 1):
        k = r + SIDE * t
        j = k + e
        b = jnp.minimum(j // SIDE, 1)
        last = jnp.clip(j - FIRST, 0, DIAGS - 1)
        to_ring = near & (k < TOTAL - FIRST)
        to_chain = near & (j >= FIRST) & (j < TOTAL)
        entries = [
            seat(jnp.maximum(j - FIRST - jnp.minimum(pick(eb, ENTRY[n]), last), 0), n) for n in (0, 1)
        ]
        v_entry = seat(jnp.maximum(j - FIRST - last, 0), 0)
        places.append((k, j, b, to_ring, to_chain, entries, v_entry))

    mo = jnp.clip(e - FIRST, 0, DIAGS - 1)
    owner = (e >= FIRST) & (e < FIRST + DIAGS)
    owned = [owner & (places[t][1] < TOTAL) for t in (0, 1)]

    def send_near(group, kind, t):
        k, j, b, to_ring, to_chain, entries, _ = places[t]
        n = "FS".index(kind)
        src = (known.at[t], schur.at[t, b])[n]
        used = e >= n
        at = 2 * n + (group == "c")
        if group == "r":
            send_any(to_ring & used, src, ring.at[eb], s_src.at[t, at], q_ring.at[eb], *seat(k, n))
        else:
            send_any(to_chain & used, src, chain.at[eb], s_src.at[t, at], q_chain.at[eb], *entries[1 - n])

    def send_own(t):
        k, j, b = places[t][:3]
        slot = FIRST + mo
        for d in range(DIAGS):
            fits = owner & (j + d < TOTAL) & (mo + d < DIAGS)
            send(fits, schur.at[t, b], ring.at[slot], s_own.at[t, 0, d], q_ring.at[slot], *seat(k, 1, lax.rem(x_at + d, XS)))
            fits = owned[t] & (mo + d < DIAGS) & (k >= d)
            send_any(fits, schur.at[t, b], chain.at[slot], s_own.at[t, 1, d], q_chain.at[slot], *seat(jnp.maximum(k - d, 0), 0))

    def send_close(t):
        k, j, b = places[t][:3]
        slot = jnp.clip(e - 1, 0, DIAGS - 2)
        for d in range(DIAGS - 1):
            fits = (e >= 1) & (e + d < DIAGS) & (j + FIRST + d < TOTAL)
            send_any(fits, schur.at[t, b], near_s.at[slot], s_near.at[t, d], q_near.at[slot], *seat(k, 0, lax.rem(x_at + d, XS)))

    for token in SENDS:
        if token == "own":
            send_own(0)
            send_own(1)
        elif token == "x":
            send_close(0)
            send_close(1)
        elif token == "v":
            for t in (0, 1):
                send(places[t][4] & (e == 0), pairs.at[t], vj, s_src.at[t, 4], q_vj.at[0], *places[t][6])
        else:
            send_near(token[0], token[1], int(token[2]))

    i0 = wrap(r - AWAY)
    few = TOTAL - SIDE - FIRST
    first0, first1 = y_at == line_of(r, 0), (r < few) & (y_at == line_of(r + SIDE, 0))
    second0, second1 = y_at == line_of(i0, 1), (i0 < few) & (y_at == line_of(i0 + SIDE, 1))
    is_second = second0 | second1
    part = first0 | first1 | is_second
    kind = jnp.where(is_second, 1, 0)
    t = jnp.where(first1 | second1, 1, 0)
    i = jnp.where(is_second, i0, r) + SIDE * t
    m = lax.rem(x_at + 2 * SIDE - i, XS)
    j = i + FIRST + m
    real = part & (j < TOTAL)
    last = jnp.minimum(DIAGS - 1, i + m)
    takes = (part & ~is_second, is_second)
    adds = (real & ~is_second, real & is_second)
    col_next = (XS * y_at + lax.rem(x_at + 1, XS), XS * y_at + lax.rem(x_at + XS - 1, XS))

    @pl.when(adds[0])
    def _():
        rows = jnp.broadcast_to(lam[pl.ds(i, 1), :], total.shape).T
        gap[...] = 1.0 / (rows - lam[pl.ds(jnp.minimum(j, TOTAL - 1), 1), :])

    @pl.when(real)
    def _():
        total[...] = jnp.zeros(total.shape, jnp.float32)

    def member(step):
        return seat(jnp.maximum(i - step, 0), kind)

    def ring_copy(x, d):
        return remote(ring.at[x], ring.at[x], s_ring.at[x, d], q_ring.at[x], r, col_next[d])

    def chain_copy(x, d):
        return remote(chain.at[x], chain.at[x], s_chain.at[x, d], q_chain.at[x], *member(1 - 2 * d))

    def v_copy():
        return remote(vj, vj, s_v.at[0], q_vj.at[0], *member(-1))

    def ring_first(n, start):
        for x in (m, m + DIAGS):

            @pl.when(takes[n] & (x >= n))
            def _():
                if start:
                    arrived(ring.at[x], q_ring.at[x])
                for d in (0, 1):
                    ring_copy(x, d).start() if start else ring_copy(x, d).wait_send()

    def ring_second(n, start):
        for high in (0, 1):
            turn = TURN[n][high]
            x = lax.rem(m + DIAGS - turn, DIAGS) + DIAGS * high

            @pl.when(takes[n] & (x >= n))
            def _():
                copy = ring_copy(x, 0 if turn == 1 else 1)
                if start:
                    arrived(ring.at[x], q_ring.at[x])
                    copy.start()
                else:
                    copy.wait_send()

    def chain_moves(n, x):
        at = jnp.minimum(ENTRY[n][x], last)
        up = adds[n] & (m >= at) & (m < last)
        down = adds[n] & (m <= at) & (m > 0)
        return up, down, jnp.abs(m - at)

    def chain_slots(n):
        return [x for x in CHAIN_ORDER if x + n > 0]

    def chain_hop(n, depth):
        for x in chain_slots(n):
            up, down, hops = chain_moves(n, x)
            now = hops == depth
            run_if((up | down) & now, lambda: arrived(chain.at[x], q_chain.at[x]))
            run_if(up & now, chain_copy(x, 0).start)
            run_if(down & now, chain_copy(x, 1).start)

    v_moves = adds[0] & (m > 0)

    def v_hop(depth):
        @pl.when(v_moves & (last - m == depth))
        def _():
            arrived(vj, q_vj.at[0])
            v_copy().start()

    for n in (0, 1):
        for token in WAITS[n]:
            if token == "e":
                ring_first(n, True)
            elif token == "l":
                ring_second(n, True)
            elif token[0] == "v":
                v_hop(int(token[1]))
            else:
                chain_hop(n, int(token))

    def ring_rest(n, x):
        away = lax.rem(m - x + 2 * DIAGS, DIAGS)
        turn = TURN[n][x // DIAGS]
        mine = takes[n] & (away != 0) & (away != lax.rem(turn + DIAGS, DIAGS))
        run_if(mine, lambda: arrived(ring.at[x], q_ring.at[x]))

    def chain_rest(n, x):
        up, down, _ = chain_moves(n, x)
        run_if(adds[n] & ~(up | down), lambda: arrived(chain.at[x], q_chain.at[x]))

    def accumulate(x):
        other_x = FIRST + m - x
        total[...] += dot(ring[jnp.where(is_second, x, other_x)], chain[jnp.where(is_second, other_x, x)])

    for x in range(FIRST):
        ring_rest(0, x)
        chain_rest(1, x)

    def far(x, carry):
        @pl.when(real & (x <= FIRST + m))
        def _():
            run_if(~is_second, lambda: arrived(chain.at[x], q_chain.at[x]))
            run_if(is_second, lambda: arrived(ring.at[x], q_ring.at[x]))
            accumulate(x)

        return carry

    lax.fori_loop(FIRST, FIRST + DIAGS, far, 0)
    for x in range(1, FIRST):
        chain_rest(0, x)
        ring_rest(1, x)
        run_if(real & (x > m), lambda: accumulate(x))

    @pl.when(adds[1])
    def _():
        fresh[...] = total[...].astype(jnp.bfloat16)

    send(adds[1], fresh, other, s_out.at[1], q_other.at[0], *seat(i, 0))

    @pl.when(adds[0])
    def _():
        arrived(other, q_other.at[0])
        total[...] -= other[...].astype(jnp.float32)

    run_if(adds[0] & (m == 0), lambda: arrived(vj, q_vj.at[0]))

    for before in range(DIAGS - 1):

        @pl.when(adds[0] & (m > before))
        def _():
            arrived(near_s.at[before], q_near.at[before])

    for before in range(DIAGS - 1):

        @pl.when(adds[0] & (m > before))
        def _():
            away = m - before
            arrived(new_r.at[before], q_new_r.at[before])
            arrived(new_c.at[before], q_new_c.at[before])
            total[...] += dot(new_r[before], chain[away]) - dot(near_s[away - 1], new_c[before])

    @pl.when(adds[0])
    def _():
        x = left_dot(pairs[t, 1], total[...])
        x = right_dot(x, vj[0]) * gap[...]
        x = left_dot(pairs[t, 0], x)
        x = right_dot(x, vj[1])
        fresh[...] = x.astype(jnp.bfloat16)
        solved[...] = x

    mine = jnp.minimum(m, DIAGS - 2)
    for d in range(1, DIAGS):
        fits = adds[0] & (m + d < DIAGS)
        send(fits & (j + d < TOTAL), fresh, new_r.at[mine], s_new.at[0, d - 1], q_new_r.at[mine], r, XS * y_at + lax.rem(x_at + d, XS))
        send(fits & (i >= d), fresh, new_c.at[mine], s_new.at[1, d - 1], q_new_c.at[mine], *seat(jnp.maximum(i - d, 0), 0))
    send_any(adds[0], solved, out.at[t], s_out.at[0], q_out.at[t], wrap(i), lax.rem(j, SIDE))

    for n in (0, 1):
        run_if(owned[n], lambda: arrived(out.at[n], q_out.at[n]))

    for cond, copy in later:
        run_if(cond, copy.wait_send)
    for n in (0, 1):
        ring_first(n, False)
        ring_second(n, False)
        for x in chain_slots(n):
            up, down, _ = chain_moves(n, x)
            run_if(up, chain_copy(x, 0).wait_send)
            run_if(down, chain_copy(x, 1).wait_send)
    run_if(v_moves, lambda: v_copy().wait_send())


def exchange(schur, known, pairs, lam):
    bs = schur.shape[-1]
    half, full = jnp.bfloat16, jnp.float32
    dma = pltpu.SemaphoreType.DMA
    vmem = pl.BlockSpec(memory_space=pltpu.VMEM)
    band = FIRST + DIAGS
    return pl.pallas_call(
        kernel,
        out_shape=jax.ShapeDtypeStruct((2, bs, bs), full),
        in_specs=[pl.BlockSpec(memory_space=pl.ANY)] * 3 + [vmem],
        out_specs=vmem,
        scratch_shapes=[
            pltpu.VMEM((2, bs, bs), half),
            pltpu.VMEM((2, 2, bs, bs), half),
            pltpu.VMEM((2, bs, bs), full),
            pltpu.VMEM((2, 2, bs, bs), full),
            pltpu.VMEM((band, bs, bs), half),
            pltpu.VMEM((band, bs, bs), half),
            pltpu.VMEM((DIAGS - 1, bs, bs), half),
            pltpu.VMEM((2, bs, bs), half),
            pltpu.VMEM((DIAGS - 1, bs, bs), half),
            pltpu.VMEM((DIAGS - 1, bs, bs), half),
            pltpu.VMEM((bs, bs), half),
            pltpu.VMEM((bs, bs), full),
            pltpu.VMEM((bs, bs), full),
            pltpu.VMEM((bs, bs), half),
            pltpu.VMEM((bs, bs), full),
            dma((3,)), dma((band,)), dma((band,)), dma((DIAGS - 1,)), dma((1,)),
            dma((DIAGS - 1,)), dma((DIAGS - 1,)), dma((1,)), dma((2,)),
            dma((2, 5)), dma((band, 2)), dma((band, 2)), dma((1,)), dma((2, 2, DIAGS)),
            dma((2, DIAGS - 1)), dma((2, DIAGS - 1)), dma((2,)),
        ],
        compiler_params=pltpu.CompilerParams(
            collective_id=0, has_side_effects=True, vmem_limit_bytes=60 * 1024 * 1024
        ),
    )(schur, known, pairs, lam)


def body(schur_blocks, known_blocks, eigen_pairs, eigenvalues):
    known = known_blocks[:, 0, :, 0]
    solved = exchange(
        schur_blocks[:, 0, :, 0],
        known,
        eigen_pairs[:, 0],
        eigenvalues,
    )
    rows = lax.axis_index("row") + SIDE * jnp.arange(2)[:, None]
    cols = lax.axis_index("col") + SIDE * jnp.arange(2)[None, :]
    away = cols - rows
    new = (away >= FIRST) & (away < FIRST + DIAGS)
    output = jnp.where(new[:, :, None, None], solved[:, None], known)
    return output[:, None, :, None]


def solution(mesh):
    return jax.shard_map(
        body,
        mesh=mesh,
        in_specs=(
            P(None, "row", None, "col", None, None),
            P(None, "row", None, "col", None, None),
            P(None, "row", None, None, None),
            P(),
        ),
        out_specs=P(None, "row", None, "col", None, None),
        check_vma=False,
    )
```

```python
import jax
import jax.numpy as jnp
from jax import lax
from jax.experimental import pallas as pl
from jax.experimental.pallas import tpu as pltpu
from jax.sharding import PartitionSpec as P

FIRST = 8
DIAGS = 4
SIDE = 16
XS = 4
TOTAL = 32
AWAY = 4
MESH = pl.DeviceIdType.MESH

SENDS = ("cF0", "rF1", "rS0", "cF1", "rS1", "rF0", "cS0", "cS1", "v", "x", "own")
WAITS = (("e", "3", "v0", "0", "1", "v2", "v1", "2", "l", "o"), ("e", "3", "0", "1", "2", "o", "l"))
ENTRY = ((2, 1, 0, 2, 0, 2, 0, 0), (0, 0, 1, 0, 0, 1, 2, 2))
TURN = ((1, 1), (1, -1))
CHAIN_ORDER = (4, 7, 0, 3, 6, 2, 5, 1)


def arrived(ref, sem):
    pltpu.make_async_copy(ref, ref, sem).wait()


def wrap(x):
    return lax.rem(x + 2 * SIDE, SIDE)


def line_of(i, second):
    return lax.rem((i + FIRST) // XS + (1 + 2 * second) * (i // SIDE), XS)


def pick(index, table):
    chosen = jnp.int32(table[0])
    for n, value in enumerate(table[1:], 1):
        chosen = jnp.where(index == n, value, chosen)
    return chosen


def dot(a, b):
    return jnp.dot(a, b, preferred_element_type=jnp.float32)


def halves(x):
    high = x.astype(jnp.bfloat16)
    return high, (x - high.astype(jnp.float32)).astype(jnp.bfloat16)


def left_dot(a, x):
    high, low = halves(x)
    return dot(a, high) + dot(a, low)


def right_dot(x, b):
    high, low = halves(x)
    return dot(high, b) + dot(low, b)


def kernel(
    schur, known_full, pairs_full, lam, out,
    known, pairs, known_in, pairs_in, ring, chain, near_s, vj, new_r, new_c, other, total, gap, fresh, solved,
    q_in, q_ring, q_chain, q_near, q_vj, q_new_r, q_new_c, q_other, q_out,
    s_src, s_ring, s_chain, s_v, s_own, s_near, s_new, s_out,
):
    r = lax.axis_index("row")
    c = lax.axis_index("col")
    x_at, y_at = lax.rem(c, XS), c // XS
    e = wrap(c - r)
    later = []

    def remote(src, dst, send_sem, recv_sem, row, col):
        return pltpu.make_async_remote_copy(
            src_ref=src, dst_ref=dst, send_sem=send_sem, recv_sem=recv_sem,
            device_id=(row, col), device_id_type=MESH,
        )

    def run_if(cond, fn):
        pl.when(cond)(fn)

    def send(cond, src, dst, send_sem, recv_sem, row, col):
        copy = remote(src, dst, send_sem, recv_sem, row, col)
        run_if(cond, copy.start)
        later.append((cond, copy))

    def send_any(cond, src, dst, send_sem, recv_sem, row, col):
        here = (row == r) & (col == c)
        run_if(cond & here, pltpu.make_async_copy(src, dst, recv_sem).start)
        send(cond & ~here, src, dst, send_sem, recv_sem, row, col)

    def seat(i, second, x=x_at):
        return wrap(i + AWAY * second), XS * line_of(i, second) + x

    fetch = [pltpu.make_async_copy(pairs_full, pairs_in, q_in.at[2])]
    for t in (0, 1):
        b = jnp.minimum((r + SIDE * t + e) // SIDE, 1)
        fetch.append(pltpu.make_async_copy(known_full.at[t, b], known_in.at[t], q_in.at[t]))
    for copy in fetch:
        copy.start()

    barrier = pltpu.get_barrier_semaphore()

    def meet(row, col):
        pl.semaphore_signal(barrier, inc=1, device_id=(row, col), device_id_type=MESH)

    def greet_line(step, carry):
        meet(lax.rem(r + step // XS, SIDE), XS * lax.rem(y_at + step, XS) + x_at)
        return carry

    def greet_row(step, carry):
        col = XS * lax.rem(step, XS) + lax.rem(x_at + 1 + step // XS, XS)
        meet(r, col)
        return carry

    lines = SIDE * XS - 1
    others = XS * (XS - 1)
    lax.fori_loop(1, lines + 1, greet_line, 0)
    lax.fori_loop(0, others, greet_row, 0)
    for copy in fetch:
        copy.wait()
    known[...] = known_in[...].astype(jnp.bfloat16)
    pairs[...] = pairs_in[...].astype(jnp.bfloat16)
    pl.semaphore_wait(barrier, lines + others)

    near = e < FIRST
    eb = jnp.minimum(e, FIRST - 1)
    places = []
    for t in (0, 1):
        k = r + SIDE * t
        j = k + e
        b = jnp.minimum(j // SIDE, 1)
        last = jnp.clip(j - FIRST, 0, DIAGS - 1)
        to_ring = near & (k < TOTAL - FIRST)
        to_chain = near & (j >= FIRST) & (j < TOTAL)
        entries = [
            seat(jnp.maximum(j - FIRST - jnp.minimum(pick(eb, ENTRY[n]), last), 0), n) for n in (0, 1)
        ]
        v_entry = seat(jnp.maximum(j - FIRST - last, 0), 0)
        places.append((k, j, b, to_ring, to_chain, entries, v_entry))

    mo = jnp.clip(e - FIRST, 0, DIAGS - 1)
    owner = (e >= FIRST) & (e < FIRST + DIAGS)
    owned = [owner & (places[t][1] < TOTAL) for t in (0, 1)]

    def send_near(group, kind, t):
        k, j, b, to_ring, to_chain, entries, _ = places[t]
        n = "FS".index(kind)
        src = (known.at[t], schur.at[t, b])[n]
        used = e >= n
        at = 2 * n + (group == "c")
        if group == "r":
            send_any(to_ring & used, src, ring.at[eb], s_src.at[t, at], q_ring.at[eb], *seat(k, n))
        else:
            send_any(to_chain & used, src, chain.at[eb], s_src.at[t, at], q_chain.at[eb], *entries[1 - n])

    def send_own(t):
        k, j, b = places[t][:3]
        slot = FIRST + mo
        send(owned[t], schur.at[t, b], ring.at[slot], s_own.at[t, 0, 0], q_ring.at[slot], *seat(k, 1))
        send_any(owned[t], schur.at[t, b], chain.at[slot], s_own.at[t, 1, 0], q_chain.at[slot], *seat(k, 0))

    def send_close(t):
        k, j, b = places[t][:3]
        slot = jnp.clip(e - 1, 0, DIAGS - 2)
        for d in range(DIAGS - 1):
            fits = (e >= 1) & (e + d < DIAGS) & (j + FIRST + d < TOTAL)
            send_any(fits, schur.at[t, b], near_s.at[slot], s_near.at[t, d], q_near.at[slot], *seat(k, 0, lax.rem(x_at + d, XS)))

    for token in SENDS:
        if token == "own":
            send_own(0)
            send_own(1)
        elif token == "x":
            send_close(0)
            send_close(1)
        elif token == "v":
            for t in (0, 1):
                send(places[t][4] & (e == 0), pairs.at[t], vj, s_src.at[t, 4], q_vj.at[0], *places[t][6])
        else:
            send_near(token[0], token[1], int(token[2]))

    i0 = wrap(r - AWAY)
    few = TOTAL - SIDE - FIRST
    first0, first1 = y_at == line_of(r, 0), (r < few) & (y_at == line_of(r + SIDE, 0))
    second0, second1 = y_at == line_of(i0, 1), (i0 < few) & (y_at == line_of(i0 + SIDE, 1))
    is_second = second0 | second1
    part = first0 | first1 | is_second
    kind = jnp.where(is_second, 1, 0)
    t = jnp.where(first1 | second1, 1, 0)
    i = jnp.where(is_second, i0, r) + SIDE * t
    m = lax.rem(x_at + 2 * SIDE - i, XS)
    j = i + FIRST + m
    real = part & (j < TOTAL)
    last = jnp.minimum(DIAGS - 1, i + m)
    takes = (part & ~is_second, is_second)
    adds = (real & ~is_second, real & is_second)
    col_next = (XS * y_at + lax.rem(x_at + 1, XS), XS * y_at + lax.rem(x_at + XS - 1, XS))

    @pl.when(adds[0])
    def _():
        rows = jnp.broadcast_to(lam[pl.ds(i, 1), :], total.shape).T
        gap[...] = 1.0 / (rows - lam[pl.ds(jnp.minimum(j, TOTAL - 1), 1), :])

    @pl.when(real)
    def _():
        total[...] = jnp.zeros(total.shape, jnp.float32)

    def member(step):
        return seat(jnp.maximum(i - step, 0), kind)

    def ring_copy(x, d):
        return remote(ring.at[x], ring.at[x], s_ring.at[x, d], q_ring.at[x], r, col_next[d])

    def chain_copy(x, d):
        return remote(chain.at[x], chain.at[x], s_chain.at[x, d], q_chain.at[x], *member(1 - 2 * d))

    def v_copy():
        return remote(vj, vj, s_v.at[0], q_vj.at[0], *member(-1))

    def ring_first(n, start):
        for x in (m, m + DIAGS):

            @pl.when(takes[n] & (x >= n))
            def _():
                if start:
                    arrived(ring.at[x], q_ring.at[x])
                for d in (0, 1):
                    ring_copy(x, d).start() if start else ring_copy(x, d).wait_send()

    def ring_second(n, start):
        for high in (0, 1):
            turn = TURN[n][high]
            x = lax.rem(m + DIAGS - turn, DIAGS) + DIAGS * high

            @pl.when(takes[n] & (x >= n))
            def _():
                copy = ring_copy(x, 0 if turn == 1 else 1)
                if start:
                    arrived(ring.at[x], q_ring.at[x])
                    copy.start()
                else:
                    copy.wait_send()

    def chain_moves(n, x):
        at = jnp.minimum(ENTRY[n][x], last)
        up = adds[n] & (m >= at) & (m < last)
        down = adds[n] & (m <= at) & (m > 0)
        return up, down, jnp.abs(m - at)

    def chain_slots(n):
        return [x for x in CHAIN_ORDER if x + n > 0]

    def chain_hop(n, depth):
        for x in chain_slots(n):
            up, down, hops = chain_moves(n, x)
            now = hops == depth
            run_if((up | down) & now, lambda: arrived(chain.at[x], q_chain.at[x]))
            run_if(up & now, chain_copy(x, 0).start)
            run_if(down & now, chain_copy(x, 1).start)

    v_moves = adds[0] & (m > 0)

    def v_hop(depth):
        @pl.when(v_moves & (last - m == depth))
        def _():
            arrived(vj, q_vj.at[0])
            v_copy().start()

    def own_hop(n):
        slot = FIRST + jnp.clip(m, 0, DIAGS - 1)
        ref, sems = ((chain, q_chain), (ring, q_ring))[n]
        run_if(adds[n], lambda: arrived(ref.at[slot], sems.at[slot]))
        for d in range(1, DIAGS):
            if n:
                fits, to = j + d < TOTAL, (r, XS * y_at + lax.rem(x_at + d, XS))
            else:
                fits, to = i >= d, seat(jnp.maximum(i - d, 0), 0)
            send(adds[n] & (m + d < DIAGS) & fits, ref.at[slot], ref.at[slot], s_own.at[2, n, d], sems.at[slot], *to)

    for n in (0, 1):
        for token in WAITS[n]:
            if token == "e":
                ring_first(n, True)
            elif token == "l":
                ring_second(n, True)
            elif token == "o":
                own_hop(n)
            elif token[0] == "v":
                v_hop(int(token[1]))
            else:
                chain_hop(n, int(token))

    def ring_rest(n, x):
        away = lax.rem(m - x + 2 * DIAGS, DIAGS)
        turn = TURN[n][x // DIAGS]
        mine = takes[n] & (away != 0) & (away != lax.rem(turn + DIAGS, DIAGS))
        run_if(mine, lambda: arrived(ring.at[x], q_ring.at[x]))

    def chain_rest(n, x):
        up, down, _ = chain_moves(n, x)
        run_if(adds[n] & ~(up | down), lambda: arrived(chain.at[x], q_chain.at[x]))

    def accumulate(x):
        other_x = FIRST + m - x
        total[...] += dot(ring[jnp.where(is_second, x, other_x)], chain[jnp.where(is_second, other_x, x)])

    for x in range(FIRST):
        ring_rest(0, x)
        chain_rest(1, x)

    def far(x, carry):
        @pl.when(real & (x <= FIRST + m))
        def _():
            sent_on = x == FIRST + m
            run_if(~is_second & ~sent_on, lambda: arrived(chain.at[x], q_chain.at[x]))
            run_if(is_second & ~sent_on, lambda: arrived(ring.at[x], q_ring.at[x]))
            accumulate(x)

        return carry

    lax.fori_loop(FIRST, FIRST + DIAGS, far, 0)
    for x in range(1, FIRST):
        chain_rest(0, x)
        ring_rest(1, x)
        run_if(real & (x > m), lambda: accumulate(x))

    @pl.when(adds[1])
    def _():
        fresh[...] = total[...].astype(jnp.bfloat16)

    send(adds[1], fresh, other, s_out.at[1], q_other.at[0], *seat(i, 0))

    @pl.when(adds[0])
    def _():
        arrived(other, q_other.at[0])
        total[...] -= other[...].astype(jnp.float32)

    run_if(adds[0] & (m == 0), lambda: arrived(vj, q_vj.at[0]))

    for before in range(DIAGS - 1):

        @pl.when(adds[0] & (m > before))
        def _():
            arrived(near_s.at[before], q_near.at[before])

    for before in range(DIAGS - 1):

        @pl.when(adds[0] & (m > before))
        def _():
            away = m - before
            arrived(new_r.at[before], q_new_r.at[before])
            arrived(new_c.at[before], q_new_c.at[before])
            total[...] += dot(new_r[before], chain[away]) - dot(near_s[away - 1], new_c[before])

    @pl.when(adds[0])
    def _():
        x = left_dot(pairs[t, 1], total[...])
        x = right_dot(x, vj[0]) * gap[...]
        x = left_dot(pairs[t, 0], x)
        x = right_dot(x, vj[1])
        fresh[...] = x.astype(jnp.bfloat16)
        solved[...] = x

    mine = jnp.minimum(m, DIAGS - 2)
    for d in range(1, DIAGS):
        fits = adds[0] & (m + d < DIAGS)
        send(fits & (j + d < TOTAL), fresh, new_r.at[mine], s_new.at[0, d - 1], q_new_r.at[mine], r, XS * y_at + lax.rem(x_at + d, XS))
        send(fits & (i >= d), fresh, new_c.at[mine], s_new.at[1, d - 1], q_new_c.at[mine], *seat(jnp.maximum(i - d, 0), 0))
    send_any(adds[0], solved, out.at[t], s_out.at[0], q_out.at[t], wrap(i), lax.rem(j, SIDE))

    for n in (0, 1):
        run_if(owned[n], lambda: arrived(out.at[n], q_out.at[n]))

    for cond, copy in later:
        run_if(cond, copy.wait_send)
    for n in (0, 1):
        ring_first(n, False)
        ring_second(n, False)
        for x in chain_slots(n):
            up, down, _ = chain_moves(n, x)
            run_if(up, chain_copy(x, 0).wait_send)
            run_if(down, chain_copy(x, 1).wait_send)
    run_if(v_moves, lambda: v_copy().wait_send())


def exchange(schur, known, pairs, lam):
    bs = schur.shape[-1]
    half, full = jnp.bfloat16, jnp.float32
    dma = pltpu.SemaphoreType.DMA
    vmem = pl.BlockSpec(memory_space=pltpu.VMEM)
    band = FIRST + DIAGS
    return pl.pallas_call(
        kernel,
        out_shape=jax.ShapeDtypeStruct((2, bs, bs), full),
        in_specs=[pl.BlockSpec(memory_space=pl.ANY)] * 3 + [vmem],
        out_specs=vmem,
        scratch_shapes=[
            pltpu.VMEM((2, bs, bs), half),
            pltpu.VMEM((2, 2, bs, bs), half),
            pltpu.VMEM((2, bs, bs), full),
            pltpu.VMEM((2, 2, bs, bs), full),
            pltpu.VMEM((band, bs, bs), half),
            pltpu.VMEM((band, bs, bs), half),
            pltpu.VMEM((DIAGS - 1, bs, bs), half),
            pltpu.VMEM((2, bs, bs), half),
            pltpu.VMEM((DIAGS - 1, bs, bs), half),
            pltpu.VMEM((DIAGS - 1, bs, bs), half),
            pltpu.VMEM((bs, bs), half),
            pltpu.VMEM((bs, bs), full),
            pltpu.VMEM((bs, bs), full),
            pltpu.VMEM((bs, bs), half),
            pltpu.VMEM((bs, bs), full),
            dma((3,)), dma((band,)), dma((band,)), dma((DIAGS - 1,)), dma((1,)),
            dma((DIAGS - 1,)), dma((DIAGS - 1,)), dma((1,)), dma((2,)),
            dma((2, 5)), dma((band, 2)), dma((band, 2)), dma((1,)), dma((3, 2, DIAGS)),
            dma((2, DIAGS - 1)), dma((2, DIAGS - 1)), dma((2,)),
        ],
        compiler_params=pltpu.CompilerParams(
            collective_id=0, has_side_effects=True, vmem_limit_bytes=60 * 1024 * 1024
        ),
    )(schur, known, pairs, lam)


def body(schur_blocks, known_blocks, eigen_pairs, eigenvalues):
    known = known_blocks[:, 0, :, 0]
    solved = exchange(
        schur_blocks[:, 0, :, 0],
        known,
        eigen_pairs[:, 0],
        eigenvalues,
    )
    rows = lax.axis_index("row") + SIDE * jnp.arange(2)[:, None]
    cols = lax.axis_index("col") + SIDE * jnp.arange(2)[None, :]
    away = cols - rows
    new = (away >= FIRST) & (away < FIRST + DIAGS)
    output = jnp.where(new[:, :, None, None], solved[:, None], known)
    return output[:, None, :, None]


def solution(mesh):
    return jax.shard_map(
        body,
        mesh=mesh,
        in_specs=(
            P(None, "row", None, "col", None, None),
            P(None, "row", None, "col", None, None),
            P(None, "row", None, None, None),
            P(),
        ),
        out_specs=P(None, "row", None, "col", None, None),
        check_vma=False,
    )
```

```python
import jax
import jax.numpy as jnp
from jax import lax
from jax.experimental import pallas as pl
from jax.experimental.pallas import tpu as pltpu
from jax.sharding import PartitionSpec as P

FIRST = 8
DIAGS = 4
SIDE = 16
XS = 4
TOTAL = 32
AWAY = 4
LATE = 24
MESH = pl.DeviceIdType.MESH

SENDS = ("cF0", "rF1", "v", "rS0", "rS1", "rF0", "cS0", "x", "cF1", "own", "cS1")
WAITS = (("e", "3", "v0", "0", "1", "v1", "2", "l", "o", "v2"), ("3", "e", "0", "1", "2", "o", "l"))
ENTRY = (((2, 1, 0, 2, 0, 1, 2, 1), (0, 1, 0, 2, 2, 2, 1, 1)), ((0, 0, 0, 2, 0, 1, 2, 2), (0, 1, 0, 0, 0, 1, 2, 2)))
TURN = ((1, 1), (1, -1))
CHAIN_ORDER = (6, 5, 0, 7, 3, 2, 1, 4)


def arrived(ref, sem):
    pltpu.make_async_copy(ref, ref, sem).wait()


def wrap(x):
    return lax.rem(x + 2 * SIDE, SIDE)


def line_of(i, second):
    return lax.rem((i + FIRST) // XS + (1 + 2 * second) * (i // SIDE), XS)


def pick(index, table):
    if isinstance(index, int):
        return table[index]
    chosen = jnp.int32(table[0])
    for n, value in enumerate(table[1:], 1):
        chosen = jnp.where(index == n, value, chosen)
    return chosen


def entry_of(n, j, index):
    early, late = ENTRY[n]
    return jnp.where(j < LATE, pick(index, early), pick(index, late))


def dot(a, b):
    return jnp.dot(a, b, preferred_element_type=jnp.float32)


def halves(x):
    high = x.astype(jnp.bfloat16)
    return high, (x - high.astype(jnp.float32)).astype(jnp.bfloat16)


def left_dot(a, x):
    high, low = halves(x)
    return dot(a, high) + dot(a, low)


def right_dot(x, b):
    high, low = halves(x)
    return dot(high, b) + dot(low, b)


def kernel(
    schur, known_full, pairs_full, lam, out,
    known, pairs, known_in, pairs_in, ring, chain, near_s, vj, new_r, new_c, other, total, gap, fresh, solved,
    q_in, q_ring, q_chain, q_near, q_vj, q_new_r, q_new_c, q_other, q_out,
    s_src, s_ring, s_chain, s_v, s_own, s_near, s_new, s_out,
):
    r = lax.axis_index("row")
    c = lax.axis_index("col")
    x_at, y_at = lax.rem(c, XS), c // XS
    e = wrap(c - r)
    later = []

    def remote(src, dst, send_sem, recv_sem, row, col):
        return pltpu.make_async_remote_copy(
            src_ref=src, dst_ref=dst, send_sem=send_sem, recv_sem=recv_sem,
            device_id=(row, col), device_id_type=MESH,
        )

    def run_if(cond, fn):
        pl.when(cond)(fn)

    def send(cond, src, dst, send_sem, recv_sem, row, col):
        copy = remote(src, dst, send_sem, recv_sem, row, col)
        run_if(cond, copy.start)
        later.append((cond, copy))

    def send_any(cond, src, dst, send_sem, recv_sem, row, col):
        here = (row == r) & (col == c)
        run_if(cond & here, pltpu.make_async_copy(src, dst, recv_sem).start)
        send(cond & ~here, src, dst, send_sem, recv_sem, row, col)

    def seat(i, second, x=x_at):
        return wrap(i + AWAY * second), XS * line_of(i, second) + x

    fetch = [pltpu.make_async_copy(pairs_full, pairs_in, q_in.at[2])]
    for t in (0, 1):
        b = jnp.minimum((r + SIDE * t + e) // SIDE, 1)
        fetch.append(pltpu.make_async_copy(known_full.at[t, b], known_in.at[t], q_in.at[t]))
    for copy in fetch:
        copy.start()

    barrier = pltpu.get_barrier_semaphore()

    def meet(row, col):
        pl.semaphore_signal(barrier, inc=1, device_id=(row, col), device_id_type=MESH)

    def greet_line(step, carry):
        meet(lax.rem(r + step // XS, SIDE), XS * lax.rem(y_at + step, XS) + x_at)
        return carry

    def greet_row(step, carry):
        col = XS * lax.rem(step, XS) + lax.rem(x_at + 1 + step // XS, XS)
        meet(r, col)
        return carry

    lines = SIDE * XS - 1
    others = XS * (XS - 1)
    lax.fori_loop(1, lines + 1, greet_line, 0)
    lax.fori_loop(0, others, greet_row, 0)
    for copy in fetch:
        copy.wait()
    known[...] = known_in[...].astype(jnp.bfloat16)
    pairs[...] = pairs_in[...].astype(jnp.bfloat16)
    pl.semaphore_wait(barrier, lines + others)

    near = e < FIRST
    eb = jnp.minimum(e, FIRST - 1)
    places = []
    for t in (0, 1):
        k = r + SIDE * t
        j = k + e
        b = jnp.minimum(j // SIDE, 1)
        last = jnp.clip(j - FIRST, 0, DIAGS - 1)
        to_ring = near & (k < TOTAL - FIRST)
        to_chain = near & (j >= FIRST) & (j < TOTAL)
        entries = [
            seat(jnp.maximum(j - FIRST - jnp.minimum(entry_of(n, j, eb), last), 0), n) for n in (0, 1)
        ]
        v_entry = seat(jnp.maximum(j - FIRST - last, 0), 0)
        places.append((k, j, b, to_ring, to_chain, entries, v_entry))

    mo = jnp.clip(e - FIRST, 0, DIAGS - 1)
    owner = (e >= FIRST) & (e < FIRST + DIAGS)
    owned = [owner & (places[t][1] < TOTAL) for t in (0, 1)]

    def send_near(group, kind, t):
        k, j, b, to_ring, to_chain, entries, _ = places[t]
        n = "FS".index(kind)
        src = (known.at[t], schur.at[t, b])[n]
        used = e >= n
        at = 2 * n + (group == "c")
        if group == "r":
            send_any(to_ring & used, src, ring.at[eb], s_src.at[t, at], q_ring.at[eb], *seat(k, n))
        else:
            send_any(to_chain & used, src, chain.at[eb], s_src.at[t, at], q_chain.at[eb], *entries[1 - n])

    def send_own(t):
        k, j, b = places[t][:3]
        slot = FIRST + mo
        send(owned[t], schur.at[t, b], ring.at[slot], s_own.at[t, 0, 0], q_ring.at[slot], *seat(k, 1))
        send_any(owned[t], schur.at[t, b], chain.at[slot], s_own.at[t, 1, 0], q_chain.at[slot], *seat(k, 0))

    def send_close(t):
        k, j, b = places[t][:3]
        slot = jnp.clip(e - 1, 0, DIAGS - 2)
        for d in range(DIAGS - 1):
            fits = (e >= 1) & (e + d < DIAGS) & (j + FIRST + d < TOTAL)
            send_any(fits, schur.at[t, b], near_s.at[slot], s_near.at[t, d], q_near.at[slot], *seat(k, 0, lax.rem(x_at + d, XS)))

    for token in SENDS:
        if token == "own":
            send_own(0)
            send_own(1)
        elif token == "x":
            send_close(0)
            send_close(1)
        elif token == "v":
            for t in (0, 1):
                send(places[t][4] & (e == 0), pairs.at[t], vj, s_src.at[t, 4], q_vj.at[0], *places[t][6])
        else:
            send_near(token[0], token[1], int(token[2]))

    i0 = wrap(r - AWAY)
    few = TOTAL - SIDE - FIRST
    first0, first1 = y_at == line_of(r, 0), (r < few) & (y_at == line_of(r + SIDE, 0))
    second0, second1 = y_at == line_of(i0, 1), (i0 < few) & (y_at == line_of(i0 + SIDE, 1))
    is_second = second0 | second1
    part = first0 | first1 | is_second
    kind = jnp.where(is_second, 1, 0)
    t = jnp.where(first1 | second1, 1, 0)
    i = jnp.where(is_second, i0, r) + SIDE * t
    m = lax.rem(x_at + 2 * SIDE - i, XS)
    j = i + FIRST + m
    real = part & (j < TOTAL)
    last = jnp.minimum(DIAGS - 1, i + m)
    takes = (part & ~is_second, is_second)
    adds = (real & ~is_second, real & is_second)
    col_next = (XS * y_at + lax.rem(x_at + 1, XS), XS * y_at + lax.rem(x_at + XS - 1, XS))

    @pl.when(adds[0])
    def _():
        rows = jnp.broadcast_to(lam[pl.ds(i, 1), :], total.shape).T
        gap[...] = 1.0 / (rows - lam[pl.ds(jnp.minimum(j, TOTAL - 1), 1), :])

    @pl.when(real)
    def _():
        total[...] = jnp.zeros(total.shape, jnp.float32)

    def member(step):
        return seat(jnp.maximum(i - step, 0), kind)

    def ring_copy(x, d):
        return remote(ring.at[x], ring.at[x], s_ring.at[x, d], q_ring.at[x], r, col_next[d])

    def chain_copy(x, d):
        return remote(chain.at[x], chain.at[x], s_chain.at[x, d], q_chain.at[x], *member(1 - 2 * d))

    def v_copy():
        return remote(vj, vj, s_v.at[0], q_vj.at[0], *member(-1))

    def ring_first(n, start):
        for x in (m, m + DIAGS):

            @pl.when(takes[n] & (x >= n))
            def _():
                if start:
                    arrived(ring.at[x], q_ring.at[x])
                for d in (0, 1):
                    ring_copy(x, d).start() if start else ring_copy(x, d).wait_send()

    def ring_second(n, start):
        for high in (0, 1):
            turn = TURN[n][high]
            x = lax.rem(m + DIAGS - turn, DIAGS) + DIAGS * high

            @pl.when(takes[n] & (x >= n))
            def _():
                copy = ring_copy(x, 0 if turn == 1 else 1)
                if start:
                    arrived(ring.at[x], q_ring.at[x])
                    copy.start()
                else:
                    copy.wait_send()

    def chain_moves(n, x):
        at = jnp.minimum(entry_of(n, j, x), last)
        up = adds[n] & (m >= at) & (m < last)
        down = adds[n] & (m <= at) & (m > 0)
        return up, down, jnp.abs(m - at)

    def chain_slots(n):
        return [x for x in CHAIN_ORDER if x + n > 0]

    def chain_hop(n, depth):
        for x in chain_slots(n):
            up, down, hops = chain_moves(n, x)
            now = hops == depth
            run_if((up | down) & now, lambda: arrived(chain.at[x], q_chain.at[x]))
            run_if(up & now, chain_copy(x, 0).start)
            run_if(down & now, chain_copy(x, 1).start)

    v_moves = adds[0] & (m > 0)

    def v_hop(depth):
        @pl.when(v_moves & (last - m == depth))
        def _():
            arrived(vj, q_vj.at[0])
            v_copy().start()

    def own_hop(n):
        slot = FIRST + jnp.clip(m, 0, DIAGS - 1)
        ref, sems = ((chain, q_chain), (ring, q_ring))[n]
        run_if(adds[n], lambda: arrived(ref.at[slot], sems.at[slot]))
        for d in range(1, DIAGS):
            if n:
                fits, to = j + d < TOTAL, (r, XS * y_at + lax.rem(x_at + d, XS))
            else:
                fits, to = i >= d, seat(jnp.maximum(i - d, 0), 0)
            send(adds[n] & (m + d < DIAGS) & fits, ref.at[slot], ref.at[slot], s_own.at[2, n, d], sems.at[slot], *to)

    for n in (0, 1):
        for token in WAITS[n]:
            if token == "e":
                ring_first(n, True)
            elif token == "l":
                ring_second(n, True)
            elif token == "o":
                own_hop(n)
            elif token[0] == "v":
                v_hop(int(token[1]))
            else:
                chain_hop(n, int(token))

    def ring_rest(n, x):
        away = lax.rem(m - x + 2 * DIAGS, DIAGS)
        turn = TURN[n][x // DIAGS]
        mine = takes[n] & (away != 0) & (away != lax.rem(turn + DIAGS, DIAGS))
        run_if(mine, lambda: arrived(ring.at[x], q_ring.at[x]))

    def chain_rest(n, x):
        up, down, _ = chain_moves(n, x)
        run_if(adds[n] & ~(up | down), lambda: arrived(chain.at[x], q_chain.at[x]))

    def accumulate(x):
        other_x = FIRST + m - x
        total[...] += dot(ring[jnp.where(is_second, x, other_x)], chain[jnp.where(is_second, other_x, x)])

    for x in range(FIRST):
        ring_rest(0, x)
        chain_rest(1, x)

    def far(x, carry):
        @pl.when(real & (x <= FIRST + m))
        def _():
            sent_on = x == FIRST + m
            run_if(~is_second & ~sent_on, lambda: arrived(chain.at[x], q_chain.at[x]))
            run_if(is_second & ~sent_on, lambda: arrived(ring.at[x], q_ring.at[x]))
            accumulate(x)

        return carry

    lax.fori_loop(FIRST, FIRST + DIAGS, far, 0)
    for x in range(1, FIRST):
        chain_rest(0, x)
        ring_rest(1, x)
        run_if(real & (x > m), lambda: accumulate(x))

    @pl.when(adds[1])
    def _():
        fresh[...] = total[...].astype(jnp.bfloat16)

    send(adds[1], fresh, other, s_out.at[1], q_other.at[0], *seat(i, 0))

    @pl.when(adds[0])
    def _():
        arrived(other, q_other.at[0])
        total[...] -= other[...].astype(jnp.float32)

    run_if(adds[0] & (m == 0), lambda: arrived(vj, q_vj.at[0]))

    for before in range(DIAGS - 1):

        @pl.when(adds[0] & (m > before))
        def _():
            arrived(near_s.at[before], q_near.at[before])

    for before in range(DIAGS - 1):

        @pl.when(adds[0] & (m > before))
        def _():
            away = m - before
            arrived(new_r.at[before], q_new_r.at[before])
            arrived(new_c.at[before], q_new_c.at[before])
            total[...] += dot(new_r[before], chain[away]) - dot(near_s[away - 1], new_c[before])

    mine = jnp.minimum(m, DIAGS - 2)
    onward = []
    for d in range(1, DIAGS):
        fits = adds[0] & (m + d < DIAGS)
        in_ring = remote(fresh, new_r.at[mine], s_new.at[0, d - 1], q_new_r.at[mine], r, XS * y_at + lax.rem(x_at + d, XS))
        in_chain = remote(fresh, new_c.at[mine], s_new.at[1, d - 1], q_new_c.at[mine], *seat(jnp.maximum(i - d, 0), 0))
        onward += [(fits & (j + d < TOTAL), in_ring), (fits & (i >= d), in_chain)]

    @pl.when(adds[0])
    def _():
        x = left_dot(pairs[t, 1], total[...])
        x = right_dot(x, vj[0]) * gap[...]
        x = left_dot(pairs[t, 0], x)
        x = right_dot(x, vj[1])
        fresh[...] = x.astype(jnp.bfloat16)
        for fits, copy in onward:
            run_if(fits, copy.start)
        solved[...] = x

    later.extend(onward)
    send_any(adds[0], solved, out.at[t], s_out.at[0], q_out.at[t], wrap(i), lax.rem(j, SIDE))

    for n in (0, 1):
        run_if(owned[n], lambda: arrived(out.at[n], q_out.at[n]))

    for cond, copy in later:
        run_if(cond, copy.wait_send)
    for n in (0, 1):
        ring_first(n, False)
        ring_second(n, False)
        for x in chain_slots(n):
            up, down, _ = chain_moves(n, x)
            run_if(up, chain_copy(x, 0).wait_send)
            run_if(down, chain_copy(x, 1).wait_send)
    run_if(v_moves, lambda: v_copy().wait_send())


def exchange(schur, known, pairs, lam):
    bs = schur.shape[-1]
    half, full = jnp.bfloat16, jnp.float32
    dma = pltpu.SemaphoreType.DMA
    vmem = pl.BlockSpec(memory_space=pltpu.VMEM)
    band = FIRST + DIAGS
    return pl.pallas_call(
        kernel,
        out_shape=jax.ShapeDtypeStruct((2, bs, bs), full),
        in_specs=[pl.BlockSpec(memory_space=pltpu.HBM)] * 3 + [vmem],
        out_specs=vmem,
        scratch_shapes=[
            pltpu.VMEM((2, bs, bs), half),
            pltpu.VMEM((2, 2, bs, bs), half),
            pltpu.VMEM((2, bs, bs), full),
            pltpu.VMEM((2, 2, bs, bs), full),
            pltpu.VMEM((band, bs, bs), half),
            pltpu.VMEM((band, bs, bs), half),
            pltpu.VMEM((DIAGS - 1, bs, bs), half),
            pltpu.VMEM((2, bs, bs), half),
            pltpu.VMEM((DIAGS - 1, bs, bs), half),
            pltpu.VMEM((DIAGS - 1, bs, bs), half),
            pltpu.VMEM((bs, bs), half),
            pltpu.VMEM((bs, bs), full),
            pltpu.VMEM((bs, bs), full),
            pltpu.VMEM((bs, bs), half),
            pltpu.VMEM((bs, bs), full),
            dma((3,)), dma((band,)), dma((band,)), dma((DIAGS - 1,)), dma((1,)),
            dma((DIAGS - 1,)), dma((DIAGS - 1,)), dma((1,)), dma((2,)),
            dma((2, 5)), dma((band, 2)), dma((band, 2)), dma((1,)), dma((3, 2, DIAGS)),
            dma((2, DIAGS - 1)), dma((2, DIAGS - 1)), dma((2,)),
        ],
        compiler_params=pltpu.CompilerParams(
            collective_id=0, has_side_effects=True, vmem_limit_bytes=40 * 1024 * 1024
        ),
    )(*(pltpu.with_memory_space_constraint(a, pltpu.HBM) for a in (schur, known, pairs)), lam)


def body(schur_blocks, known_blocks, eigen_pairs, eigenvalues):
    known = known_blocks[:, 0, :, 0]
    solved = exchange(
        schur_blocks[:, 0, :, 0],
        known,
        eigen_pairs[:, 0],
        eigenvalues,
    )
    rows = lax.axis_index("row") + SIDE * jnp.arange(2)[:, None]
    cols = lax.axis_index("col") + SIDE * jnp.arange(2)[None, :]
    away = cols - rows
    new = (away >= FIRST) & (away < FIRST + DIAGS)
    output = jnp.where(new[:, :, None, None], solved[:, None], known)
    return output[:, None, :, None]


def solution(mesh):
    return jax.shard_map(
        body,
        mesh=mesh,
        in_specs=(
            P(None, "row", None, "col", None, None),
            P(None, "row", None, "col", None, None),
            P(None, "row", None, None, None),
            P(),
        ),
        out_specs=P(None, "row", None, "col", None, None),
        check_vma=False,
    )
```

```python
import jax
import jax.numpy as jnp
from jax import lax
from jax.experimental import pallas as pl
from jax.experimental.pallas import tpu as pltpu
from jax.sharding import PartitionSpec as P

FIRST = 8
DIAGS = 4
SIDE = 16
XS = 4
TOTAL = 32
AWAY = 4
LATE = 24
MESH = pl.DeviceIdType.MESH

SENDS = ("cF0", "rF1", "v", "rS0", "rS1", "rF0", "cS0", "x", "cF1", "own", "cS1")
WAITS = (("e", "3", "v0", "0", "1", "v1", "2", "l", "o", "v2"), ("3", "e", "0", "1", "2", "o", "l"))
ENTRY = (((2, 1, 0, 2, 0, 1, 2, 1), (0, 1, 0, 2, 2, 2, 1, 1)), ((0, 0, 0, 2, 0, 1, 2, 2), (0, 1, 0, 0, 0, 1, 2, 2)))
TURN = ((1, 1), (1, -1))
CHAIN_ORDER = (6, 5, 0, 7, 3, 2, 1, 4)


def arrived(ref, sem):
    pltpu.make_async_copy(ref, ref, sem).wait()


def wrap(x):
    return lax.rem(x + 2 * SIDE, SIDE)


def line_of(i, second):
    return lax.rem((i + FIRST) // XS + (1 + 2 * second) * (i // SIDE), XS)


def pick(index, table):
    if isinstance(index, int):
        return table[index]
    chosen = jnp.int32(table[0])
    for n, value in enumerate(table[1:], 1):
        chosen = jnp.where(index == n, value, chosen)
    return chosen


def entry_of(n, j, index):
    early, late = ENTRY[n]
    return jnp.where(j < LATE, pick(index, early), pick(index, late))


def dot(a, b):
    return jnp.dot(a, b, preferred_element_type=jnp.float32)


def halves(x):
    high = x.astype(jnp.bfloat16)
    return high, (x - high.astype(jnp.float32)).astype(jnp.bfloat16)


def left_dot(a, x):
    high, low = halves(x)
    return dot(a, high) + dot(a, low)


def right_dot(x, b):
    high, low = halves(x)
    return dot(high, b) + dot(low, b)


def kernel(
    schur, known_full, pairs_full, lam_full, out,
    lam, known, pairs, known_in, pairs_in, ring, chain, near_s, vj, new_r, new_c, other, total, gap, fresh, solved,
    q_in, q_ring, q_chain, q_near, q_vj, q_new_r, q_new_c, q_other, q_out,
    s_src, s_ring, s_chain, s_v, s_own, s_near, s_new, s_out,
):
    r = lax.axis_index("row")
    c = lax.axis_index("col")
    x_at, y_at = lax.rem(c, XS), c // XS
    e = wrap(c - r)
    later = []

    def remote(src, dst, send_sem, recv_sem, row, col):
        return pltpu.make_async_remote_copy(
            src_ref=src, dst_ref=dst, send_sem=send_sem, recv_sem=recv_sem,
            device_id=(row, col), device_id_type=MESH,
        )

    def run_if(cond, fn):
        pl.when(cond)(fn)

    def send(cond, src, dst, send_sem, recv_sem, row, col):
        copy = remote(src, dst, send_sem, recv_sem, row, col)
        run_if(cond, copy.start)
        later.append((cond, copy))

    def send_any(cond, src, dst, send_sem, recv_sem, row, col):
        here = (row == r) & (col == c)
        run_if(cond & here, pltpu.make_async_copy(src, dst, recv_sem).start)
        send(cond & ~here, src, dst, send_sem, recv_sem, row, col)

    def seat(i, second, x=x_at):
        return wrap(i + AWAY * second), XS * line_of(i, second) + x

    fetch = [
        pltpu.make_async_copy(pairs_full, pairs_in, q_in.at[2]),
        pltpu.make_async_copy(lam_full, lam, q_in.at[3]),
    ]
    for t in (0, 1):
        b = jnp.minimum((r + SIDE * t + e) // SIDE, 1)
        fetch.append(pltpu.make_async_copy(known_full.at[t, b], known_in.at[t], q_in.at[t]))
    for copy in fetch:
        copy.start()

    barrier = pltpu.get_barrier_semaphore()

    def meet(row, col):
        pl.semaphore_signal(barrier, inc=1, device_id=(row, col), device_id_type=MESH)

    def greet_line(step, carry):
        meet(lax.rem(r + step // XS, SIDE), XS * lax.rem(y_at + step, XS) + x_at)
        return carry

    def greet_row(step, carry):
        col = XS * lax.rem(step, XS) + lax.rem(x_at + 1 + step // XS, XS)
        meet(r, col)
        return carry

    lines = SIDE * XS - 1
    others = XS * (XS - 1)
    lax.fori_loop(1, lines + 1, greet_line, 0)
    lax.fori_loop(0, others, greet_row, 0)
    for copy in fetch:
        copy.wait()
    known[...] = known_in[...].astype(jnp.bfloat16)
    pairs[...] = pairs_in[...].astype(jnp.bfloat16)
    pl.semaphore_wait(barrier, lines + others)

    near = e < FIRST
    eb = jnp.minimum(e, FIRST - 1)
    places = []
    for t in (0, 1):
        k = r + SIDE * t
        j = k + e
        b = jnp.minimum(j // SIDE, 1)
        last = jnp.clip(j - FIRST, 0, DIAGS - 1)
        to_ring = near & (k < TOTAL - FIRST)
        to_chain = near & (j >= FIRST) & (j < TOTAL)
        entries = [
            seat(jnp.maximum(j - FIRST - jnp.minimum(entry_of(n, j, eb), last), 0), n) for n in (0, 1)
        ]
        v_entry = seat(jnp.maximum(j - FIRST - last, 0), 0)
        places.append((k, j, b, to_ring, to_chain, entries, v_entry))

    mo = jnp.clip(e - FIRST, 0, DIAGS - 1)
    owner = (e >= FIRST) & (e < FIRST + DIAGS)
    owned = [owner & (places[t][1] < TOTAL) for t in (0, 1)]

    def send_near(group, kind, t):
        k, j, b, to_ring, to_chain, entries, _ = places[t]
        n = "FS".index(kind)
        src = (known.at[t], schur.at[t, b])[n]
        used = e >= n
        at = 2 * n + (group == "c")
        if group == "r":
            send_any(to_ring & used, src, ring.at[eb], s_src.at[t, at], q_ring.at[eb], *seat(k, n))
        else:
            send_any(to_chain & used, src, chain.at[eb], s_src.at[t, at], q_chain.at[eb], *entries[1 - n])

    def send_own(t):
        k, j, b = places[t][:3]
        slot = FIRST + mo
        send(owned[t], schur.at[t, b], ring.at[slot], s_own.at[t, 0, 0], q_ring.at[slot], *seat(k, 1))
        send_any(owned[t], schur.at[t, b], chain.at[slot], s_own.at[t, 1, 0], q_chain.at[slot], *seat(k, 0))

    def send_close(t):
        k, j, b = places[t][:3]
        slot = jnp.clip(e - 1, 0, DIAGS - 2)
        for d in range(DIAGS - 1):
            fits = (e >= 1) & (e + d < DIAGS) & (j + FIRST + d < TOTAL)
            send_any(fits, schur.at[t, b], near_s.at[slot], s_near.at[t, d], q_near.at[slot], *seat(k, 0, lax.rem(x_at + d, XS)))

    for token in SENDS:
        if token == "own":
            send_own(0)
            send_own(1)
        elif token == "x":
            send_close(0)
            send_close(1)
        elif token == "v":
            for t in (0, 1):
                send(places[t][4] & (e == 0), pairs.at[t], vj, s_src.at[t, 4], q_vj.at[0], *places[t][6])
        else:
            send_near(token[0], token[1], int(token[2]))

    i0 = wrap(r - AWAY)
    few = TOTAL - SIDE - FIRST
    first0, first1 = y_at == line_of(r, 0), (r < few) & (y_at == line_of(r + SIDE, 0))
    second0, second1 = y_at == line_of(i0, 1), (i0 < few) & (y_at == line_of(i0 + SIDE, 1))
    is_second = second0 | second1
    part = first0 | first1 | is_second
    kind = jnp.where(is_second, 1, 0)
    t = jnp.where(first1 | second1, 1, 0)
    i = jnp.where(is_second, i0, r) + SIDE * t
    m = lax.rem(x_at + 2 * SIDE - i, XS)
    j = i + FIRST + m
    real = part & (j < TOTAL)
    last = jnp.minimum(DIAGS - 1, i + m)
    takes = (part & ~is_second, is_second)
    adds = (real & ~is_second, real & is_second)
    col_next = (XS * y_at + lax.rem(x_at + 1, XS), XS * y_at + lax.rem(x_at + XS - 1, XS))

    @pl.when(adds[0])
    def _():
        rows = jnp.broadcast_to(lam[pl.ds(i, 1), :], total.shape).T
        gap[...] = 1.0 / (rows - lam[pl.ds(jnp.minimum(j, TOTAL - 1), 1), :])

    @pl.when(real)
    def _():
        total[...] = jnp.zeros(total.shape, jnp.float32)

    def member(step):
        return seat(jnp.maximum(i - step, 0), kind)

    def ring_copy(x, d):
        return remote(ring.at[x], ring.at[x], s_ring.at[x, d], q_ring.at[x], r, col_next[d])

    def chain_copy(x, d):
        return remote(chain.at[x], chain.at[x], s_chain.at[x, d], q_chain.at[x], *member(1 - 2 * d))

    def v_copy():
        return remote(vj, vj, s_v.at[0], q_vj.at[0], *member(-1))

    def ring_first(n, start):
        for x in (m, m + DIAGS):

            @pl.when(takes[n] & (x >= n))
            def _():
                if start:
                    arrived(ring.at[x], q_ring.at[x])
                for d in (0, 1):
                    ring_copy(x, d).start() if start else ring_copy(x, d).wait_send()

    def ring_second(n, start):
        for high in (0, 1):
            turn = TURN[n][high]
            x = lax.rem(m + DIAGS - turn, DIAGS) + DIAGS * high

            @pl.when(takes[n] & (x >= n))
            def _():
                copy = ring_copy(x, 0 if turn == 1 else 1)
                if start:
                    arrived(ring.at[x], q_ring.at[x])
                    copy.start()
                else:
                    copy.wait_send()

    def chain_moves(n, x):
        at = jnp.minimum(entry_of(n, j, x), last)
        up = adds[n] & (m >= at) & (m < last)
        down = adds[n] & (m <= at) & (m > 0)
        return up, down, jnp.abs(m - at)

    def chain_slots(n):
        return [x for x in CHAIN_ORDER if x + n > 0]

    def chain_hop(n, depth):
        for x in chain_slots(n):
            up, down, hops = chain_moves(n, x)
            now = hops == depth
            run_if((up | down) & now, lambda: arrived(chain.at[x], q_chain.at[x]))
            run_if(up & now, chain_copy(x, 0).start)
            run_if(down & now, chain_copy(x, 1).start)

    v_moves = adds[0] & (m > 0)

    def v_hop(depth):
        @pl.when(v_moves & (last - m == depth))
        def _():
            arrived(vj, q_vj.at[0])
            v_copy().start()

    def own_hop(n):
        slot = FIRST + jnp.clip(m, 0, DIAGS - 1)
        ref, sems = ((chain, q_chain), (ring, q_ring))[n]
        run_if(adds[n], lambda: arrived(ref.at[slot], sems.at[slot]))
        for d in range(1, DIAGS):
            if n:
                fits, to = j + d < TOTAL, (r, XS * y_at + lax.rem(x_at + d, XS))
            else:
                fits, to = i >= d, seat(jnp.maximum(i - d, 0), 0)
            send(adds[n] & (m + d < DIAGS) & fits, ref.at[slot], ref.at[slot], s_own.at[2, n, d], sems.at[slot], *to)

    for n in (0, 1):
        for token in WAITS[n]:
            if token == "e":
                ring_first(n, True)
            elif token == "l":
                ring_second(n, True)
            elif token == "o":
                own_hop(n)
            elif token[0] == "v":
                v_hop(int(token[1]))
            else:
                chain_hop(n, int(token))

    def ring_rest(n, x):
        away = lax.rem(m - x + 2 * DIAGS, DIAGS)
        turn = TURN[n][x // DIAGS]
        mine = takes[n] & (away != 0) & (away != lax.rem(turn + DIAGS, DIAGS))
        run_if(mine, lambda: arrived(ring.at[x], q_ring.at[x]))

    def chain_rest(n, x):
        up, down, _ = chain_moves(n, x)
        run_if(adds[n] & ~(up | down), lambda: arrived(chain.at[x], q_chain.at[x]))

    def accumulate(x):
        other_x = FIRST + m - x
        total[...] += dot(ring[jnp.where(is_second, x, other_x)], chain[jnp.where(is_second, other_x, x)])

    for x in range(FIRST):
        ring_rest(0, x)
        chain_rest(1, x)

    def far(x, carry):
        @pl.when(real & (x <= FIRST + m))
        def _():
            sent_on = x == FIRST + m
            run_if(~is_second & ~sent_on, lambda: arrived(chain.at[x], q_chain.at[x]))
            run_if(is_second & ~sent_on, lambda: arrived(ring.at[x], q_ring.at[x]))
            accumulate(x)

        return carry

    lax.fori_loop(FIRST, FIRST + DIAGS, far, 0)
    for x in range(1, FIRST):
        chain_rest(0, x)
        ring_rest(1, x)
        run_if(real & (x > m), lambda: accumulate(x))

    @pl.when(adds[1])
    def _():
        fresh[...] = total[...].astype(jnp.bfloat16)

    send(adds[1], fresh, other, s_out.at[1], q_other.at[0], *seat(i, 0))

    @pl.when(adds[0])
    def _():
        arrived(other, q_other.at[0])
        total[...] -= other[...].astype(jnp.float32)

    run_if(adds[0] & (m == 0), lambda: arrived(vj, q_vj.at[0]))

    for before in range(DIAGS - 1):

        @pl.when(adds[0] & (m > before))
        def _():
            arrived(near_s.at[before], q_near.at[before])

    for before in range(DIAGS - 1):

        @pl.when(adds[0] & (m > before))
        def _():
            away = m - before
            arrived(new_r.at[before], q_new_r.at[before])
            arrived(new_c.at[before], q_new_c.at[before])
            total[...] += dot(new_r[before], chain[away]) - dot(near_s[away - 1], new_c[before])

    mine = jnp.minimum(m, DIAGS - 2)
    onward = []
    for d in range(1, DIAGS):
        fits = adds[0] & (m + d < DIAGS)
        in_ring = remote(fresh, new_r.at[mine], s_new.at[0, d - 1], q_new_r.at[mine], r, XS * y_at + lax.rem(x_at + d, XS))
        in_chain = remote(fresh, new_c.at[mine], s_new.at[1, d - 1], q_new_c.at[mine], *seat(jnp.maximum(i - d, 0), 0))
        onward += [(fits & (j + d < TOTAL), in_ring), (fits & (i >= d), in_chain)]

    @pl.when(adds[0])
    def _():
        x = left_dot(pairs[t, 1], total[...])
        x = right_dot(x, vj[0]) * gap[...]
        x = left_dot(pairs[t, 0], x)
        x = right_dot(x, vj[1])
        fresh[...] = x.astype(jnp.bfloat16)
        for fits, copy in onward:
            run_if(fits, copy.start)
        solved[...] = x

    later.extend(onward)
    send_any(adds[0], solved, out.at[t], s_out.at[0], q_out.at[t], wrap(i), lax.rem(j, SIDE))

    for n in (0, 1):
        run_if(owned[n], lambda: arrived(out.at[n], q_out.at[n]))

    for cond, copy in later:
        run_if(cond, copy.wait_send)
    for n in (0, 1):
        ring_first(n, False)
        ring_second(n, False)
        for x in chain_slots(n):
            up, down, _ = chain_moves(n, x)
            run_if(up, chain_copy(x, 0).wait_send)
            run_if(down, chain_copy(x, 1).wait_send)
    run_if(v_moves, lambda: v_copy().wait_send())


def exchange(schur, known, pairs, lam):
    bs = schur.shape[-1]
    half, full = jnp.bfloat16, jnp.float32
    dma = pltpu.SemaphoreType.DMA
    vmem = pl.BlockSpec(memory_space=pltpu.VMEM)
    band = FIRST + DIAGS
    return pl.pallas_call(
        kernel,
        out_shape=jax.ShapeDtypeStruct((2, bs, bs), full),
        in_specs=[pl.BlockSpec(memory_space=pltpu.HBM)] * 4,
        out_specs=vmem,
        scratch_shapes=[
            pltpu.VMEM(lam.shape, full),
            pltpu.VMEM((2, bs, bs), half),
            pltpu.VMEM((2, 2, bs, bs), half),
            pltpu.VMEM((2, bs, bs), full),
            pltpu.VMEM((2, 2, bs, bs), full),
            pltpu.VMEM((band, bs, bs), half),
            pltpu.VMEM((band, bs, bs), half),
            pltpu.VMEM((DIAGS - 1, bs, bs), half),
            pltpu.VMEM((2, bs, bs), half),
            pltpu.VMEM((DIAGS - 1, bs, bs), half),
            pltpu.VMEM((DIAGS - 1, bs, bs), half),
            pltpu.VMEM((bs, bs), half),
            pltpu.VMEM((bs, bs), full),
            pltpu.VMEM((bs, bs), full),
            pltpu.VMEM((bs, bs), half),
            pltpu.VMEM((bs, bs), full),
            dma((4,)), dma((band,)), dma((band,)), dma((DIAGS - 1,)), dma((1,)),
            dma((DIAGS - 1,)), dma((DIAGS - 1,)), dma((1,)), dma((2,)),
            dma((2, 5)), dma((band, 2)), dma((band, 2)), dma((1,)), dma((3, 2, DIAGS)),
            dma((2, DIAGS - 1)), dma((2, DIAGS - 1)), dma((2,)),
        ],
        compiler_params=pltpu.CompilerParams(
            collective_id=0, has_side_effects=True, vmem_limit_bytes=40 * 1024 * 1024
        ),
    )(*(pltpu.with_memory_space_constraint(a, pltpu.HBM) for a in (schur, known, pairs, lam)))


def body(schur_blocks, known_blocks, eigen_pairs, eigenvalues):
    known = known_blocks[:, 0, :, 0]
    solved = exchange(
        schur_blocks[:, 0, :, 0],
        known,
        eigen_pairs[:, 0],
        eigenvalues,
    )
    rows = lax.axis_index("row") + SIDE * jnp.arange(2)[:, None]
    cols = lax.axis_index("col") + SIDE * jnp.arange(2)[None, :]
    away = cols - rows
    new = (away >= FIRST) & (away < FIRST + DIAGS)
    output = jnp.where(new[:, :, None, None], solved[:, None], known)
    return output[:, None, :, None]


def solution(mesh):
    return jax.shard_map(
        body,
        mesh=mesh,
        in_specs=(
            P(None, "row", None, "col", None, None),
            P(None, "row", None, "col", None, None),
            P(None, "row", None, None, None),
            P(),
        ),
        out_specs=P(None, "row", None, "col", None, None),
        check_vma=False,
    )
```

```python
import jax
import jax.numpy as jnp
from jax import lax
from jax.experimental import pallas as pl
from jax.experimental.pallas import tpu as pltpu
from jax.sharding import PartitionSpec as P

FIRST = 8
DIAGS = 4
SIDE = 16
XS = 4
TOTAL = 32
AWAY = 4
LATE = 24
MESH = pl.DeviceIdType.MESH

SENDS = ("rS1", "rF1", "cF0", "rF0", "rS0", "cF1", "x", "own", "cS0", "v", "cS1")
WAITS = (("e", "0", "v1", "v0", "1", "2", "3", "o", "l", "v2"), ("e", "0", "1", "2", "l", "o", "3"))
ENTRY = (((3, 1, 1, 2, 0, 1, 1, 1), (0, 1, 0, 2, 1, 0, 1, 1)), ((1, 0, 0, 0, 0, 1, 2, 2), (0, 1, 0, 0, 0, 1, 2, 3)))
TURN = ((1, -1), (1, -1))
CHAIN_ORDER = (0, 5, 7, 3, 6, 1, 2, 4)


def arrived(ref, sem):
    pltpu.make_async_copy(ref, ref, sem).wait()


def wrap(x):
    return lax.rem(x + 2 * SIDE, SIDE)


def line_of(i, second):
    return lax.rem((i + FIRST) // XS + (1 + 2 * second) * (i // SIDE), XS)


def pick(index, table):
    if isinstance(index, int):
        return table[index]
    chosen = jnp.int32(table[0])
    for n, value in enumerate(table[1:], 1):
        chosen = jnp.where(index == n, value, chosen)
    return chosen


def entry_of(n, j, index):
    early, late = ENTRY[n]
    return jnp.where(j < LATE, pick(index, early), pick(index, late))


def dot(a, b):
    return jnp.dot(a, b, preferred_element_type=jnp.float32)


def halves(x):
    high = x.astype(jnp.bfloat16)
    return high, (x - high.astype(jnp.float32)).astype(jnp.bfloat16)


def left_dot(a, x):
    high, low = halves(x)
    return dot(a, high) + dot(a, low)


def right_dot(x, b):
    high, low = halves(x)
    return dot(high, b) + dot(low, b)


def kernel(
    schur, known_full, pairs_full, lam_full, out,
    lam, known, pairs, known_in, pairs_in, ring, chain, near_s, vj, new_r, new_c, other, total, gap, fresh, solved,
    q_in, q_ring, q_chain, q_near, q_vj, q_new_r, q_new_c, q_other, q_out,
    s_src, s_ring, s_chain, s_v, s_own, s_near, s_new, s_out,
):
    r = lax.axis_index("row")
    c = lax.axis_index("col")
    x_at, y_at = lax.rem(c, XS), c // XS
    e = wrap(c - r)
    later = []

    def remote(src, dst, send_sem, recv_sem, row, col):
        return pltpu.make_async_remote_copy(
            src_ref=src, dst_ref=dst, send_sem=send_sem, recv_sem=recv_sem,
            device_id=(row, col), device_id_type=MESH,
        )

    def run_if(cond, fn):
        pl.when(cond)(fn)

    def send(cond, src, dst, send_sem, recv_sem, row, col):
        copy = remote(src, dst, send_sem, recv_sem, row, col)
        run_if(cond, copy.start)
        later.append((cond, copy))

    def send_any(cond, src, dst, send_sem, recv_sem, row, col):
        here = (row == r) & (col == c)
        run_if(cond & here, pltpu.make_async_copy(src, dst, recv_sem).start)
        send(cond & ~here, src, dst, send_sem, recv_sem, row, col)

    def seat(i, second, x=x_at):
        return wrap(i + AWAY * second), XS * line_of(i, second) + x

    fetch = [
        pltpu.make_async_copy(pairs_full, pairs_in, q_in.at[2]),
        pltpu.make_async_copy(lam_full, lam, q_in.at[3]),
    ]
    for t in (0, 1):
        b = jnp.minimum((r + SIDE * t + e) // SIDE, 1)
        fetch.append(pltpu.make_async_copy(known_full.at[t, b], known_in.at[t], q_in.at[t]))
    for copy in fetch:
        copy.start()

    barrier = pltpu.get_barrier_semaphore()

    def meet(row, col):
        pl.semaphore_signal(barrier, inc=1, device_id=(row, col), device_id_type=MESH)

    def greet_line(step, carry):
        meet(lax.rem(r + step // XS, SIDE), XS * lax.rem(y_at + step, XS) + x_at)
        return carry

    def greet_row(step, carry):
        col = XS * lax.rem(step, XS) + lax.rem(x_at + 1 + step // XS, XS)
        meet(r, col)
        return carry

    lines = SIDE * XS - 1
    others = XS * (XS - 1)
    lax.fori_loop(1, lines + 1, greet_line, 0)
    lax.fori_loop(0, others, greet_row, 0)
    for copy in fetch:
        copy.wait()
    known[...] = known_in[...].astype(jnp.bfloat16)
    pairs[...] = pairs_in[...].astype(jnp.bfloat16)
    pl.semaphore_wait(barrier, lines + others)

    near = e < FIRST
    eb = jnp.minimum(e, FIRST - 1)
    places = []
    for t in (0, 1):
        k = r + SIDE * t
        j = k + e
        b = jnp.minimum(j // SIDE, 1)
        last = jnp.clip(j - FIRST, 0, DIAGS - 1)
        to_ring = near & (k < TOTAL - FIRST)
        to_chain = near & (j >= FIRST) & (j < TOTAL)
        entries = [
            seat(jnp.maximum(j - FIRST - jnp.minimum(entry_of(n, j, eb), last), 0), n) for n in (0, 1)
        ]
        v_entry = seat(jnp.maximum(j - FIRST - last, 0), 0)
        places.append((k, j, b, to_ring, to_chain, entries, v_entry))

    mo = jnp.clip(e - FIRST, 0, DIAGS - 1)
    owner = (e >= FIRST) & (e < FIRST + DIAGS)
    owned = [owner & (places[t][1] < TOTAL) for t in (0, 1)]

    def send_near(group, kind, t):
        k, j, b, to_ring, to_chain, entries, _ = places[t]
        n = "FS".index(kind)
        src = (known.at[t], schur.at[t, b])[n]
        used = e >= n
        at = 2 * n + (group == "c")
        if group == "r":
            send_any(to_ring & used, src, ring.at[eb], s_src.at[t, at], q_ring.at[eb], *seat(k, n))
        else:
            send_any(to_chain & used, src, chain.at[eb], s_src.at[t, at], q_chain.at[eb], *entries[1 - n])

    def send_own(t):
        k, j, b = places[t][:3]
        slot = FIRST + mo
        send(owned[t], schur.at[t, b], ring.at[slot], s_own.at[t, 0, 0], q_ring.at[slot], *seat(k, 1))
        send_any(owned[t], schur.at[t, b], chain.at[slot], s_own.at[t, 1, 0], q_chain.at[slot], *seat(k, 0))

    def send_close(t):
        k, j, b = places[t][:3]
        slot = jnp.clip(e - 1, 0, DIAGS - 2)
        for d in range(DIAGS - 1):
            fits = (e >= 1) & (e + d < DIAGS) & (j + FIRST + d < TOTAL)
            send_any(fits, schur.at[t, b], near_s.at[slot], s_near.at[t, d], q_near.at[slot], *seat(k, 0, lax.rem(x_at + d, XS)))

    for token in SENDS:
        if token == "own":
            send_own(0)
            send_own(1)
        elif token == "x":
            send_close(0)
            send_close(1)
        elif token == "v":
            for t in (0, 1):
                send(places[t][4] & (e == 0), pairs.at[t], vj, s_src.at[t, 4], q_vj.at[0], *places[t][6])
        else:
            send_near(token[0], token[1], int(token[2]))

    i0 = wrap(r - AWAY)
    few = TOTAL - SIDE - FIRST
    first0, first1 = y_at == line_of(r, 0), (r < few) & (y_at == line_of(r + SIDE, 0))
    second0, second1 = y_at == line_of(i0, 1), (i0 < few) & (y_at == line_of(i0 + SIDE, 1))
    is_second = second0 | second1
    part = first0 | first1 | is_second
    kind = jnp.where(is_second, 1, 0)
    t = jnp.where(first1 | second1, 1, 0)
    i = jnp.where(is_second, i0, r) + SIDE * t
    m = lax.rem(x_at + 2 * SIDE - i, XS)
    j = i + FIRST + m
    real = part & (j < TOTAL)
    last = jnp.minimum(DIAGS - 1, i + m)
    takes = (part & ~is_second, is_second)
    adds = (real & ~is_second, real & is_second)
    col_next = (XS * y_at + lax.rem(x_at + 1, XS), XS * y_at + lax.rem(x_at + XS - 1, XS))

    @pl.when(adds[0])
    def _():
        rows = jnp.broadcast_to(lam[pl.ds(i, 1), :], total.shape).T
        gap[...] = 1.0 / (rows - lam[pl.ds(jnp.minimum(j, TOTAL - 1), 1), :])

    @pl.when(real)
    def _():
        total[...] = jnp.zeros(total.shape, jnp.float32)

    def member(step):
        return seat(jnp.maximum(i - step, 0), kind)

    def ring_copy(x, d):
        return remote(ring.at[x], ring.at[x], s_ring.at[x, d], q_ring.at[x], r, col_next[d])

    def chain_copy(x, d):
        return remote(chain.at[x], chain.at[x], s_chain.at[x, d], q_chain.at[x], *member(1 - 2 * d))

    def v_copy():
        return remote(vj, vj, s_v.at[0], q_vj.at[0], *member(-1))

    def ring_first(n, start):
        for x in (m, m + DIAGS):

            @pl.when(takes[n] & (x >= n))
            def _():
                if start:
                    arrived(ring.at[x], q_ring.at[x])
                for d in (0, 1):
                    ring_copy(x, d).start() if start else ring_copy(x, d).wait_send()

    def ring_second(n, start):
        for high in (0, 1):
            turn = TURN[n][high]
            x = lax.rem(m + DIAGS - turn, DIAGS) + DIAGS * high

            @pl.when(takes[n] & (x >= n))
            def _():
                copy = ring_copy(x, 0 if turn == 1 else 1)
                if start:
                    arrived(ring.at[x], q_ring.at[x])
                    copy.start()
                else:
                    copy.wait_send()

    def chain_moves(n, x):
        at = jnp.minimum(entry_of(n, j, x), last)
        up = adds[n] & (m >= at) & (m < last)
        down = adds[n] & (m <= at) & (m > 0)
        return up, down, jnp.abs(m - at)

    def chain_slots(n):
        return [x for x in CHAIN_ORDER if x + n > 0]

    def chain_hop(n, depth):
        for x in chain_slots(n):
            up, down, hops = chain_moves(n, x)
            now = hops == depth
            run_if((up | down) & now, lambda: arrived(chain.at[x], q_chain.at[x]))
            run_if(up & now, chain_copy(x, 0).start)
            run_if(down & now, chain_copy(x, 1).start)

    v_moves = adds[0] & (m > 0)

    def v_hop(depth):
        @pl.when(v_moves & (last - m == depth))
        def _():
            arrived(vj, q_vj.at[0])
            v_copy().start()

    def own_hop(n):
        slot = FIRST + jnp.clip(m, 0, DIAGS - 1)
        ref, sems = ((chain, q_chain), (ring, q_ring))[n]
        run_if(adds[n], lambda: arrived(ref.at[slot], sems.at[slot]))
        for d in range(1, DIAGS):
            if n:
                fits, to = j + d < TOTAL, (r, XS * y_at + lax.rem(x_at + d, XS))
            else:
                fits, to = i >= d, seat(jnp.maximum(i - d, 0), 0)
            send(adds[n] & (m + d < DIAGS) & fits, ref.at[slot], ref.at[slot], s_own.at[2, n, d], sems.at[slot], *to)

    for n in (0, 1):
        for token in WAITS[n]:
            if token == "e":
                ring_first(n, True)
            elif token == "l":
                ring_second(n, True)
            elif token == "o":
                own_hop(n)
            elif token[0] == "v":
                v_hop(int(token[1]))
            else:
                chain_hop(n, int(token))

    def ring_rest(n, x):
        away = lax.rem(m - x + 2 * DIAGS, DIAGS)
        turn = TURN[n][x // DIAGS]
        mine = takes[n] & (away != 0) & (away != lax.rem(turn + DIAGS, DIAGS))
        run_if(mine, lambda: arrived(ring.at[x], q_ring.at[x]))

    def chain_rest(n, x):
        up, down, _ = chain_moves(n, x)
        run_if(adds[n] & ~(up | down), lambda: arrived(chain.at[x], q_chain.at[x]))

    def accumulate(x):
        other_x = FIRST + m - x
        total[...] += dot(ring[jnp.where(is_second, x, other_x)], chain[jnp.where(is_second, other_x, x)])

    for x in range(FIRST):
        ring_rest(0, x)
        chain_rest(1, x)

    def far(x, carry):
        @pl.when(real & (x <= FIRST + m))
        def _():
            sent_on = x == FIRST + m
            run_if(~is_second & ~sent_on, lambda: arrived(chain.at[x], q_chain.at[x]))
            run_if(is_second & ~sent_on, lambda: arrived(ring.at[x], q_ring.at[x]))
            accumulate(x)

        return carry

    lax.fori_loop(FIRST, FIRST + DIAGS, far, 0)
    for x in range(1, FIRST):
        chain_rest(0, x)
        ring_rest(1, x)
        run_if(real & (x > m), lambda: accumulate(x))

    @pl.when(adds[1])
    def _():
        fresh[...] = total[...].astype(jnp.bfloat16)

    send(adds[1], fresh, other, s_out.at[1], q_other.at[0], *seat(i, 0))

    @pl.when(adds[0])
    def _():
        arrived(other, q_other.at[0])
        total[...] -= other[...].astype(jnp.float32)

    run_if(adds[0] & (m == 0), lambda: arrived(vj, q_vj.at[0]))

    for before in range(DIAGS - 1):

        @pl.when(adds[0] & (m > before))
        def _():
            arrived(near_s.at[before], q_near.at[before])

    for before in range(DIAGS - 1):

        @pl.when(adds[0] & (m > before))
        def _():
            away = m - before
            arrived(new_r.at[before], q_new_r.at[before])
            arrived(new_c.at[before], q_new_c.at[before])
            total[...] += dot(new_r[before], chain[away]) - dot(near_s[away - 1], new_c[before])

    mine = jnp.minimum(m, DIAGS - 2)
    onward = []
    for d in range(1, DIAGS):
        fits = adds[0] & (m + d < DIAGS)
        in_ring = remote(fresh, new_r.at[mine], s_new.at[0, d - 1], q_new_r.at[mine], r, XS * y_at + lax.rem(x_at + d, XS))
        in_chain = remote(fresh, new_c.at[mine], s_new.at[1, d - 1], q_new_c.at[mine], *seat(jnp.maximum(i - d, 0), 0))
        onward += [(fits & (j + d < TOTAL), in_ring), (fits & (i >= d), in_chain)]

    @pl.when(adds[0])
    def _():
        x = left_dot(pairs[t, 1], total[...])
        x = right_dot(x, vj[0]) * gap[...]
        x = left_dot(pairs[t, 0], x)
        x = right_dot(x, vj[1])
        fresh[...] = x.astype(jnp.bfloat16)
        for fits, copy in onward:
            run_if(fits, copy.start)
        solved[...] = x

    later.extend(onward)
    send_any(adds[0], solved, out.at[t], s_out.at[0], q_out.at[t], wrap(i), lax.rem(j, SIDE))

    for n in (0, 1):
        run_if(owned[n], lambda: arrived(out.at[n], q_out.at[n]))

    for cond, copy in later:
        run_if(cond, copy.wait_send)
    for n in (0, 1):
        ring_first(n, False)
        ring_second(n, False)
        for x in chain_slots(n):
            up, down, _ = chain_moves(n, x)
            run_if(up, chain_copy(x, 0).wait_send)
            run_if(down, chain_copy(x, 1).wait_send)
    run_if(v_moves, lambda: v_copy().wait_send())


def exchange(schur, known, pairs, lam):
    bs = schur.shape[-1]
    half, full = jnp.bfloat16, jnp.float32
    dma = pltpu.SemaphoreType.DMA
    vmem = pl.BlockSpec(memory_space=pltpu.VMEM)
    band = FIRST + DIAGS
    return pl.pallas_call(
        kernel,
        out_shape=jax.ShapeDtypeStruct((2, bs, bs), full),
        in_specs=[pl.BlockSpec(memory_space=pltpu.HBM)] * 4,
        out_specs=vmem,
        scratch_shapes=[
            pltpu.VMEM(lam.shape, full),
            pltpu.VMEM((2, bs, bs), half),
            pltpu.VMEM((2, 2, bs, bs), half),
            pltpu.VMEM((2, bs, bs), full),
            pltpu.VMEM((2, 2, bs, bs), full),
            pltpu.VMEM((band, bs, bs), half),
            pltpu.VMEM((band, bs, bs), half),
            pltpu.VMEM((DIAGS - 1, bs, bs), half),
            pltpu.VMEM((2, bs, bs), half),
            pltpu.VMEM((DIAGS - 1, bs, bs), half),
            pltpu.VMEM((DIAGS - 1, bs, bs), half),
            pltpu.VMEM((bs, bs), half),
            pltpu.VMEM((bs, bs), full),
            pltpu.VMEM((bs, bs), full),
            pltpu.VMEM((bs, bs), half),
            pltpu.VMEM((bs, bs), full),
            dma((4,)), dma((band,)), dma((band,)), dma((DIAGS - 1,)), dma((1,)),
            dma((DIAGS - 1,)), dma((DIAGS - 1,)), dma((1,)), dma((2,)),
            dma((2, 5)), dma((band, 2)), dma((band, 2)), dma((1,)), dma((3, 2, DIAGS)),
            dma((2, DIAGS - 1)), dma((2, DIAGS - 1)), dma((2,)),
        ],
        compiler_params=pltpu.CompilerParams(
            collective_id=0, has_side_effects=True, vmem_limit_bytes=40 * 1024 * 1024
        ),
    )(*(pltpu.with_memory_space_constraint(a, pltpu.HBM) for a in (schur, known, pairs, lam)))


def body(schur_blocks, known_blocks, eigen_pairs, eigenvalues):
    known = known_blocks[:, 0, :, 0]
    solved = exchange(
        schur_blocks[:, 0, :, 0],
        known,
        eigen_pairs[:, 0],
        eigenvalues,
    )
    rows = lax.axis_index("row") + SIDE * jnp.arange(2)[:, None]
    cols = lax.axis_index("col") + SIDE * jnp.arange(2)[None, :]
    away = cols - rows
    new = (away >= FIRST) & (away < FIRST + DIAGS)
    output = jnp.where(new[:, :, None, None], solved[:, None], known)
    return output[:, None, :, None]


def solution(mesh):
    return jax.shard_map(
        body,
        mesh=mesh,
        in_specs=(
            P(None, "row", None, "col", None, None),
            P(None, "row", None, "col", None, None),
            P(None, "row", None, None, None),
            P(),
        ),
        out_specs=P(None, "row", None, "col", None, None),
        check_vma=False,
    )
```

```python
import jax
import jax.numpy as jnp
from jax import lax
from jax.experimental import pallas as pl
from jax.experimental.pallas import tpu as pltpu
from jax.sharding import PartitionSpec as P

FIRST = 8
DIAGS = 4
SIDE = 16
XS = 4
TOTAL = 32
AWAY = 4
LATE = 24
MESH = pl.DeviceIdType.MESH

SENDS = ("rS1", "cF0", "rF0", "rF1", "rS0", "x", "v", "cS1", "own", "cF1", "cS0")
WAITS = (("0", "e", "v1", "v0", "1", "2", "o", "l", "3", "v2"), ("e", "0", "1", "2", "l", "3", "o"))
ENTRY = (((0, 1, 1, 2, 0, 1, 1, 1), (0, 1, 0, 2, 1, 0, 1, 1)), ((1, 0, 0, 0, 0, 1, 2, 2), (0, 1, 0, 0, 0, 1, 1, 3)))
TURN = ((-1, -1), (1, -1))
CHAIN_ORDER = (5, 7, 3, 0, 6, 1, 2, 4)


def arrived(ref, sem):
    pltpu.make_async_copy(ref, ref, sem).wait()


def wrap(x):
    return lax.rem(x + 2 * SIDE, SIDE)


def line_of(i, second):
    return lax.rem((i + FIRST) // XS + (1 + 2 * second) * (i // SIDE), XS)


def pick(index, table):
    if isinstance(index, int):
        return table[index]
    chosen = jnp.int32(table[0])
    for n, value in enumerate(table[1:], 1):
        chosen = jnp.where(index == n, value, chosen)
    return chosen


def entry_of(n, j, index):
    early, late = ENTRY[n]
    return jnp.where(j < LATE, pick(index, early), pick(index, late))


def dot(a, b):
    return jnp.dot(a, b, preferred_element_type=jnp.float32)


def halves(x):
    high = x.astype(jnp.bfloat16)
    return high, (x - high.astype(jnp.float32)).astype(jnp.bfloat16)


def left_dot(a, x):
    high, low = halves(x)
    return dot(a, high) + dot(a, low)


def right_dot(x, b):
    high, low = halves(x)
    return dot(high, b) + dot(low, b)


def kernel(
    schur, known_full, pairs_full, lam_full, out,
    lam, known, pairs, known_in, pairs_in, ring, chain, near_s, vj, new_r, new_c, other, total, gap, fresh, solved,
    q_in, q_ring, q_chain, q_near, q_vj, q_new_r, q_new_c, q_other, q_out,
    s_src, s_ring, s_chain, s_v, s_own, s_near, s_new, s_out,
):
    r = lax.axis_index("row")
    c = lax.axis_index("col")
    x_at, y_at = lax.rem(c, XS), c // XS
    e = wrap(c - r)
    later = []

    def remote(src, dst, send_sem, recv_sem, row, col):
        return pltpu.make_async_remote_copy(
            src_ref=src, dst_ref=dst, send_sem=send_sem, recv_sem=recv_sem,
            device_id=(row, col), device_id_type=MESH,
        )

    def run_if(cond, fn):
        pl.when(cond)(fn)

    def send(cond, src, dst, send_sem, recv_sem, row, col):
        copy = remote(src, dst, send_sem, recv_sem, row, col)
        run_if(cond, copy.start)
        later.append((cond, copy))

    def send_any(cond, src, dst, send_sem, recv_sem, row, col):
        here = (row == r) & (col == c)
        run_if(cond & here, pltpu.make_async_copy(src, dst, recv_sem).start)
        send(cond & ~here, src, dst, send_sem, recv_sem, row, col)

    def seat(i, second, x=x_at):
        return wrap(i + AWAY * second), XS * line_of(i, second) + x

    fetch = [
        pltpu.make_async_copy(pairs_full, pairs_in, q_in.at[2]),
        pltpu.make_async_copy(lam_full, lam, q_in.at[3]),
    ]
    for t in (0, 1):
        b = jnp.minimum((r + SIDE * t + e) // SIDE, 1)
        fetch.append(pltpu.make_async_copy(known_full.at[t, b], known_in.at[t], q_in.at[t]))
    for copy in fetch:
        copy.start()

    barrier = pltpu.get_barrier_semaphore()

    def meet(row, col):
        pl.semaphore_signal(barrier, inc=1, device_id=(row, col), device_id_type=MESH)

    def greet_line(step, carry):
        meet(lax.rem(r + step // XS, SIDE), XS * lax.rem(y_at + step, XS) + x_at)
        return carry

    def greet_row(step, carry):
        col = XS * lax.rem(step, XS) + lax.rem(x_at + 1 + step // XS, XS)
        meet(r, col)
        return carry

    lines = SIDE * XS - 1
    others = XS * (XS - 1)
    lax.fori_loop(1, lines + 1, greet_line, 0)
    lax.fori_loop(0, others, greet_row, 0)
    for copy in fetch:
        copy.wait()
    known[...] = known_in[...].astype(jnp.bfloat16)
    pairs[...] = pairs_in[...].astype(jnp.bfloat16)
    pl.semaphore_wait(barrier, lines + others)

    near = e < FIRST
    eb = jnp.minimum(e, FIRST - 1)
    places = []
    for t in (0, 1):
        k = r + SIDE * t
        j = k + e
        b = jnp.minimum(j // SIDE, 1)
        last = jnp.clip(j - FIRST, 0, DIAGS - 1)
        to_ring = near & (k < TOTAL - FIRST)
        to_chain = near & (j >= FIRST) & (j < TOTAL)
        entries = [
            seat(jnp.maximum(j - FIRST - jnp.minimum(entry_of(n, j, eb), last), 0), n) for n in (0, 1)
        ]
        v_entry = seat(jnp.maximum(j - FIRST - last, 0), 0)
        places.append((k, j, b, to_ring, to_chain, entries, v_entry))

    mo = jnp.clip(e - FIRST, 0, DIAGS - 1)
    owner = (e >= FIRST) & (e < FIRST + DIAGS)
    owned = [owner & (places[t][1] < TOTAL) for t in (0, 1)]

    def send_near(group, kind, t):
        k, j, b, to_ring, to_chain, entries, _ = places[t]
        n = "FS".index(kind)
        src = (known.at[t], schur.at[t, b])[n]
        used = e >= n
        at = 2 * n + (group == "c")
        if group == "r":
            send_any(to_ring & used, src, ring.at[eb], s_src.at[t, at], q_ring.at[eb], *seat(k, n))
        else:
            send_any(to_chain & used, src, chain.at[eb], s_src.at[t, at], q_chain.at[eb], *entries[1 - n])

    def send_own(t):
        k, j, b = places[t][:3]
        slot = FIRST + mo
        send(owned[t], schur.at[t, b], ring.at[slot], s_own.at[t, 0, 0], q_ring.at[slot], *seat(k, 1))
        send_any(owned[t], schur.at[t, b], chain.at[slot], s_own.at[t, 1, 0], q_chain.at[slot], *seat(k, 0))

    def send_close(t):
        k, j, b = places[t][:3]
        slot = jnp.clip(e - 1, 0, DIAGS - 2)
        for d in range(DIAGS - 1):
            fits = (e >= 1) & (e + d < DIAGS) & (j + FIRST + d < TOTAL)
            send_any(fits, schur.at[t, b], near_s.at[slot], s_near.at[t, d], q_near.at[slot], *seat(k, 0, lax.rem(x_at + d, XS)))

    for token in SENDS:
        if token == "own":
            send_own(0)
            send_own(1)
        elif token == "x":
            send_close(0)
            send_close(1)
        elif token == "v":
            for t in (0, 1):
                send(places[t][4] & (e == 0), pairs.at[t], vj, s_src.at[t, 4], q_vj.at[0], *places[t][6])
        else:
            send_near(token[0], token[1], int(token[2]))

    i0 = wrap(r - AWAY)
    few = TOTAL - SIDE - FIRST
    first0, first1 = y_at == line_of(r, 0), (r < few) & (y_at == line_of(r + SIDE, 0))
    second0, second1 = y_at == line_of(i0, 1), (i0 < few) & (y_at == line_of(i0 + SIDE, 1))
    is_second = second0 | second1
    part = first0 | first1 | is_second
    kind = jnp.where(is_second, 1, 0)
    t = jnp.where(first1 | second1, 1, 0)
    i = jnp.where(is_second, i0, r) + SIDE * t
    m = lax.rem(x_at + 2 * SIDE - i, XS)
    j = i + FIRST + m
    real = part & (j < TOTAL)
    last = jnp.minimum(DIAGS - 1, i + m)
    takes = (part & ~is_second, is_second)
    adds = (real & ~is_second, real & is_second)
    col_next = (XS * y_at + lax.rem(x_at + 1, XS), XS * y_at + lax.rem(x_at + XS - 1, XS))

    @pl.when(adds[0])
    def _():
        rows = jnp.broadcast_to(lam[pl.ds(i, 1), :], total.shape).T
        gap[...] = 1.0 / (rows - lam[pl.ds(jnp.minimum(j, TOTAL - 1), 1), :])

    @pl.when(real)
    def _():
        total[...] = jnp.zeros(total.shape, jnp.float32)

    def member(step):
        return seat(jnp.maximum(i - step, 0), kind)

    def ring_copy(x, d):
        return remote(ring.at[x], ring.at[x], s_ring.at[x, d], q_ring.at[x], r, col_next[d])

    def chain_copy(x, d):
        return remote(chain.at[x], chain.at[x], s_chain.at[x, d], q_chain.at[x], *member(1 - 2 * d))

    def v_copy():
        return remote(vj, vj, s_v.at[0], q_vj.at[0], *member(-1))

    def ring_first(n, start):
        for x in (m, m + DIAGS):

            @pl.when(takes[n] & (x >= n))
            def _():
                if start:
                    arrived(ring.at[x], q_ring.at[x])
                for d in (0, 1):
                    ring_copy(x, d).start() if start else ring_copy(x, d).wait_send()

    def ring_second(n, start):
        for high in (0, 1):
            turn = TURN[n][high]
            x = lax.rem(m + DIAGS - turn, DIAGS) + DIAGS * high

            @pl.when(takes[n] & (x >= n))
            def _():
                copy = ring_copy(x, 0 if turn == 1 else 1)
                if start:
                    arrived(ring.at[x], q_ring.at[x])
                    copy.start()
                else:
                    copy.wait_send()

    def chain_moves(n, x):
        at = jnp.minimum(entry_of(n, j, x), last)
        up = adds[n] & (m >= at) & (m < last)
        down = adds[n] & (m <= at) & (m > 0)
        return up, down, jnp.abs(m - at)

    def chain_slots(n):
        return [x for x in CHAIN_ORDER if x + n > 0]

    def chain_hop(n, depth):
        for x in chain_slots(n):
            up, down, hops = chain_moves(n, x)
            now = hops == depth
            run_if((up | down) & now, lambda: arrived(chain.at[x], q_chain.at[x]))
            run_if(up & now, chain_copy(x, 0).start)
            run_if(down & now, chain_copy(x, 1).start)

    v_moves = adds[0] & (m > 0)

    def v_hop(depth):
        @pl.when(v_moves & (last - m == depth))
        def _():
            arrived(vj, q_vj.at[0])
            v_copy().start()

    def own_hop(n):
        slot = FIRST + jnp.clip(m, 0, DIAGS - 1)
        ref, sems = ((chain, q_chain), (ring, q_ring))[n]
        run_if(adds[n], lambda: arrived(ref.at[slot], sems.at[slot]))
        for d in range(1, DIAGS):
            if n:
                fits, to = j + d < TOTAL, (r, XS * y_at + lax.rem(x_at + d, XS))
            else:
                fits, to = i >= d, seat(jnp.maximum(i - d, 0), 0)
            send(adds[n] & (m + d < DIAGS) & fits, ref.at[slot], ref.at[slot], s_own.at[2, n, d], sems.at[slot], *to)

    for n in (0, 1):
        for token in WAITS[n]:
            if token == "e":
                ring_first(n, True)
            elif token == "l":
                ring_second(n, True)
            elif token == "o":
                own_hop(n)
            elif token[0] == "v":
                v_hop(int(token[1]))
            else:
                chain_hop(n, int(token))

    def ring_rest(n, x):
        away = lax.rem(m - x + 2 * DIAGS, DIAGS)
        turn = TURN[n][x // DIAGS]
        mine = takes[n] & (away != 0) & (away != lax.rem(turn + DIAGS, DIAGS))
        run_if(mine, lambda: arrived(ring.at[x], q_ring.at[x]))

    def chain_rest(n, x):
        up, down, _ = chain_moves(n, x)
        run_if(adds[n] & ~(up | down), lambda: arrived(chain.at[x], q_chain.at[x]))

    def accumulate(x):
        other_x = FIRST + m - x
        total[...] += dot(ring[jnp.where(is_second, x, other_x)], chain[jnp.where(is_second, other_x, x)])

    for x in range(FIRST):
        ring_rest(0, x)
        chain_rest(1, x)

    def far(x, carry):
        @pl.when(real & (x <= FIRST + m))
        def _():
            sent_on = x == FIRST + m
            run_if(~is_second & ~sent_on, lambda: arrived(chain.at[x], q_chain.at[x]))
            run_if(is_second & ~sent_on, lambda: arrived(ring.at[x], q_ring.at[x]))
            accumulate(x)

        return carry

    lax.fori_loop(FIRST, FIRST + DIAGS, far, 0)
    for x in range(1, FIRST):
        chain_rest(0, x)
        ring_rest(1, x)
        run_if(real & (x > m), lambda: accumulate(x))

    @pl.when(adds[1])
    def _():
        fresh[...] = total[...].astype(jnp.bfloat16)

    send(adds[1], fresh, other, s_out.at[1], q_other.at[0], *seat(i, 0))

    @pl.when(adds[0])
    def _():
        arrived(other, q_other.at[0])
        total[...] -= other[...].astype(jnp.float32)

    run_if(adds[0] & (m == 0), lambda: arrived(vj, q_vj.at[0]))

    for before in range(DIAGS - 1):

        @pl.when(adds[0] & (m > before))
        def _():
            arrived(near_s.at[before], q_near.at[before])

    for before in range(DIAGS - 1):

        @pl.when(adds[0] & (m > before))
        def _():
            away = m - before
            arrived(new_r.at[before], q_new_r.at[before])
            arrived(new_c.at[before], q_new_c.at[before])
            total[...] += dot(new_r[before], chain[away]) - dot(near_s[away - 1], new_c[before])

    mine = jnp.minimum(m, DIAGS - 2)
    onward = []
    for d in range(1, DIAGS):
        fits = adds[0] & (m + d < DIAGS)
        in_ring = remote(fresh, new_r.at[mine], s_new.at[0, d - 1], q_new_r.at[mine], r, XS * y_at + lax.rem(x_at + d, XS))
        in_chain = remote(fresh, new_c.at[mine], s_new.at[1, d - 1], q_new_c.at[mine], *seat(jnp.maximum(i - d, 0), 0))
        onward += [(fits & (j + d < TOTAL), in_ring), (fits & (i >= d), in_chain)]

    @pl.when(adds[0])
    def _():
        x = left_dot(pairs[t, 1], total[...])
        x = right_dot(x, vj[0]) * gap[...]
        x = left_dot(pairs[t, 0], x)
        x = right_dot(x, vj[1])
        fresh[...] = x.astype(jnp.bfloat16)
        for fits, copy in onward:
            run_if(fits, copy.start)
        solved[...] = x

    later.extend(onward)
    send_any(adds[0], solved, out.at[t], s_out.at[0], q_out.at[t], wrap(i), lax.rem(j, SIDE))

    for n in (0, 1):
        run_if(owned[n], lambda: arrived(out.at[n], q_out.at[n]))

    for cond, copy in later:
        run_if(cond, copy.wait_send)
    for n in (0, 1):
        ring_first(n, False)
        ring_second(n, False)
        for x in chain_slots(n):
            up, down, _ = chain_moves(n, x)
            run_if(up, chain_copy(x, 0).wait_send)
            run_if(down, chain_copy(x, 1).wait_send)
    run_if(v_moves, lambda: v_copy().wait_send())


def exchange(schur, known, pairs, lam):
    bs = schur.shape[-1]
    half, full = jnp.bfloat16, jnp.float32
    dma = pltpu.SemaphoreType.DMA
    vmem = pl.BlockSpec(memory_space=pltpu.VMEM)
    band = FIRST + DIAGS
    return pl.pallas_call(
        kernel,
        out_shape=jax.ShapeDtypeStruct((2, bs, bs), full),
        in_specs=[pl.BlockSpec(memory_space=pltpu.HBM)] * 4,
        out_specs=vmem,
        scratch_shapes=[
            pltpu.VMEM(lam.shape, full),
            pltpu.VMEM((2, bs, bs), half),
            pltpu.VMEM((2, 2, bs, bs), half),
            pltpu.VMEM((2, bs, bs), full),
            pltpu.VMEM((2, 2, bs, bs), full),
            pltpu.VMEM((band, bs, bs), half),
            pltpu.VMEM((band, bs, bs), half),
            pltpu.VMEM((DIAGS - 1, bs, bs), half),
            pltpu.VMEM((2, bs, bs), half),
            pltpu.VMEM((DIAGS - 1, bs, bs), half),
            pltpu.VMEM((DIAGS - 1, bs, bs), half),
            pltpu.VMEM((bs, bs), half),
            pltpu.VMEM((bs, bs), full),
            pltpu.VMEM((bs, bs), full),
            pltpu.VMEM((bs, bs), half),
            pltpu.VMEM((bs, bs), full),
            dma((4,)), dma((band,)), dma((band,)), dma((DIAGS - 1,)), dma((1,)),
            dma((DIAGS - 1,)), dma((DIAGS - 1,)), dma((1,)), dma((2,)),
            dma((2, 5)), dma((band, 2)), dma((band, 2)), dma((1,)), dma((3, 2, DIAGS)),
            dma((2, DIAGS - 1)), dma((2, DIAGS - 1)), dma((2,)),
        ],
        compiler_params=pltpu.CompilerParams(
            collective_id=0, has_side_effects=True, vmem_limit_bytes=40 * 1024 * 1024
        ),
    )(*(pltpu.with_memory_space_constraint(a, pltpu.HBM) for a in (schur, known, pairs, lam)))


def body(schur_blocks, known_blocks, eigen_pairs, eigenvalues):
    known = known_blocks[:, 0, :, 0]
    solved = exchange(
        schur_blocks[:, 0, :, 0],
        known,
        eigen_pairs[:, 0],
        eigenvalues,
    )
    rows = lax.axis_index("row") + SIDE * jnp.arange(2)[:, None]
    cols = lax.axis_index("col") + SIDE * jnp.arange(2)[None, :]
    away = cols - rows
    new = (away >= FIRST) & (away < FIRST + DIAGS)
    output = jnp.where(new[:, :, None, None], solved[:, None], known)
    return output[:, None, :, None]


def solution(mesh):
    return jax.shard_map(
        body,
        mesh=mesh,
        in_specs=(
            P(None, "row", None, "col", None, None),
            P(None, "row", None, "col", None, None),
            P(None, "row", None, None, None),
            P(),
        ),
        out_specs=P(None, "row", None, "col", None, None),
        check_vma=False,
    )
```

```python
import jax
import jax.numpy as jnp
from jax import lax
from jax.experimental import pallas as pl
from jax.experimental.pallas import tpu as pltpu
from jax.sharding import PartitionSpec as P

FIRST = 8
DIAGS = 4
SIDE = 16
XS = 4
TOTAL = 32
AWAY = 4
LATE = 24
MESH = pl.DeviceIdType.MESH

SENDS = ("rF1", "own", "rS0", "v", "cS0", "rF0", "rS1", "cF1", "x", "cF0", "cS1")
WAITS = (("e", "0", "l", "3", "1", "v0", "v2", "v1", "o", "2"), ("0", "3", "e", "o", "1", "2", "l"))
ENTRY = (((3, 3, 1, 0, 0, 1, 1, 1), (1, 1, 0, 0, 1, 1, 2, 1)), ((1, 0, 3, 0, 0, 0, 2, 2), (0, 1, 0, 2, 0, 1, 3, 3)))
TURN = ((-1, -1), (1, -1))
SUMS = ((6, 2, 5, 4, 3, 7, 1), (1, 4, 7, 2, 6, 3, 5))
CHAIN_ORDER = (6, 5, 7, 0, 3, 4, 2, 1)


def arrived(ref, sem):
    pltpu.make_async_copy(ref, ref, sem).wait()


def wrap(x):
    return lax.rem(x + 2 * SIDE, SIDE)


def line_of(i, second):
    return lax.rem((i + FIRST) // XS + (1 + 2 * second) * (i // SIDE), XS)


def pick(index, table):
    if isinstance(index, int):
        return table[index]
    chosen = jnp.int32(table[0])
    for n, value in enumerate(table[1:], 1):
        chosen = jnp.where(index == n, value, chosen)
    return chosen


def entry_of(n, j, index):
    early, late = ENTRY[n]
    return jnp.where(j < LATE, pick(index, early), pick(index, late))


def dot(a, b):
    return jnp.dot(a, b, preferred_element_type=jnp.float32)


def halves(x):
    high = x.astype(jnp.bfloat16)
    return high, (x - high.astype(jnp.float32)).astype(jnp.bfloat16)


def left_dot(a, x):
    high, low = halves(x)
    return dot(a, high) + dot(a, low)


def right_dot(x, b):
    high, low = halves(x)
    return dot(high, b) + dot(low, b)


def kernel(
    schur, known_full, pairs_full, lam_full, out,
    lam, known, pairs, known_in, pairs_in, ring, chain, near_s, vj, new_r, new_c, other, total, gap, fresh, solved,
    q_in, q_ring, q_chain, q_near, q_vj, q_new_r, q_new_c, q_other, q_out,
    s_src, s_ring, s_chain, s_v, s_own, s_near, s_new, s_out,
):
    r = lax.axis_index("row")
    c = lax.axis_index("col")
    x_at, y_at = lax.rem(c, XS), c // XS
    e = wrap(c - r)
    later = []

    def remote(src, dst, send_sem, recv_sem, row, col):
        return pltpu.make_async_remote_copy(
            src_ref=src, dst_ref=dst, send_sem=send_sem, recv_sem=recv_sem,
            device_id=(row, col), device_id_type=MESH,
        )

    def run_if(cond, fn):
        pl.when(cond)(fn)

    def send(cond, src, dst, send_sem, recv_sem, row, col):
        copy = remote(src, dst, send_sem, recv_sem, row, col)
        run_if(cond, copy.start)
        later.append((cond, copy))

    def send_any(cond, src, dst, send_sem, recv_sem, row, col):
        here = (row == r) & (col == c)
        run_if(cond & here, pltpu.make_async_copy(src, dst, recv_sem).start)
        send(cond & ~here, src, dst, send_sem, recv_sem, row, col)

    def seat(i, second, x=x_at):
        return wrap(i + AWAY * second), XS * line_of(i, second) + x

    fetch = [
        pltpu.make_async_copy(pairs_full, pairs_in, q_in.at[2]),
        pltpu.make_async_copy(lam_full, lam, q_in.at[3]),
    ]
    for t in (0, 1):
        b = jnp.minimum((r + SIDE * t + e) // SIDE, 1)
        fetch.append(pltpu.make_async_copy(known_full.at[t, b], known_in.at[t], q_in.at[t]))
    for copy in fetch:
        copy.start()

    barrier = pltpu.get_barrier_semaphore()

    def meet(row, col):
        pl.semaphore_signal(barrier, inc=1, device_id=(row, col), device_id_type=MESH)

    def greet_line(step, carry):
        meet(lax.rem(r + step // XS, SIDE), XS * lax.rem(y_at + step, XS) + x_at)
        return carry

    def greet_row(step, carry):
        col = XS * lax.rem(step, XS) + lax.rem(x_at + 1 + step // XS, XS)
        meet(r, col)
        return carry

    lines = SIDE * XS - 1
    others = XS * (XS - 1)
    lax.fori_loop(1, lines + 1, greet_line, 0)
    lax.fori_loop(0, others, greet_row, 0)
    for copy in fetch:
        copy.wait()
    known[...] = known_in[...].astype(jnp.bfloat16)
    pairs[...] = pairs_in[...].astype(jnp.bfloat16)
    pl.semaphore_wait(barrier, lines + others)

    near = e < FIRST
    eb = jnp.minimum(e, FIRST - 1)
    places = []
    for t in (0, 1):
        k = r + SIDE * t
        j = k + e
        b = jnp.minimum(j // SIDE, 1)
        last = jnp.clip(j - FIRST, 0, DIAGS - 1)
        to_ring = near & (k < TOTAL - FIRST)
        to_chain = near & (j >= FIRST) & (j < TOTAL)
        entries = [
            seat(jnp.maximum(j - FIRST - jnp.minimum(entry_of(n, j, eb), last), 0), n) for n in (0, 1)
        ]
        v_entry = seat(jnp.maximum(j - FIRST - last, 0), 0)
        places.append((k, j, b, to_ring, to_chain, entries, v_entry))

    mo = jnp.clip(e - FIRST, 0, DIAGS - 1)
    owner = (e >= FIRST) & (e < FIRST + DIAGS)
    owned = [owner & (places[t][1] < TOTAL) for t in (0, 1)]

    def send_near(group, kind, t):
        k, j, b, to_ring, to_chain, entries, _ = places[t]
        n = "FS".index(kind)
        src = (known.at[t], schur.at[t, b])[n]
        used = e >= n
        at = 2 * n + (group == "c")
        if group == "r":
            send_any(to_ring & used, src, ring.at[eb], s_src.at[t, at], q_ring.at[eb], *seat(k, n))
        else:
            send_any(to_chain & used, src, chain.at[eb], s_src.at[t, at], q_chain.at[eb], *entries[1 - n])

    def send_own(t):
        k, j, b = places[t][:3]
        slot = FIRST + mo
        send(owned[t], schur.at[t, b], ring.at[slot], s_own.at[t, 0, 0], q_ring.at[slot], *seat(k, 1))
        send_any(owned[t], schur.at[t, b], chain.at[slot], s_own.at[t, 1, 0], q_chain.at[slot], *seat(k, 0))

    def send_close(t):
        k, j, b = places[t][:3]
        slot = jnp.clip(e - 1, 0, DIAGS - 2)
        for d in range(DIAGS - 1):
            fits = (e >= 1) & (e + d < DIAGS) & (j + FIRST + d < TOTAL)
            send_any(fits, schur.at[t, b], near_s.at[slot], s_near.at[t, d], q_near.at[slot], *seat(k, 0, lax.rem(x_at + d, XS)))

    for token in SENDS:
        if token == "own":
            send_own(0)
            send_own(1)
        elif token == "x":
            send_close(0)
            send_close(1)
        elif token == "v":
            for t in (0, 1):
                send(places[t][4] & (e == 0), pairs.at[t], vj, s_src.at[t, 4], q_vj.at[0], *places[t][6])
        else:
            send_near(token[0], token[1], int(token[2]))

    i0 = wrap(r - AWAY)
    few = TOTAL - SIDE - FIRST
    first0, first1 = y_at == line_of(r, 0), (r < few) & (y_at == line_of(r + SIDE, 0))
    second0, second1 = y_at == line_of(i0, 1), (i0 < few) & (y_at == line_of(i0 + SIDE, 1))
    is_second = second0 | second1
    part = first0 | first1 | is_second
    kind = jnp.where(is_second, 1, 0)
    t = jnp.where(first1 | second1, 1, 0)
    i = jnp.where(is_second, i0, r) + SIDE * t
    m = lax.rem(x_at + 2 * SIDE - i, XS)
    j = i + FIRST + m
    real = part & (j < TOTAL)
    last = jnp.minimum(DIAGS - 1, i + m)
    takes = (part & ~is_second, is_second)
    adds = (real & ~is_second, real & is_second)
    col_next = (XS * y_at + lax.rem(x_at + 1, XS), XS * y_at + lax.rem(x_at + XS - 1, XS))

    @pl.when(adds[0])
    def _():
        rows = jnp.broadcast_to(lam[pl.ds(i, 1), :], total.shape).T
        gap[...] = 1.0 / (rows - lam[pl.ds(jnp.minimum(j, TOTAL - 1), 1), :])

    @pl.when(real)
    def _():
        total[...] = jnp.zeros(total.shape, jnp.float32)

    def member(step):
        return seat(jnp.maximum(i - step, 0), kind)

    def ring_copy(x, d):
        return remote(ring.at[x], ring.at[x], s_ring.at[x, d], q_ring.at[x], r, col_next[d])

    def chain_copy(x, d):
        return remote(chain.at[x], chain.at[x], s_chain.at[x, d], q_chain.at[x], *member(1 - 2 * d))

    def v_copy():
        return remote(vj, vj, s_v.at[0], q_vj.at[0], *member(-1))

    def ring_first(n, start):
        for x in (m, m + DIAGS):

            @pl.when(takes[n] & (x >= n))
            def _():
                if start:
                    arrived(ring.at[x], q_ring.at[x])
                for d in (0, 1):
                    ring_copy(x, d).start() if start else ring_copy(x, d).wait_send()

    def ring_second(n, start):
        for high in (0, 1):
            turn = TURN[n][high]
            x = lax.rem(m + DIAGS - turn, DIAGS) + DIAGS * high

            @pl.when(takes[n] & (x >= n))
            def _():
                copy = ring_copy(x, 0 if turn == 1 else 1)
                if start:
                    arrived(ring.at[x], q_ring.at[x])
                    copy.start()
                else:
                    copy.wait_send()

    def chain_moves(n, x):
        at = jnp.minimum(entry_of(n, j, x), last)
        up = adds[n] & (m >= at) & (m < last)
        down = adds[n] & (m <= at) & (m > 0)
        return up, down, jnp.abs(m - at)

    def chain_slots(n):
        return [x for x in CHAIN_ORDER if x + n > 0]

    def chain_hop(n, depth):
        for x in chain_slots(n):
            up, down, hops = chain_moves(n, x)
            now = hops == depth
            run_if((up | down) & now, lambda: arrived(chain.at[x], q_chain.at[x]))
            run_if(up & now, chain_copy(x, 0).start)
            run_if(down & now, chain_copy(x, 1).start)

    v_moves = adds[0] & (m > 0)

    def v_hop(depth):
        @pl.when(v_moves & (last - m == depth))
        def _():
            arrived(vj, q_vj.at[0])
            v_copy().start()

    def own_hop(n):
        slot = FIRST + jnp.clip(m, 0, DIAGS - 1)
        ref, sems = ((chain, q_chain), (ring, q_ring))[n]
        run_if(adds[n], lambda: arrived(ref.at[slot], sems.at[slot]))
        for d in range(1, DIAGS):
            if n:
                fits, to = j + d < TOTAL, (r, XS * y_at + lax.rem(x_at + d, XS))
            else:
                fits, to = i >= d, seat(jnp.maximum(i - d, 0), 0)
            send(adds[n] & (m + d < DIAGS) & fits, ref.at[slot], ref.at[slot], s_own.at[2, n, d], sems.at[slot], *to)

    for n in (0, 1):
        for token in WAITS[n]:
            if token == "e":
                ring_first(n, True)
            elif token == "l":
                ring_second(n, True)
            elif token == "o":
                own_hop(n)
            elif token[0] == "v":
                v_hop(int(token[1]))
            else:
                chain_hop(n, int(token))

    def ring_rest(n, x):
        away = lax.rem(m - x + 2 * DIAGS, DIAGS)
        turn = TURN[n][x // DIAGS]
        mine = takes[n] & (away != 0) & (away != lax.rem(turn + DIAGS, DIAGS))
        run_if(mine, lambda: arrived(ring.at[x], q_ring.at[x]))

    def chain_rest(n, x):
        up, down, _ = chain_moves(n, x)
        run_if(adds[n] & ~(up | down), lambda: arrived(chain.at[x], q_chain.at[x]))

    def accumulate(x):
        other_x = FIRST + m - x
        total[...] += dot(ring[jnp.where(is_second, x, other_x)], chain[jnp.where(is_second, other_x, x)])

    for x in range(FIRST):
        ring_rest(0, x)
        chain_rest(1, x)

    def far(x, carry):
        @pl.when(real & (x <= FIRST + m))
        def _():
            sent_on = x == FIRST + m
            run_if(~is_second & ~sent_on, lambda: arrived(chain.at[x], q_chain.at[x]))
            run_if(is_second & ~sent_on, lambda: arrived(ring.at[x], q_ring.at[x]))
            accumulate(x)

        return carry

    lax.fori_loop(FIRST, FIRST + DIAGS, far, 0)
    for n in (0, 1):
        for x in SUMS[n]:
            ring_rest(1, x) if n else chain_rest(0, x)
            run_if(adds[n] & (x > m), lambda: accumulate(x))

    @pl.when(adds[1])
    def _():
        fresh[...] = total[...].astype(jnp.bfloat16)

    send(adds[1], fresh, other, s_out.at[1], q_other.at[0], *seat(i, 0))

    @pl.when(adds[0])
    def _():
        arrived(other, q_other.at[0])
        total[...] -= other[...].astype(jnp.float32)

    run_if(adds[0] & (m == 0), lambda: arrived(vj, q_vj.at[0]))

    for before in range(DIAGS - 1):

        @pl.when(adds[0] & (m > before))
        def _():
            arrived(near_s.at[before], q_near.at[before])

    for before in range(DIAGS - 1):

        @pl.when(adds[0] & (m > before))
        def _():
            away = m - before
            arrived(new_r.at[before], q_new_r.at[before])
            arrived(new_c.at[before], q_new_c.at[before])
            total[...] += dot(new_r[before], chain[away]) - dot(near_s[away - 1], new_c[before])

    mine = jnp.minimum(m, DIAGS - 2)
    onward = []
    for d in range(1, DIAGS):
        fits = adds[0] & (m + d < DIAGS)
        in_ring = remote(fresh, new_r.at[mine], s_new.at[0, d - 1], q_new_r.at[mine], r, XS * y_at + lax.rem(x_at + d, XS))
        in_chain = remote(fresh, new_c.at[mine], s_new.at[1, d - 1], q_new_c.at[mine], *seat(jnp.maximum(i - d, 0), 0))
        onward += [(fits & (j + d < TOTAL), in_ring), (fits & (i >= d), in_chain)]

    @pl.when(adds[0])
    def _():
        x = left_dot(pairs[t, 1], total[...])
        x = right_dot(x, vj[0]) * gap[...]
        x = left_dot(pairs[t, 0], x)
        x = right_dot(x, vj[1])
        fresh[...] = x.astype(jnp.bfloat16)
        for fits, copy in onward:
            run_if(fits, copy.start)
        solved[...] = x

    later.extend(onward)
    send_any(adds[0], solved, out.at[t], s_out.at[0], q_out.at[t], wrap(i), lax.rem(j, SIDE))

    for n in (0, 1):
        run_if(owned[n], lambda: arrived(out.at[n], q_out.at[n]))

    for cond, copy in later:
        run_if(cond, copy.wait_send)
    for n in (0, 1):
        ring_first(n, False)
        ring_second(n, False)
        for x in chain_slots(n):
            up, down, _ = chain_moves(n, x)
            run_if(up, chain_copy(x, 0).wait_send)
            run_if(down, chain_copy(x, 1).wait_send)
    run_if(v_moves, lambda: v_copy().wait_send())


def exchange(schur, known, pairs, lam):
    bs = schur.shape[-1]
    half, full = jnp.bfloat16, jnp.float32
    dma = pltpu.SemaphoreType.DMA
    vmem = pl.BlockSpec(memory_space=pltpu.VMEM)
    band = FIRST + DIAGS
    return pl.pallas_call(
        kernel,
        out_shape=jax.ShapeDtypeStruct((2, bs, bs), full),
        in_specs=[pl.BlockSpec(memory_space=pltpu.HBM)] * 4,
        out_specs=vmem,
        scratch_shapes=[
            pltpu.VMEM(lam.shape, full),
            pltpu.VMEM((2, bs, bs), half),
            pltpu.VMEM((2, 2, bs, bs), half),
            pltpu.VMEM((2, bs, bs), full),
            pltpu.VMEM((2, 2, bs, bs), full),
            pltpu.VMEM((band, bs, bs), half),
            pltpu.VMEM((band, bs, bs), half),
            pltpu.VMEM((DIAGS - 1, bs, bs), half),
            pltpu.VMEM((2, bs, bs), half),
            pltpu.VMEM((DIAGS - 1, bs, bs), half),
            pltpu.VMEM((DIAGS - 1, bs, bs), half),
            pltpu.VMEM((bs, bs), half),
            pltpu.VMEM((bs, bs), full),
            pltpu.VMEM((bs, bs), full),
            pltpu.VMEM((bs, bs), half),
            pltpu.VMEM((bs, bs), full),
            dma((4,)), dma((band,)), dma((band,)), dma((DIAGS - 1,)), dma((1,)),
            dma((DIAGS - 1,)), dma((DIAGS - 1,)), dma((1,)), dma((2,)),
            dma((2, 5)), dma((band, 2)), dma((band, 2)), dma((1,)), dma((3, 2, DIAGS)),
            dma((2, DIAGS - 1)), dma((2, DIAGS - 1)), dma((2,)),
        ],
        compiler_params=pltpu.CompilerParams(
            collective_id=0, has_side_effects=True, vmem_limit_bytes=40 * 1024 * 1024
        ),
    )(*(pltpu.with_memory_space_constraint(a, pltpu.HBM) for a in (schur, known, pairs, lam)))


def body(schur_blocks, known_blocks, eigen_pairs, eigenvalues):
    known = known_blocks[:, 0, :, 0]
    solved = exchange(
        schur_blocks[:, 0, :, 0],
        known,
        eigen_pairs[:, 0],
        eigenvalues,
    )
    rows = lax.axis_index("row") + SIDE * jnp.arange(2)[:, None]
    cols = lax.axis_index("col") + SIDE * jnp.arange(2)[None, :]
    away = cols - rows
    new = (away >= FIRST) & (away < FIRST + DIAGS)
    output = jnp.where(new[:, :, None, None], solved[:, None], known)
    return output[:, None, :, None]


def solution(mesh):
    return jax.shard_map(
        body,
        mesh=mesh,
        in_specs=(
            P(None, "row", None, "col", None, None),
            P(None, "row", None, "col", None, None),
            P(None, "row", None, None, None),
            P(),
        ),
        out_specs=P(None, "row", None, "col", None, None),
        check_vma=False,
    )
```

```python
import jax
import jax.numpy as jnp
from jax import lax
from jax.experimental import pallas as pl
from jax.experimental.pallas import tpu as pltpu
from jax.sharding import PartitionSpec as P

FIRST = 8
DIAGS = 4
SIDE = 16
XS = 4
TOTAL = 32
AWAY = 4
LATE = 24
MESH = pl.DeviceIdType.MESH

SENDS = ("rS1", "cF0", "rF0", "rF1", "rS0", "x", "v", "cS1", "own", "cF1", "cS0")
WAITS = (("0", "e", "v1", "v0", "1", "2", "o", "l", "3", "v2"), ("e", "0", "1", "2", "l", "3", "o"))
ENTRY = (((0, 1, 1, 2, 0, 1, 1, 1), (0, 0, 0, 2, 0, 0, 1, 1)), ((1, 0, 0, 0, 0, 1, 2, 2), (0, 1, 0, 0, 0, 1, 1, 3)))
TURN = ((-1, -1), (1, -1))
CHAIN_ORDER = (5, 7, 3, 0, 6, 1, 2, 4)


def arrived(ref, sem):
    pltpu.make_async_copy(ref, ref, sem).wait()


def wrap(x):
    return lax.rem(x + 2 * SIDE, SIDE)


def line_of(i, second):
    return lax.rem((i + FIRST) // XS + (1 + 2 * second) * (i // SIDE), XS)


def pick(index, table):
    if isinstance(index, int):
        return table[index]
    chosen = jnp.int32(table[0])
    for n, value in enumerate(table[1:], 1):
        chosen = jnp.where(index == n, value, chosen)
    return chosen


def entry_of(n, j, index):
    early, late = ENTRY[n]
    return jnp.where(j < LATE, pick(index, early), pick(index, late))


def dot(a, b):
    return jnp.dot(a, b, preferred_element_type=jnp.float32)


def halves(x):
    high = x.astype(jnp.bfloat16)
    return high, (x - high.astype(jnp.float32)).astype(jnp.bfloat16)


def left_dot(a, x):
    high, low = halves(x)
    return dot(a, high) + dot(a, low)


def right_dot(x, b):
    high, low = halves(x)
    return dot(high, b) + dot(low, b)


def kernel(
    schur, known_full, pairs_full, lam_full, out,
    lam, known, pairs, known_in, pairs_in, ring, chain, near_s, vj, new_r, new_c, other, total, gap, fresh, solved,
    q_in, q_ring, q_chain, q_near, q_vj, q_new_r, q_new_c, q_other, q_out,
    s_src, s_ring, s_chain, s_v, s_own, s_near, s_new, s_out,
):
    r = lax.axis_index("row")
    c = lax.axis_index("col")
    x_at, y_at = lax.rem(c, XS), c // XS
    e = wrap(c - r)
    later = []

    def remote(src, dst, send_sem, recv_sem, row, col):
        return pltpu.make_async_remote_copy(
            src_ref=src, dst_ref=dst, send_sem=send_sem, recv_sem=recv_sem,
            device_id=(row, col), device_id_type=MESH,
        )

    def run_if(cond, fn):
        pl.when(cond)(fn)

    def send(cond, src, dst, send_sem, recv_sem, row, col):
        copy = remote(src, dst, send_sem, recv_sem, row, col)
        run_if(cond, copy.start)
        later.append((cond, copy))

    def send_any(cond, src, dst, send_sem, recv_sem, row, col):
        here = (row == r) & (col == c)
        run_if(cond & here, pltpu.make_async_copy(src, dst, recv_sem).start)
        send(cond & ~here, src, dst, send_sem, recv_sem, row, col)

    def seat(i, second, x=x_at):
        return wrap(i + AWAY * second), XS * line_of(i, second) + x

    fetch = [
        pltpu.make_async_copy(pairs_full, pairs_in, q_in.at[2]),
        pltpu.make_async_copy(lam_full, lam, q_in.at[3]),
    ]
    for t in (0, 1):
        b = jnp.minimum((r + SIDE * t + e) // SIDE, 1)
        fetch.append(pltpu.make_async_copy(known_full.at[t, b], known_in.at[t], q_in.at[t]))
    for copy in fetch:
        copy.start()

    barrier = pltpu.get_barrier_semaphore()

    def meet(row, col):
        pl.semaphore_signal(barrier, inc=1, device_id=(row, col), device_id_type=MESH)

    def greet_line(step, carry):
        meet(lax.rem(r + step // XS, SIDE), XS * lax.rem(y_at + step, XS) + x_at)
        return carry

    def greet_row(step, carry):
        col = XS * lax.rem(step, XS) + lax.rem(x_at + 1 + step // XS, XS)
        meet(r, col)
        return carry

    lines = SIDE * XS - 1
    others = XS * (XS - 1)
    lax.fori_loop(1, lines + 1, greet_line, 0)
    lax.fori_loop(0, others, greet_row, 0)
    for copy in fetch:
        copy.wait()
    known[...] = known_in[...].astype(jnp.bfloat16)
    pairs[...] = pairs_in[...].astype(jnp.bfloat16)
    pl.semaphore_wait(barrier, lines + others)

    near = e < FIRST
    eb = jnp.minimum(e, FIRST - 1)
    places = []
    for t in (0, 1):
        k = r + SIDE * t
        j = k + e
        b = jnp.minimum(j // SIDE, 1)
        last = jnp.clip(j - FIRST, 0, DIAGS - 1)
        to_ring = near & (k < TOTAL - FIRST)
        to_chain = near & (j >= FIRST) & (j < TOTAL)
        entries = [
            seat(jnp.maximum(j - FIRST - jnp.minimum(entry_of(n, j, eb), last), 0), n) for n in (0, 1)
        ]
        v_entry = seat(jnp.maximum(j - FIRST - last, 0), 0)
        places.append((k, j, b, to_ring, to_chain, entries, v_entry))

    mo = jnp.clip(e - FIRST, 0, DIAGS - 1)
    owner = (e >= FIRST) & (e < FIRST + DIAGS)
    owned = [owner & (places[t][1] < TOTAL) for t in (0, 1)]

    def send_near(group, kind, t):
        k, j, b, to_ring, to_chain, entries, _ = places[t]
        n = "FS".index(kind)
        src = (known.at[t], schur.at[t, b])[n]
        used = e >= n
        at = 2 * n + (group == "c")
        if group == "r":
            send_any(to_ring & used, src, ring.at[eb], s_src.at[t, at], q_ring.at[eb], *seat(k, n))
        else:
            send_any(to_chain & used, src, chain.at[eb], s_src.at[t, at], q_chain.at[eb], *entries[1 - n])

    def send_own(t):
        k, j, b = places[t][:3]
        slot = FIRST + mo
        send(owned[t], schur.at[t, b], ring.at[slot], s_own.at[t, 0, 0], q_ring.at[slot], *seat(k, 1))
        send_any(owned[t], schur.at[t, b], chain.at[slot], s_own.at[t, 1, 0], q_chain.at[slot], *seat(k, 0))

    def send_close(t):
        k, j, b = places[t][:3]
        slot = jnp.clip(e - 1, 0, DIAGS - 2)
        for d in range(DIAGS - 1):
            fits = (e >= 1) & (e + d < DIAGS) & (j + FIRST + d < TOTAL)
            send_any(fits, schur.at[t, b], near_s.at[slot], s_near.at[t, d], q_near.at[slot], *seat(k, 0, lax.rem(x_at + d, XS)))

    for token in SENDS:
        if token == "own":
            send_own(0)
            send_own(1)
        elif token == "x":
            send_close(0)
            send_close(1)
        elif token == "v":
            for t in (0, 1):
                send(places[t][4] & (e == 0), pairs.at[t], vj, s_src.at[t, 4], q_vj.at[0], *places[t][6])
        else:
            send_near(token[0], token[1], int(token[2]))

    i0 = wrap(r - AWAY)
    few = TOTAL - SIDE - FIRST
    first0, first1 = y_at == line_of(r, 0), (r < few) & (y_at == line_of(r + SIDE, 0))
    second0, second1 = y_at == line_of(i0, 1), (i0 < few) & (y_at == line_of(i0 + SIDE, 1))
    is_second = second0 | second1
    part = first0 | first1 | is_second
    kind = jnp.where(is_second, 1, 0)
    t = jnp.where(first1 | second1, 1, 0)
    i = jnp.where(is_second, i0, r) + SIDE * t
    m = lax.rem(x_at + 2 * SIDE - i, XS)
    j = i + FIRST + m
    real = part & (j < TOTAL)
    last = jnp.minimum(DIAGS - 1, i + m)
    takes = (part & ~is_second, is_second)
    adds = (real & ~is_second, real & is_second)
    col_next = (XS * y_at + lax.rem(x_at + 1, XS), XS * y_at + lax.rem(x_at + XS - 1, XS))

    @pl.when(adds[0])
    def _():
        rows = jnp.broadcast_to(lam[pl.ds(i, 1), :], total.shape).T
        gap[...] = 1.0 / (rows - lam[pl.ds(jnp.minimum(j, TOTAL - 1), 1), :])

    @pl.when(real)
    def _():
        total[...] = jnp.zeros(total.shape, jnp.float32)

    def member(step):
        return seat(jnp.maximum(i - step, 0), kind)

    def ring_copy(x, d):
        return remote(ring.at[x], ring.at[x], s_ring.at[x, d], q_ring.at[x], r, col_next[d])

    def chain_copy(x, d):
        return remote(chain.at[x], chain.at[x], s_chain.at[x, d], q_chain.at[x], *member(1 - 2 * d))

    def v_copy():
        return remote(vj, vj, s_v.at[0], q_vj.at[0], *member(-1))

    def ring_first(n, start):
        for x in (m, m + DIAGS):

            @pl.when(takes[n] & (x >= n))
            def _():
                if start:
                    arrived(ring.at[x], q_ring.at[x])
                for d in (0, 1):
                    ring_copy(x, d).start() if start else ring_copy(x, d).wait_send()

    def ring_second(n, start):
        for high in (0, 1):
            turn = TURN[n][high]
            x = lax.rem(m + DIAGS - turn, DIAGS) + DIAGS * high

            @pl.when(takes[n] & (x >= n))
            def _():
                copy = ring_copy(x, 0 if turn == 1 else 1)
                if start:
                    arrived(ring.at[x], q_ring.at[x])
                    copy.start()
                else:
                    copy.wait_send()

    def chain_moves(n, x):
        at = jnp.minimum(entry_of(n, j, x), last)
        up = adds[n] & (m >= at) & (m < last)
        down = adds[n] & (m <= at) & (m > 0)
        return up, down, jnp.abs(m - at)

    def chain_slots(n):
        return [x for x in CHAIN_ORDER if x + n > 0]

    def chain_hop(n, depth):
        for x in chain_slots(n):
            up, down, hops = chain_moves(n, x)
            now = hops == depth
            run_if((up | down) & now, lambda: arrived(chain.at[x], q_chain.at[x]))
            run_if(up & now, chain_copy(x, 0).start)
            run_if(down & now, chain_copy(x, 1).start)

    v_moves = adds[0] & (m > 0)

    def v_hop(depth):
        @pl.when(v_moves & (last - m == depth))
        def _():
            arrived(vj, q_vj.at[0])
            v_copy().start()

    def own_hop(n):
        slot = FIRST + jnp.clip(m, 0, DIAGS - 1)
        ref, sems = ((chain, q_chain), (ring, q_ring))[n]
        run_if(adds[n], lambda: arrived(ref.at[slot], sems.at[slot]))
        for d in range(1, DIAGS):
            if n:
                fits, to = j + d < TOTAL, (r, XS * y_at + lax.rem(x_at + d, XS))
            else:
                fits, to = i >= d, seat(jnp.maximum(i - d, 0), 0)
            send(adds[n] & (m + d < DIAGS) & fits, ref.at[slot], ref.at[slot], s_own.at[2, n, d], sems.at[slot], *to)

    for n in (0, 1):
        for token in WAITS[n]:
            if token == "e":
                ring_first(n, True)
            elif token == "l":
                ring_second(n, True)
            elif token == "o":
                own_hop(n)
            elif token[0] == "v":
                v_hop(int(token[1]))
            else:
                chain_hop(n, int(token))

    def ring_rest(n, x):
        away = lax.rem(m - x + 2 * DIAGS, DIAGS)
        turn = TURN[n][x // DIAGS]
        mine = takes[n] & (away != 0) & (away != lax.rem(turn + DIAGS, DIAGS))
        run_if(mine, lambda: arrived(ring.at[x], q_ring.at[x]))

    def chain_rest(n, x):
        up, down, _ = chain_moves(n, x)
        run_if(adds[n] & ~(up | down), lambda: arrived(chain.at[x], q_chain.at[x]))

    def accumulate(x):
        other_x = FIRST + m - x
        total[...] += dot(ring[jnp.where(is_second, x, other_x)], chain[jnp.where(is_second, other_x, x)])

    for x in range(FIRST):
        ring_rest(0, x)
        chain_rest(1, x)

    def far(x, carry):
        @pl.when(real & (x <= FIRST + m))
        def _():
            sent_on = x == FIRST + m
            run_if(~is_second & ~sent_on, lambda: arrived(chain.at[x], q_chain.at[x]))
            run_if(is_second & ~sent_on, lambda: arrived(ring.at[x], q_ring.at[x]))
            accumulate(x)

        return carry

    lax.fori_loop(FIRST, FIRST + DIAGS, far, 0)
    for x in range(1, FIRST):
        chain_rest(0, x)
        ring_rest(1, x)
        run_if(real & (x > m), lambda: accumulate(x))

    @pl.when(adds[1])
    def _():
        fresh[...] = total[...].astype(jnp.bfloat16)

    send(adds[1], fresh, other, s_out.at[1], q_other.at[0], *seat(i, 0))

    @pl.when(adds[0])
    def _():
        arrived(other, q_other.at[0])
        total[...] -= other[...].astype(jnp.float32)

    run_if(adds[0] & (m == 0), lambda: arrived(vj, q_vj.at[0]))

    for before in range(DIAGS - 1):

        @pl.when(adds[0] & (m > before))
        def _():
            arrived(near_s.at[before], q_near.at[before])

    for before in range(DIAGS - 1):

        @pl.when(adds[0] & (m > before))
        def _():
            away = m - before
            arrived(new_r.at[before], q_new_r.at[before])
            arrived(new_c.at[before], q_new_c.at[before])
            total[...] += dot(new_r[before], chain[away]) - dot(near_s[away - 1], new_c[before])

    mine = jnp.minimum(m, DIAGS - 2)
    onward = []
    for d in range(1, DIAGS):
        fits = adds[0] & (m + d < DIAGS)
        in_ring = remote(fresh, new_r.at[mine], s_new.at[0, d - 1], q_new_r.at[mine], r, XS * y_at + lax.rem(x_at + d, XS))
        in_chain = remote(fresh, new_c.at[mine], s_new.at[1, d - 1], q_new_c.at[mine], *seat(jnp.maximum(i - d, 0), 0))
        onward += [(fits & (j + d < TOTAL), in_ring), (fits & (i >= d), in_chain)]

    @pl.when(adds[0])
    def _():
        x = left_dot(pairs[t, 1], total[...])
        x = right_dot(x, vj[0]) * gap[...]
        x = left_dot(pairs[t, 0], x)
        x = right_dot(x, vj[1])
        fresh[...] = x.astype(jnp.bfloat16)
        for fits, copy in onward:
            run_if(fits, copy.start)
        solved[...] = x

    later.extend(onward)
    send_any(adds[0], solved, out.at[t], s_out.at[0], q_out.at[t], wrap(i), lax.rem(j, SIDE))

    for n in (0, 1):
        run_if(owned[n], lambda: arrived(out.at[n], q_out.at[n]))

    for cond, copy in later:
        run_if(cond, copy.wait_send)
    for n in (0, 1):
        ring_first(n, False)
        ring_second(n, False)
        for x in chain_slots(n):
            up, down, _ = chain_moves(n, x)
            run_if(up, chain_copy(x, 0).wait_send)
            run_if(down, chain_copy(x, 1).wait_send)
    run_if(v_moves, lambda: v_copy().wait_send())


def exchange(schur, known, pairs, lam):
    bs = schur.shape[-1]
    half, full = jnp.bfloat16, jnp.float32
    dma = pltpu.SemaphoreType.DMA
    vmem = pl.BlockSpec(memory_space=pltpu.VMEM)
    band = FIRST + DIAGS
    return pl.pallas_call(
        kernel,
        out_shape=jax.ShapeDtypeStruct((2, bs, bs), full),
        in_specs=[pl.BlockSpec(memory_space=pltpu.HBM)] * 4,
        out_specs=vmem,
        scratch_shapes=[
            pltpu.VMEM(lam.shape, full),
            pltpu.VMEM((2, bs, bs), half),
            pltpu.VMEM((2, 2, bs, bs), half),
            pltpu.VMEM((2, bs, bs), full),
            pltpu.VMEM((2, 2, bs, bs), full),
            pltpu.VMEM((band, bs, bs), half),
            pltpu.VMEM((band, bs, bs), half),
            pltpu.VMEM((DIAGS - 1, bs, bs), half),
            pltpu.VMEM((2, bs, bs), half),
            pltpu.VMEM((DIAGS - 1, bs, bs), half),
            pltpu.VMEM((DIAGS - 1, bs, bs), half),
            pltpu.VMEM((bs, bs), half),
            pltpu.VMEM((bs, bs), full),
            pltpu.VMEM((bs, bs), full),
            pltpu.VMEM((bs, bs), half),
            pltpu.VMEM((bs, bs), full),
            dma((4,)), dma((band,)), dma((band,)), dma((DIAGS - 1,)), dma((1,)),
            dma((DIAGS - 1,)), dma((DIAGS - 1,)), dma((1,)), dma((2,)),
            dma((2, 5)), dma((band, 2)), dma((band, 2)), dma((1,)), dma((3, 2, DIAGS)),
            dma((2, DIAGS - 1)), dma((2, DIAGS - 1)), dma((2,)),
        ],
        compiler_params=pltpu.CompilerParams(
            collective_id=0, has_side_effects=True, vmem_limit_bytes=40 * 1024 * 1024
        ),
    )(*(pltpu.with_memory_space_constraint(a, pltpu.HBM) for a in (schur, known, pairs, lam)))


def body(schur_blocks, known_blocks, eigen_pairs, eigenvalues):
    known = known_blocks[:, 0, :, 0]
    solved = exchange(
        schur_blocks[:, 0, :, 0],
        known,
        eigen_pairs[:, 0],
        eigenvalues,
    )
    rows = lax.axis_index("row") + SIDE * jnp.arange(2)[:, None]
    cols = lax.axis_index("col") + SIDE * jnp.arange(2)[None, :]
    away = cols - rows
    new = (away >= FIRST) & (away < FIRST + DIAGS)
    output = jnp.where(new[:, :, None, None], solved[:, None], known)
    return output[:, None, :, None]


def solution(mesh):
    return jax.shard_map(
        body,
        mesh=mesh,
        in_specs=(
            P(None, "row", None, "col", None, None),
            P(None, "row", None, "col", None, None),
            P(None, "row", None, None, None),
            P(),
        ),
        out_specs=P(None, "row", None, "col", None, None),
        check_vma=False,
    )
```
